32 devices in a mesh: dp: 16 (over z, x, core), tensor: 2 (over y).
Axes of the slice: x: 2, y: 2, z: 4, core: 2. Of those that a mesh axis runs over, the one named last changes fastest.
Arguments:
- tokens: bfloat16 [2048, 2048], P('dp'), may hold values from -6 to 6
- cotangent: bfloat16 [2048, 2048], P('dp'), may hold values from -6 to 6
- owner_slot: int32 [2048], replicated, may hold values from 0 to 2047, as said below
- sequence_lengths: int32 [32, 3], P('dp'), may hold values from 1 to 32, 64 in all within a row
- norm_gain: bfloat16 [2048], P('dp'), may hold values from 0.25 to 1.75
- inner_weight: bfloat16 [2048, 2, 4096], P('dp', None, 'tensor'), may hold values from -0.125 to 0.125
- filter_weight: float32 [4, 4096], P(None, 'tensor'), may hold values from -3 to 3
- convolution_bias: float32 [4096], P('tensor'), may hold values from -3 to 3
- select_weight: bfloat16 [4096, 160], P('tensor'), may hold values from -0.09375 to 0.09375
- step_weight: bfloat16 [128, 4096], P(None, 'tensor'), may hold values from -0.5 to 0.5
- step_bias: float32 [4096], P('tensor'), may hold values from -6 to -2
- decay_log: float32 [16, 4096], P(None, 'tensor'), may hold values from -1 to 2.77
- skip_weight: float32 [4096], P('tensor'), may hold values from 0.5 to 1.5
- output_weight: bfloat16 [4096, 2048], P('tensor', 'dp'), may hold values from -0.25 to 0.25
Outputs:
- output: bfloat16 [2048, 2048], P('dp')
- input_grad: float32 [2048, 2048], P('dp')
- norm_gain_grad: float32 [2048], P('dp')
- inner_weight_grad: float32 [2048, 2, 4096], P('dp', None, 'tensor')
- filter_weight_grad: float32 [4, 4096], P(None, 'tensor')
- filter_bias_grad: float32 [4096], P('tensor')
- select_weight_grad: float32 [4096, 160], P('tensor')
- step_weight_grad: float32 [128, 4096], P(None, 'tensor')
- step_bias_grad: float32 [4096], P('tensor')
- decay_log_grad: float32 [16, 4096], P(None, 'tensor')
- skip_weight_grad: float32 [4096], P('tensor')
- output_weight_grad: float32 [4096, 2048], P('tensor', 'dp')
The draws below stay inside these ranges and needn't reach their ends.
Inputs may be any that keep to these rules, and one draw needn't show every extreme that they name: `owner_slot`: a permutation; the input rows of each index of dp (blocks of 128) send exactly 8 tokens to the owner block of every index. `sequence_lengths`: each row sums to 64; its largest entry is 32.
All inputs are finite; a program needn't handle non-finite values.
Results may differ from the reference program's by a relative error of at most 0.0098.
Values may be sent and summed in bfloat16 or wider, within the bound.
No kernel may reach another device: no remote copies, remote signals or barrier semaphores. Data moves between devices by JAX's collectives and lax.ppermute only.
A program may use at most 96 MiB of HBM per device.

```python
import math
import jax
import jax.numpy as jnp
import numpy as np
from jax import lax

D = 2048
E = 4096
STATE = 16
RANK = 128
CONV = 4
TOK_MB = 64
MB = 2
SEQS = 3
LONGEST = 32
TOK_DEV = 128
TOKENS = 2048
SHARE = 8
N_DP = 16


def draw_owner_slot(key, part):
    sources = TOKENS // TOK_DEV
    send_key, recv_key = jax.random.split(jax.random.fold_in(key, 7))
    sender_rank = jax.vmap(lambda single: jax.random.permutation(single, TOK_DEV))(jax.random.split(send_key, sources))
    recv_rank = jax.vmap(lambda single: jax.random.permutation(single, TOK_DEV))(jax.random.split(recv_key, sources))
    target = sender_rank // SHARE
    within = sender_rank % SHARE
    source_index = jnp.arange(sources, dtype=jnp.int32)[:, None]
    placed = recv_rank[target, source_index * SHARE + within]
    return (target * TOK_DEV + placed).reshape(-1).astype(jnp.int32)


def levels(own_key, dims, pieces, least, top_value):
    factor_of = 1.0
    for dim, shards_of in pieces:
        steps = jax.random.uniform(jax.random.fold_in(jax.random.fold_in(own_key, 6), dim), (shards_of,), jnp.float32, least / len(pieces), top_value / len(pieces))
        factor_of = factor_of * jnp.repeat(jnp.exp(steps), dims[dim] // shards_of).reshape((-1,) + (1,) * (len(dims) - 1 - dim))
    return factor_of


def profile(count, total, most, skew):
    loads = [(1 << 20) // math.isqrt(grade ** skew) + 1 for grade in range(2, count + 1)]
    rest, given = total - most - (count - 1), [1] * (count - 1)
    while rest > 0:
        candidates = [i for i in range(count - 1) if given[i] < most]
        mass, left = sum([loads[i] for i in candidates]), rest
        for i in candidates:
            more = min(most - given[i], max(1, left * loads[i] // mass), rest)
            given[i] = given[i] + more
            rest = rest - more
    return np.array([most] + given)


def ragged(rng, amount, total, limit, lean):
    if amount == 2:
        one = jax.random.randint(rng, (), max(1, total - limit), min(limit, total - 1) + 1)
        return jnp.stack([one, total - one])
    sizes = jnp.asarray(profile(amount, total, limit, lean), jnp.int32)
    couples = (amount - 1) // 2
    source_of, receiver = sizes[1:1 + 2 * couples:2], sizes[2:2 + 2 * couples:2]
    slack = jnp.minimum(source_of - 1, limit - receiver)
    passed = jax.random.randint(jax.random.fold_in(rng, 1), (couples,), 0, 1 << 20) % (slack + 1)
    sizes = sizes.at[1:1 + 2 * couples:2].set(source_of - passed).at[2:2 + 2 * couples:2].set(receiver + passed)
    return sizes[jax.random.permutation(jax.random.fold_in(rng, 2), amount)]


def normal_values(own_key, dims, spread, most, cuts=(), held_as=jnp.bfloat16):
    values = jax.random.normal(own_key, dims, jnp.float32) * spread
    if len(cuts) > 0:
        values = levels(own_key, dims, cuts, -0.22, 0.18) * values
    return jnp.clip(values, min=-most, max=most).astype(held_as)


def setup_inputs(seed: int = 0) -> dict:
    arg_keys = jax.random.split(jax.random.key(seed), 15)
    return {
        "tokens": normal_values(arg_keys[0], (TOKENS, D), 1.0, 6.0, ((0, 16),)),
        "cotangent": normal_values(arg_keys[1], (TOKENS, D), 1.0, 6.0, ((0, 16),)),
        "owner_slot": draw_owner_slot(jax.random.fold_in(arg_keys[14], 71), 0),
        "sequence_lengths": jax.vmap(lambda own: ragged(own, SEQS, TOK_MB, LONGEST, 2))(jax.random.split(arg_keys[3], (N_DP * MB))).reshape((N_DP * MB, SEQS)).astype(jnp.int32),
        "norm_gain": jnp.clip(1.0 + 0.15 * jax.random.normal(arg_keys[4], (D,), jnp.float32), 0.25, 1.75).astype(jnp.bfloat16),
        "inner_weight": normal_values(arg_keys[5], (D, 2, E), D ** -0.5, 0.125, ((0, 16), (2, 2))),
        "filter_weight": normal_values(arg_keys[6], (CONV, E), CONV ** -0.5, 3.0, ((1, 2),), jnp.float32),
        "convolution_bias": normal_values(arg_keys[7], (E,), 0.5, 3.0, ((0, 2),), jnp.float32),
        "select_weight": normal_values(arg_keys[8], (E, RANK + 2 * STATE), E ** -0.5, 0.09375, ((0, 2),)),
        "step_weight": normal_values(arg_keys[9], (RANK, E), RANK ** -0.5, 0.5, ((1, 2),)),
        "step_bias": jnp.clip(-6.0 + 4.0 * jax.random.uniform(arg_keys[10], (E,), jnp.float32) ** levels(arg_keys[10], (E,), ((0, 2),), -0.2, 0.2), -6.0, -2.0),
        "decay_log": jnp.clip(-1.0 + 3.77 * jax.random.uniform(arg_keys[11], (STATE, E), jnp.float32) ** levels(arg_keys[11], (STATE, E), ((1, 2),), -0.2, 0.2), -1.0, 2.77),
        "skip_weight": jnp.clip(0.5 + 1.0 * jax.random.uniform(arg_keys[12], (E,), jnp.float32) ** levels(arg_keys[12], (E,), ((0, 2),), -0.2, 0.2), 0.5, 1.5),
        "output_weight": normal_values(arg_keys[13], (E, D), (E // 8) ** -0.5, 0.25, ((0, 2), (1, 16))),
    }


@jax.custom_vjp
def low(v):
    return lax.optimization_barrier(v.astype(jnp.bfloat16)).astype(jnp.float32)

@jax.custom_vjp
def low_back(v):
    return v

def low_keep(v):
    return (low(v), None)

def low_pass(kept, grad):
    return (grad,)

def back_keep(v):
    return (v, None)

def back_low(kept, grad):
    return (low(grad),)
low.defvjp(low_keep, low_pass)
low_back.defvjp(back_keep, back_low)
EPSILON = 1e-05
HIGHEST = lax.Precision.HIGHEST

def positions(lengths_table, segment_rows):
    starts = jnp.cumsum(lengths_table, axis=1, dtype=jnp.int32) - lengths_table
    index_row = jnp.arange(segment_rows, dtype=jnp.int32)
    begins = lax.optimization_barrier(jnp.max(jnp.where(starts[:, None, :] <= index_row[None, :, None], starts[:, None, :], 0), axis=2))
    return (index_row[None, :] - begins).astype(jnp.int32)

def conv_silu(stream, filter_weight, convolution_bias, position):
    row_count = stream.shape[0]
    total = jnp.zeros(stream.shape, jnp.float32) + convolution_bias[None, :]
    for lag_steps in range(CONV):
        shifted = jnp.pad(stream, ((lag_steps, 0), (0, 0)))[:row_count]
        valid = (position >= lag_steps)[:, None]
        total = total + filter_weight[CONV - 1 - lag_steps][None, :] * jnp.where(valid, shifted, jnp.zeros_like(shifted))
    return jax.nn.silu(total)

def selective(activated, gate_in, step_pre, coupling_in, coupling_out, decay_log, skip_weight, keep_mask):
    step_rate = jax.nn.softplus(step_pre)
    decay_rate = -jnp.exp(decay_log)
    row_count, channels = activated.shape

    def advance(carried, inputs):
        act_row, rate_row, in_row, out_row, keep_row = inputs
        carried = carried * (keep_row * jnp.exp(rate_row[None, :] * decay_rate)) + in_row[:, None] * (rate_row * act_row)[None, :]
        return (carried, lax.optimization_barrier(jnp.sum(out_row[:, None] * carried, axis=0)))

    def block_run(carried, inputs):
        return lax.scan(advance, carried, inputs)
    block_count = row_count // 64
    inputs = (activated.reshape(block_count, 64, channels), step_rate.reshape(block_count, 64, channels), coupling_in.reshape(block_count, 64, -1), coupling_out.reshape(block_count, 64, -1), keep_mask.reshape(block_count, 64))
    initial = jnp.zeros(decay_rate.shape, jnp.float32)
    _, scan_result = lax.scan(jax.checkpoint(block_run), initial, inputs)
    mixed_out = scan_result.reshape(row_count, channels) + skip_weight[None, :] * activated
    return mixed_out * jax.nn.silu(gate_in)

def forward_group(weight_table, inputs, position):
    norm_gain, inner_weight, filter_weight, convolution_bias, select_weight, step_weight, step_bias, decay_log, skip_weight, output_weight = weight_table
    square_mean = lax.optimization_barrier(jnp.mean(inputs * inputs, axis=1, keepdims=True))
    normed = low(inputs * lax.rsqrt(square_mean + EPSILON) * norm_gain[None, :])
    projected = low_back(jnp.einsum('rd,dce->rce', normed, inner_weight, precision=HIGHEST))
    activated = conv_silu(projected[:, 0], filter_weight, convolution_bias, position)
    selected = low_back(jnp.dot(low(activated), select_weight, precision=HIGHEST))
    step_pre = low_back(jnp.dot(low(selected[:, :RANK]), step_weight, precision=HIGHEST)) + step_bias[None, :]
    keep_mask = (position > 0).astype(jnp.float32)
    gated = selective(activated, projected[:, 1], step_pre, selected[:, RANK:RANK + STATE], selected[:, RANK + STATE:], decay_log, skip_weight, keep_mask)
    return inputs + jnp.dot(low(gated), output_weight, precision=HIGHEST)

def reference(tokens, cotangent, owner_slot, sequence_lengths, norm_gain, inner_weight, filter_weight, convolution_bias, select_weight, step_weight, step_bias, decay_log, skip_weight, output_weight):
    inverse = jnp.zeros((TOKENS,), jnp.int32).at[owner_slot].set(jnp.arange(TOKENS, dtype=jnp.int32))
    owned = tokens.astype(jnp.float32)[inverse]
    owned_cot = cotangent.astype(jnp.float32)[inverse]
    group_segments = math.gcd(MB * N_DP, max(1, 4096 // TOK_MB))
    group_rows = group_segments * TOK_MB
    group_count = TOKENS // group_rows
    position_all = positions(sequence_lengths, TOK_MB).reshape(group_count, group_rows)
    weight_table = (norm_gain.astype(jnp.float32), inner_weight.astype(jnp.float32), filter_weight.astype(jnp.float32), convolution_bias.astype(jnp.float32), select_weight.astype(jnp.float32), step_weight.astype(jnp.float32), step_bias.astype(jnp.float32), decay_log.astype(jnp.float32), skip_weight.astype(jnp.float32), output_weight.astype(jnp.float32))
    checked = jax.checkpoint(forward_group)

    def run_all(weight_set, owned_rows):

        def one_group(pair):
            return checked(weight_set, pair[0], pair[1])
        return lax.map(one_group, (owned_rows.reshape(group_count, group_rows, D), position_all))
    owned_output_rows, pull = jax.vjp(run_all, weight_table, owned)
    weight_grads, owned_grad = pull(owned_cot.reshape(group_count, group_rows, D))
    output = owned_output_rows.reshape(TOKENS, D)[owner_slot].astype(jnp.bfloat16)
    input_grad = owned_grad.reshape(TOKENS, D)[owner_slot]
    return (output, input_grad, weight_grads[0], weight_grads[1], weight_grads[2], weight_grads[3], weight_grads[4], weight_grads[5], weight_grads[6], weight_grads[7], weight_grads[8], weight_grads[9])
```

```python
from functools import partial

import jax
import jax.numpy as jnp
from jax import lax
from jax.experimental import pallas as pl
from jax.experimental.pallas import tpu as pltpu
from jax.sharding import Mesh, PartitionSpec as P

MB = 2
EPSILON = 1e-05
ZK = ("z", "k")
DP = ("r", "z", "x", "k")
SWAP = [(0, 1), (1, 0)]
LOG2E = 1.4426950408889634
RESET_RATE = 1e30
LANES = 128
SUBLANES = 8
F32 = jnp.float32
BF16 = jnp.bfloat16
NT = ((1,), (1,))
TN = ((0,), (0,))


def dot(lhs, rhs, contract=((1,), (0,))):
    return lax.dot_general(lhs, rhs, (contract, ((), ())), preferred_element_type=F32)


def split_dot(lhs, rhs, contract=((1,), (0,))):
    high = lhs.astype(BF16)
    rest = (lhs - high.astype(F32)).astype(BF16)
    return dot(high, rhs, contract) + dot(rest, rhs, contract)


def shape(dims, dtype):
    return jax.ShapeDtypeStruct(dims, dtype)


def whole(kernel, name, scalars, arrays, outs, scratch=(), flops=0):
    scalars = [jnp.reshape(v, (1,)).astype(jnp.int32) for v in scalars]
    size = sum(v.size * v.dtype.itemsize for v in (*arrays, *outs))
    few, many = len(scalars), len(arrays)

    def copied(*refs):
        inputs, rest = refs[few : few + many], refs[few + many : -many - 1]
        held, semaphores = refs[-many - 1 : -1], refs[-1]
        copies = [
            pltpu.make_async_copy(source, target, semaphores.at[i])
            for i, (source, target) in enumerate(zip(inputs, held))
        ]
        for copy in copies:
            copy.start()
        for copy in copies:
            copy.wait()
        kernel(*refs[:few], *held, *rest)

    return pl.pallas_call(
        copied,
        in_specs=[pl.BlockSpec(memory_space=pltpu.SMEM)] * few
        + [pl.BlockSpec(memory_space=pl.ANY)] * many,
        out_specs=[pl.BlockSpec(memory_space=pltpu.VMEM)] * len(outs),
        out_shape=list(outs),
        scratch_shapes=[
            *scratch,
            *(pltpu.VMEM(v.shape, v.dtype) for v in arrays),
            pltpu.SemaphoreType.DMA((many,)),
        ],
        compiler_params=pltpu.CompilerParams(vmem_limit_bytes=40 << 20),
        cost_estimate=pl.CostEstimate(flops=flops, bytes_accessed=size, transcendentals=0),
        name=name,
    )(*scalars, *arrays)


def row_matches(places, count):
    rows = lax.broadcasted_iota(jnp.int32, (count, places.shape[1]), 0)
    return (rows == places).astype(F32).astype(BF16)


def column_matches(places, count):
    columns = lax.broadcasted_iota(jnp.int32, (places.shape[0], count), 1)
    return (columns == places).astype(F32).astype(BF16)


def tiles(count, size):
    return [slice(i, i + size) for i in range(0, count, size)]


def prep_kernel(x_ref, place_ref, tok_ref, cot_ref, note_ref, tok_keep, tok_send, cot_keep, cot_send):
    share = tok_keep.shape[0]
    width = tok_ref.shape[1]
    half = width // 2
    order = row_matches(place_ref[...], 2 * share)
    for source, outs in ((tok_ref, (tok_keep, tok_send)), (cot_ref, (cot_keep, cot_send))):
        rows = dot(order, source[...])
        for side in (0, 1):
            part = rows[side * share : (side + 1) * share]
            for x in (0, 1):
                same = x_ref[0] == (x ^ side)
                for zk in range(half // LANES):
                    place = (zk // 2) * 4 + zk % 2
                    zero = part[:, place * LANES : (place + 1) * LANES]
                    one = part[:, (place + 2) * LANES : (place + 3) * LANES]
                    to = slice(x * half + zk * LANES, x * half + (zk + 1) * LANES)
                    outs[side][:, to] = jnp.where(same, zero, one).astype(BF16)
    tok_keep[:, width:] = note_ref[...]
    tok_send[:, width:] = note_ref[...]


def place_rows(x_ref, place_ref, near_ref, far_ref):
    share = near_ref.shape[0] // 2
    width = near_ref.shape[1]
    half = width // 2
    order = column_matches(place_ref[...], 4 * share)
    total = None
    for group in range(4):
        source = (near_ref, far_ref)[group // 2]
        rows = slice((group % 2) * share, (group % 2 + 1) * share)
        blocks = []
        for block in range(width // LANES):
            z, x, k = block // 4, (block // 2) % 2, block % 2
            same = x_ref[0] == (x ^ (group % 2))
            at = (z * 2 + k) * LANES
            first = source[rows, at : at + LANES].astype(F32)
            second = source[rows, half + at : half + at + LANES].astype(F32)
            blocks.append(jnp.where(same, first, second).astype(BF16))
        piece = dot(order[:, group * share : (group + 1) * share], jnp.concatenate(blocks, 1))
        total = piece if total is None else total + piece
    return total


def output_kernel(x_ref, place_ref, near_ref, far_ref, tok_ref, out_ref):
    rows = place_rows(x_ref, place_ref, near_ref, far_ref)
    out_ref[...] = (tok_ref[...].astype(F32) + rows).astype(BF16)


def input_kernel(x_ref, place_ref, near_ref, far_ref, tok_ref, cot_ref, gain_ref, out_ref):
    rows = place_rows(x_ref, place_ref, near_ref, far_ref)
    x = tok_ref[...].astype(F32)
    inverse = lax.rsqrt(jnp.mean(x * x, axis=1, keepdims=True) + EPSILON)
    hat = x * inverse
    half = gain_ref.shape[1] // 2
    gains = []
    for block in range(x.shape[1] // LANES):
        z, side, k = block // 4, (block // 2) % 2, block % 2
        at = (z * 2 + k) * LANES
        gains.append(
            jnp.where(
                x_ref[0] == side,
                gain_ref[0:1, at : at + LANES],
                gain_ref[0:1, half + at : half + at + LANES],
            )
        )
    grad = rows * jnp.concatenate(gains, 1)
    out_ref[...] = cot_ref[...].astype(F32) + inverse * (
        grad - hat * jnp.mean(grad * hat, axis=1, keepdims=True)
    )


def column_sum(rows_ref, pieces):
    own, by_x, by_t, *diagonal = pieces
    depth = own.shape[0]
    near, far = rows_ref[:, :depth], rows_ref[:, depth:]
    a = dot(near, own[...]) + dot(far, by_x[...])
    b = dot(near, by_t[...])
    for i, at in enumerate(tiles(depth, diagonal[0].shape[0])):
        b = b + dot(far[:, at], diagonal[i][...])
    return a, b


def z_block(z_ref, step, size):
    return lax.rem(z_ref[0] + (size - step), size)


def row_sum(z_ref, sides, out_refs):
    depth = sides[0][1][0].shape[0]
    rows = sides[0][0].shape[0] // 2
    block = 2 * LANES
    for base in range(0, 2 * depth, block):
        at = slice(base % depth, base % depth + block)
        value = None
        for lhs, (own, by_x, by_t, *diagonal) in sides:
            part = lhs.shape[1] // 2
            if base < depth:
                near, far = own[at, :], by_t[at, :]
            else:
                size = diagonal[0].shape[0]
                inner = slice(at.start % size, at.start % size + block)
                near, far = by_x[at, :], diagonal[at.start // size][inner, :]
            term = dot(lhs[:, :part], near, NT) + dot(lhs[:, part:], far, NT)
            value = term if value is None else value + term
        place = z_block(z_ref, at.start // block, depth // block) * block
        to = pl.ds(pl.multiple_of(base // depth * depth + place, block), block)
        for i, out in enumerate(out_refs):
            out[:, to] = value[i * rows : (i + 1) * rows].astype(BF16)


def reorder_rows(z_ref, order, source, out):
    block = 2 * LANES
    half = out.shape[1] // 2
    for base in range(0, 2 * half, block):
        step = base % half // block
        place = base // half * half + z_block(z_ref, step, half // block) * block
        at = pl.ds(pl.multiple_of(place, block), block)
        out[:, base : base + block] = dot(order, source[:, at]).astype(BF16)


def grad_pieces(z_ref, channels_t, rows_ref, outs):
    part = channels_t.shape[0] // 2
    depth = rows_ref.shape[1] // 2
    for at in tiles(2 * depth, 2 * LANES):
        value = dot(channels_t, rows_ref[:, at])
        near_out, far_out = (outs[0], outs[2]) if at.start < depth else (outs[1], outs[3])
        block = 2 * z_block(z_ref, (at.start % depth) // (2 * LANES), depth // (2 * LANES))
        for i in (0, 1):
            lanes = value[:, i * LANES : (i + 1) * LANES].astype(BF16)
            for refs, rows in ((near_out, lanes[:part]), (far_out, lanes[part:])):
                size = part // len(refs)
                for j, ref in enumerate(refs):
                    ref[block + i, :, :] = rows[j * size : (j + 1) * size]


def first_pack_kernel(z_ref, k_ref, stream, gate, outer, keep, send):
    count = keep.shape[0] // 3
    part = keep.shape[2]
    for i, source in enumerate((stream, gate, outer)):
        for step in range(count):
            z = lax.rem(z_ref[0] + step, count)
            for out, core in ((keep, k_ref[0]), (send, 1 - k_ref[0])):
                at = pl.ds(pl.multiple_of((z * 2 + core) * part, part), part)
                out[i * count + step] = source[:, at]


def second_pack_kernel(k_ref, kept, got, *outs):
    first = k_ref[0] == 0
    height = kept.shape[1]
    for i, out in enumerate(outs):
        mine, other = kept[i].astype(F32), got[i].astype(F32)
        out[:height, :] = jnp.where(first, mine, other).astype(BF16)
        out[height:, :] = jnp.where(first, other, mine).astype(BF16)


def down(value, count):
    if count == 0:
        return value
    return jnp.concatenate([jnp.zeros((count, value.shape[1]), value.dtype), value[:-count]], 0)


def up(value, count):
    if count == 0:
        return value
    return jnp.concatenate([value[count:], jnp.zeros((count, value.shape[1]), value.dtype)], 0)


def lag_masks(place, taps):
    return [None] + [place >= lag for lag in range(1, taps)]


def masked(value, mask):
    return value if mask is None else jnp.where(mask, value, 0.0)


def filter_sum(stream, masks, weights):
    taps = len(masks)
    total = weights[taps : taps + 1, :] + weights[taps - 1 : taps, :] * stream
    for lag in range(1, taps):
        total = total + weights[taps - 1 - lag : taps - lag, :] * masked(
            down(stream, SUBLANES * lag), masks[lag]
        )
    return total


def places(notes, rows, per_device):
    segments = len(notes) * MB
    zero = lax.broadcasted_iota(jnp.int32, (segments, LANES), 0) % MB
    lane = lax.broadcasted_iota(jnp.int32, (segments, LANES), 1)
    table = jnp.concatenate([v for v in notes for _ in range(MB)], 0)
    begin = jnp.zeros((segments, 1), F32)
    step = lax.broadcasted_iota(jnp.int32, (rows, LANES), 0) // segments
    step = step.astype(F32)
    latest = jnp.zeros((rows, LANES), F32)
    for i in range(per_device - 1):
        picked = jnp.where(lane == zero * per_device + i, table, 0.0)
        begin = begin + jnp.sum(picked, axis=1, keepdims=True)
        every = jnp.concatenate(
            [jnp.broadcast_to(begin, (segments, LANES))] * (rows // segments), 0
        )
        latest = jnp.where(every <= step, every, latest)
    return step - latest


def front_kernel(
    sizes, core_ref, tensor_ref, z_ref, x_ref, place_ref, own, by_x, by_t, low, high, par_ref, sel_ref,
    n_ref, stream_ref, act_ref, mine_ref, other_ref, pos_ref, gain_ref, nrm, act_low,
):
    taps, per_device = sizes
    rows = x_ref.shape[0]
    width = n_ref.shape[1]
    depth = width // 2
    part = own.shape[1]
    members = depth // LANES
    share = rows // (2 * members)
    note = slice(width, width + LANES)
    for side in (0, 1):
        for member in range(members):
            row = member * 2 * share + side * share
            at = side * depth + member * LANES
            gain_ref[0:1, at : at + LANES] = x_ref[row : row + 16, note].astype(F32)[0:1]
    notes = []
    for z in range(members // 2):
        two = [
            x_ref[m * 2 * share : m * 2 * share + 16, note].astype(F32)[1:2]
            for m in (2 * z, 2 * z + 1)
        ]
        notes.append(jnp.where(tensor_ref[0] == 0, two[0], two[1]))
    place = places(notes, rows, per_device)
    pos_ref[...] = place

    def norm(i, _):
        at = pl.ds(pl.multiple_of(i * 64, 64), 64)
        x = x_ref[at, :width].astype(F32)
        inverse = lax.rsqrt(jnp.mean(x * x, axis=1, keepdims=True) + EPSILON)
        nrm[at, :] = (x * inverse * gain_ref[0:1, :]).astype(BF16)
        return 0

    lax.fori_loop(0, rows // 64, norm, 0)
    reorder_rows(z_ref, row_matches(place_ref[...], rows), nrm, n_ref)
    near, far = column_sum(n_ref, (own, by_x, by_t, low, high))
    stream_ref[:, :part] = near
    stream_ref[:, part:] = far
    masks = lag_masks(place, taps)
    for at in tiles(2 * part, LANES):
        filtered = filter_sum(stream_ref[:, at], masks, par_ref[:, at])
        act = filtered * jax.nn.sigmoid(filtered)
        act_ref[:, at] = act
        act_low[:, at] = act.astype(BF16)
    selected = dot(sel_ref[...], act_low[...], NT)
    first = core_ref[0] == 0
    mine_ref[...] = jnp.where(first, selected[:, : rows // 2], selected[:, rows // 2 :])
    other_ref[...] = jnp.where(first, selected[:, rows // 2 :], selected[:, : rows // 2])


def late_kernel(z_ref, cot_ref, place_ref, n_ref, *refs):
    gate_pieces, out_pieces = refs[:4], refs[4:8]
    up_ref, gate_ref, gg_ref = refs[8:]
    part = gate_pieces[0].shape[1]
    reorder_rows(z_ref, row_matches(place_ref[...], cot_ref.shape[0]), cot_ref, up_ref)
    for source, out, pieces in ((n_ref, gate_ref, gate_pieces), (up_ref, gg_ref, out_pieces)):
        near, far = column_sum(source, pieces)
        out[:, :part] = near
        out[:, part:] = far


def out_kernel(z_ref, place_ref, gated_ref, *refs):
    order = column_matches(place_ref[...], gated_ref.shape[0])
    rows = dot(order, gated_ref[...]).astype(BF16)
    row_sum(z_ref, [(rows, refs[:4])], refs[4:])


def late_grad_kernel(z_ref, n_ref, up_ref, gate_grad_ref, gated_ref, *outs):
    for i, (source, rows_ref) in enumerate(((gate_grad_ref, n_ref), (gated_ref, up_ref))):
        grad_pieces(
            z_ref, source[...].astype(F32).T.astype(BF16), rows_ref, [[v] for v in outs[4 * i : 4 * i + 4]]
        )


def back_kernel(
    taps, core_ref, z_ref, total_ref, rest_ref, pos_ref, stream_ref, sact_ref, par_ref, sel_ref, n_ref,
    low_ref, small_ref, *refs,
):
    *outs, act_low, grad_t = refs
    rows, channels = stream_ref.shape
    first = core_ref[0] == 0
    total, rest = total_ref[...], rest_ref[...]
    selected_t = jnp.concatenate(
        [jnp.where(first, total, rest), jnp.where(first, rest, total)], 1
    )
    selected_low = selected_t.astype(BF16)
    count = selected_t.shape[0]
    padded = jnp.concatenate(
        [selected_t, jnp.zeros((-count % LANES, rows), F32)], 0
    )
    selected = padded.T.astype(BF16)
    masks = lag_masks(pos_ref[...], taps)
    spare = jnp.zeros((SUBLANES - taps - 1, LANES), F32)
    for at in tiles(channels, LANES):
        stream = stream_ref[:, at]
        weights = par_ref[:, at]
        filtered = filter_sum(stream, masks, weights)
        slope = jax.nn.sigmoid(filtered)
        act_low[:, at] = (filtered * slope).astype(BF16)
        select = jnp.concatenate(
            [sel_ref[:, at], jnp.zeros((-count % LANES, LANES), BF16)], 0
        )
        act_grad = sact_ref[:, at] + dot(selected, select)
        grad = act_grad * (slope * (1.0 + filtered * (1.0 - slope)))
        stream_grad = weights[taps - 1 : taps, :] * grad
        sums = [jnp.sum(grad * stream, axis=0, keepdims=True)]
        for lag in range(1, taps):
            part_grad = masked(grad, masks[lag])
            sums.append(
                jnp.sum(part_grad * down(stream, SUBLANES * lag), axis=0, keepdims=True)
            )
            stream_grad = stream_grad + weights[taps - 1 - lag : taps - lag, :] * up(
                part_grad, SUBLANES * lag
            )
        sums = sums[::-1] + [jnp.sum(grad, axis=0, keepdims=True), spare]
        small_ref[count:, at] = jnp.concatenate(sums, 0).astype(BF16)
        low_ref[:, at] = stream_grad.astype(BF16)
        grad_t[at, :] = stream_grad.T.astype(BF16)
    small_ref[:count, :] = dot(selected_low, act_low[...]).astype(BF16)
    grad_pieces(z_ref, grad_t[...], n_ref, [outs[2 * i : 2 * i + 2] for i in range(4)])


def in_kernel(z_ref, place_ref, low_ref, gate_grad_ref, *refs):
    stream_pieces, gate_pieces, outs, stage = refs[:5], refs[5:9], refs[9:11], refs[11]
    channels = low_ref.shape[1]
    order = column_matches(place_ref[...], low_ref.shape[0])
    stage[:, :channels] = dot(order, low_ref[...]).astype(BF16)
    stage[:, channels:] = dot(order, gate_grad_ref[...]).astype(BF16)
    row_sum(
        z_ref, [(stage[:, :channels], stream_pieces), (stage[:, channels:], gate_pieces)], outs
    )


def small_kernel(
    sizes, z_ref, k_ref, *refs,
):
    count, states, taps = sizes
    blocks = refs[:-7]
    select, step_w, decay, filters, filter_b, step_b, skip = refs[-7:]
    part = blocks[0].shape[1]
    zs = len(blocks) // 2
    rank = step_w.shape[0]
    for i, block in enumerate(blocks):
        core = k_ref[0] if i % 2 == 0 else 1 - k_ref[0]
        place = (z_block(z_ref, i // 2, zs) * 2 + core) * part
        at = pl.ds(pl.multiple_of(place, part), part)
        first = block[: states + 8, :].astype(F32)
        step_b[:, at] = first[0:1]
        skip[:, at] = first[1:2]
        decay[:, at] = first[8:]
        step_w[:, at] = block[states + 8 : states + 8 + rank, :].astype(F32)
        rest = block[states + 8 + rank :, :].astype(F32)
        filters[:, at] = rest[count : count + taps]
        filter_b[:, at] = rest[count + taps : count + taps + 1]
        chosen = jnp.concatenate([rest[:count], jnp.zeros((-count % LANES, part), F32)], 0)
        select[at, :] = chosen.T[:, :count]


def scan_kernel(
    layout, core_ref, pos_ref, act_ref, gate_ref, gg_ref, total_ref, rest_ref, sw_ref, par_ref,
    gated_ref, gateg_ref, sact_ref, small_ref, mine_ref, other_ref,
    bb, cb, hist, fac, ci_acc, co_acc, rate_s, reff_s, u_s, ds_s, y_s, s2_s, decb, sel_t, rate_low, rank_t,
):
    rank_width, states, bias_row, decay_row, skip_row = layout
    rows, lanes = act_ref.shape
    steps = rows // SUBLANES
    block = pl.program_id(0)
    wide = states * lanes
    first = core_ref[0] == 0
    spread = (
        lax.broadcasted_iota(jnp.int32, (states, wide), 1) // lanes
        == lax.broadcasted_iota(jnp.int32, (states, wide), 0)
    ).astype(F32).astype(BF16)

    @pl.when(block == 0)
    def _():
        total, rest = total_ref[...], rest_ref[...]
        sel_t[:, : rows // 2] = jnp.where(first, total, rest)
        sel_t[:, rows // 2 :] = jnp.where(first, rest, total)
        rate_low[...] = sel_t[:rank_width, :].T.astype(BF16)
        bb[...] = split_dot(sel_t[rank_width : rank_width + states, :], spread, TN)
        cb[...] = split_dot(sel_t[rank_width + states :, :], spread, TN)
        hist[0:SUBLANES, :] = jnp.zeros((SUBLANES, wide), F32)
        ci_acc[...] = jnp.zeros_like(ci_acc)
        co_acc[...] = jnp.zeros_like(co_acc)
        rank_t[...] = jnp.zeros_like(rank_t)

    decay = -jnp.exp(par_ref[decay_row : decay_row + states, :])
    for n in range(states):
        decb[8 * n : 8 * n + 8, :] = jnp.broadcast_to(decay[n : n + 1, :], (8, lanes))

    step_pre = dot(rate_low[...], sw_ref[...]) + par_ref[bias_row : bias_row + 1, :]
    step_slope = jax.nn.sigmoid(step_pre)
    rate = jnp.maximum(step_pre, 0.0) + jnp.log1p(jnp.exp(-jnp.abs(step_pre)))
    rate_s[...] = rate
    reff_s[...] = jnp.where(pos_ref[...] > 0.0, rate * LOG2E, RESET_RATE)
    u_s[...] = rate * act_ref[...]
    gate = gate_ref[...]
    ds_s[...] = gg_ref[...] * (gate * jax.nn.sigmoid(gate))

    def cols(n):
        return slice(n * lanes, (n + 1) * lanes)

    def forward(t, h):
        row = pl.ds(pl.multiple_of(t * 8, 8), 8)
        next_row = pl.ds(pl.multiple_of(t * 8 + 8, 8), 8)
        reff = reff_s[row, :]
        u = u_s[row, :]
        y = jnp.zeros((8, lanes), F32)
        fresh = []
        for n in range(states):
            a = jnp.exp2(reff * decb[8 * n : 8 * n + 8, :])
            hn = a * h[n] + bb[row, cols(n)] * u
            hist[next_row, cols(n)] = hn
            fac[row, cols(n)] = a
            y = y + cb[row, cols(n)] * hn
            fresh.append(hn)
        y_s[row, :] = y
        return tuple(fresh)

    zero = jnp.zeros((8, lanes), F32)
    lax.fori_loop(0, steps, forward, (zero,) * states)

    def backward(i, carried):
        g, dacc = carried
        t = steps - 1 - i
        row = pl.ds(pl.multiple_of(t * 8, 8), 8)
        next_row = pl.ds(pl.multiple_of(t * 8 + 8, 8), 8)
        ds = ds_s[row, :]
        u = u_s[row, :]
        rt = rate_s[row, :]
        s1 = jnp.zeros((8, lanes), F32)
        s2 = jnp.zeros((8, lanes), F32)
        g_new, d_new = [], []
        for n in range(states):
            lam = cb[row, cols(n)] * ds + g[n]
            q = lam * fac[row, cols(n)]
            hp = hist[row, cols(n)] * q
            s1 = s1 + hp * decb[8 * n : 8 * n + 8, :]
            s2 = s2 + lam * bb[row, cols(n)]
            ci_acc[row, cols(n)] += lam * u
            co_acc[row, cols(n)] += ds * hist[next_row, cols(n)]
            g_new.append(q)
            d_new.append(dacc[n] + hp * rt)
        s2_s[row, :] = s2
        reff_s[row, :] = s1
        return tuple(g_new), tuple(d_new)

    _, dacc = lax.fori_loop(0, steps, backward, ((zero,) * states, (zero,) * states))

    act = act_ref[...]
    skip = par_ref[skip_row : skip_row + 1, :]
    scanned = y_s[...] + skip * act
    sig = jax.nn.sigmoid(gate)
    gated_ref[...] = (scanned * (gate * sig)).astype(BF16)
    gateg_ref[...] = (gg_ref[...] * scanned * (sig * (1.0 + gate * (1.0 - sig)))).astype(BF16)
    s2_all = s2_s[...]
    dscan = ds_s[...]
    sact_ref[...] = rate_s[...] * s2_all + skip * dscan
    spre = (reff_s[...] + act * s2_all) * step_slope
    spre_low = spre.astype(BF16)
    sums = [jnp.sum(spre, axis=0, keepdims=True), jnp.sum(dscan * act, axis=0, keepdims=True)]
    sums.append(jnp.zeros((6, lanes), F32))
    for n in range(states):
        sums.append(jnp.sum(dacc[n], axis=0, keepdims=True) * decb[8 * n : 8 * n + 1, :])
    small_ref[: states + 8, :] = jnp.concatenate(sums, 0).astype(BF16)
    small_ref[states + 8 :, :] = dot(
        sel_t[:rank_width, :].astype(BF16), spre_low
    ).astype(BF16)
    rank_t[...] += dot(sw_ref[...], spre_low, NT)

    @pl.when(block == pl.num_programs(0) - 1)
    def _():
        high, low = slice(0, rows // 2), slice(rows // 2, rows)
        for acc, base in ((ci_acc, rank_width), (co_acc, rank_width + states)):
            sums_t = split_dot(acc[...], spread, NT).T
            sel_t[base : base + states, :] = sums_t
        sel_t[:rank_width, :] = rank_t[...]
        mine_ref[...] = jnp.where(first, sel_t[:, high], sel_t[:, low])
        other_ref[...] = jnp.where(first, sel_t[:, low], sel_t[:, high])


def mixer(layout, core, position, act, gate, gated_grad, total, rest, step_w, params):
    rows, channels = act.shape
    rank_width, states = layout[:2]
    lanes = LANES
    count = total.shape[0]

    def block(height):
        return pl.BlockSpec((height, lanes), lambda i: (0, i))

    def fixed(*dims):
        return pl.BlockSpec(dims, lambda i: (0, 0))

    tall = block(rows)
    wide = states * lanes
    return pl.pallas_call(
        partial(scan_kernel, layout),
        grid=(channels // lanes,),
        in_specs=[
            pl.BlockSpec(memory_space=pltpu.SMEM), fixed(rows, lanes), tall, tall, tall,
            fixed(count, rows // 2), fixed(count, rows // 2), block(rank_width),
            block(params.shape[0]),
        ],
        out_specs=[
            tall, tall, tall, block(rank_width + states + 8),
            fixed(count, rows // 2), fixed(count, rows // 2),
        ],
        out_shape=[
            shape((rows, channels), BF16), shape((rows, channels), BF16),
            shape((rows, channels), F32), shape((rank_width + states + 8, channels), BF16),
            shape((count, rows // 2), F32), shape((count, rows // 2), F32),
        ],
        scratch_shapes=[
            pltpu.VMEM((rows, wide), F32),
            pltpu.VMEM((rows, wide), F32),
            pltpu.VMEM((rows + 8, wide), F32),
            pltpu.VMEM((rows, wide), F32),
            pltpu.VMEM((rows, wide), F32),
            pltpu.VMEM((rows, wide), F32),
        ]
        + [pltpu.VMEM((rows, lanes), F32)] * 6
        + [
            pltpu.VMEM((8 * states, lanes), F32), pltpu.VMEM((count, rows), F32),
            pltpu.VMEM((rows, rank_width), BF16), pltpu.VMEM((rank_width, rows), F32),
        ],
        compiler_params=pltpu.CompilerParams(
            dimension_semantics=("arbitrary",), vmem_limit_bytes=48 << 20
        ),
        cost_estimate=pl.CostEstimate(
            flops=20 * rows * channels * states,
            bytes_accessed=30 * rows * channels,
            transcendentals=rows * channels * states,
        ),
        name="mixer",
    )(jnp.reshape(core, (1,)).astype(jnp.int32), position, act, gate, gated_grad, total, rest, step_w, params)


def after(value, *others):
    return lax.optimization_barrier((value, others))[0]


def swap(value, axis, name="swap"):
    with jax.named_scope(f"{name}_{axis}"):
        return lax.ppermute(value, axis, SWAP)


def sum_zk(mine, other, fillers=()):
    fillers = list(fillers) + [()] * 8
    total = mine + after(swap(other, "k", "select"), fillers.pop(0))
    first = None
    size = lax.axis_size("z")
    distance = 1
    while distance < size:
        sent = total.astype(BF16)
        got = lax.ppermute(sent, "z", [(i, i ^ distance) for i in range(size)])
        total = sent.astype(F32) + after(got, fillers.pop(0)).astype(F32)
        first = total if first is None else first
        distance *= 2
    return total, swap(total, "k", "select_rest"), first


def return_core(mine, other):
    return (mine.astype(F32) + swap(other, "k", "rows").astype(F32)).astype(BF16)


def return_rows(total):
    rows = lax.psum_scatter(total, "z", scatter_dimension=0, tiled=True)
    share = rows.shape[0] // 2
    near = jnp.concatenate([rows[:share], swap(rows[share:], "x", "rows")], 0)
    return near, swap(near, "t", "rows")


def exchange_halves(low, high):
    low_x, high_t = swap(low, "x", "gate_w"), swap(high, "t", "outer_w")
    low_t, high_x = swap(low, "t", "gate_w"), swap(high, "x", "outer_w")
    low_d, high_d = swap(low_x, "t", "gate_w_far"), swap(high_t, "x", "outer_w_far")
    return (low, low_x, low_t, low_d), (high, high_x, high_t, high_d)


def exchange_weight(own):
    half = own.shape[0] // 2
    by_x = swap(own, "x", "stream_w")
    by_t = swap(own, "t", "stream_w")
    low = swap(by_x[:half], "t", "stream_w_far")
    return own, by_x, by_t, low, swap(by_t[half:], "x", "stream_w_far")


def plus(value, *more):
    total = value.astype(F32)
    for v in more:
        total = total + v.astype(F32)
    return total.astype(BF16)


def diagonal_grads(low, high, name):
    return swap(low[3], "x", name + "_far"), swap(high[3], "t", name + "_far")


def first_grads(low, high, name):
    return swap(low[1], "x", name), swap(high[2], "t", name)


def second_grads(low, high, diagonal, name, ready=()):
    low_t = swap(plus(low[2], after(diagonal[0], ready)), "t", name + "_sum")
    high_x = swap(plus(high[1], after(diagonal[1], ready)), "x", name + "_sum")
    return low_t, high_x


def to_owners(value):
    return lax.all_to_all(value, ZK, 0, 0, tiled=True)


def rank_in_class(keys):
    count = keys.shape[1]
    earlier = jnp.arange(count)[:, None] > jnp.arange(count)[None, :]
    same = (keys[:, :, None] == keys[:, None, :]) & earlier[None]
    return jnp.sum(same.astype(jnp.int32), axis=2)


def body(
    tokens, cotangent, owner_slot, sequence_lengths, norm_gain, inner_weight, filter_weight,
    convolution_bias, select_weight, step_weight, step_bias, decay_log, skip_weight, output_weight,
):
    rings = lax.axis_size("r")
    zs = lax.axis_size("z")
    members = zs * 4
    ri, zi, xi, ki, ti = (lax.axis_index(a) for a in ("r", "z", "x", "k", "t"))
    local_rows, width = tokens.shape
    rank_width = step_weight.shape[0]
    states = decay_log.shape[0]
    taps = filter_weight.shape[0]
    half_channels = inner_weight.shape[2]
    part = half_channels // (2 * zs)
    channels = 2 * part
    block_rows = inner_weight.shape[0]
    ring_rows = rings * block_rows
    depth = width // 2
    batch_rows = local_rows // MB
    group_rows = zs * local_rows
    segments = group_rows // batch_rows
    share = local_rows // 4

    def to_blocks(value):
        if rings == 1:
            return value
        value = value.reshape(-1, rings, members, block_rows)
        return value.transpose(0, 2, 1, 3).reshape(-1, width)

    def from_blocks(value):
        if rings == 1:
            return value
        value = value.reshape(-1, members, rings, block_rows)
        return value.transpose(0, 2, 1, 3).reshape(-1, width)

    inner = inner_weight
    outer = output_weight.T
    gain = norm_gain[None, :]
    if rings > 1:
        inner = lax.all_gather(inner, "r", axis=0, tiled=True)
        outer = lax.all_gather(outer, "r", axis=0, tiled=True)
        gain = lax.all_gather(gain, "r", axis=1, tiled=True)

    blocks_w = 3 * zs
    kept, sent = whole(
        first_pack_kernel, "pack", [zi, ki], (inner[:, 0], inner[:, 1], outer),
        [shape((blocks_w, ring_rows, part), BF16)] * 2,
    )
    packed = whole(
        second_pack_kernel, "pack_cores", [ki], (kept, swap(sent, "k", "weights")),
        [shape((2 * ring_rows, part), BF16)] * blocks_w,
    )

    def from_z(blocks, name, ready=()):
        blocks = after(blocks, ready)
        got = [blocks[0]]
        for step in range(1, zs):
            with jax.named_scope(name):
                got.append(
                    lax.ppermute(blocks[step], "z", [(i, (i + step) % zs) for i in range(zs)])
                )
        return jnp.concatenate(got, 0)

    stream_own = from_z(packed[:zs], "stream_w_z")
    ws = exchange_weight(stream_own)
    gate_own = from_z(packed[zs : 2 * zs], "gate_w_z", stream_own)
    outer_own = from_z(packed[2 * zs :], "outer_w_z", gate_own)
    wg, wo = exchange_halves(gate_own, outer_own)

    slot_rows = owner_slot.reshape(rings, members, local_rows)
    tok, cot = tokens, cotangent
    ring_block = members * local_rows
    if rings > 1:
        per_ring = local_rows // rings
        flat = slot_rows.reshape(rings * members, local_rows)
        target = flat // ring_block
        place = target * per_ring + rank_in_class(target)
        chosen = jnp.arange(local_rows, dtype=jnp.int32)[None, :, None] == place[:, None, :]
        ordered = jnp.sum(jnp.where(chosen, flat[:, None, :], 0), axis=2)
        ordered = ordered.reshape(rings, members, rings, per_ring)
        ordered = lax.dynamic_index_in_dim(ordered, ri, 2, keepdims=False)
        slots = ordered.transpose(1, 0, 2).reshape(members, local_rows)
        own_place = lax.dynamic_index_in_dim(place, ri * members + zi * 4 + xi * 2 + ki, 0, False)
        ring_order = (
            jnp.arange(local_rows, dtype=jnp.int32)[:, None] == own_place[None, :]
        ).astype(BF16)

        def over_rings(value):
            value = value.reshape(rings, per_ring, width)
            return lax.all_to_all(value, "r", 0, 0, tiled=True).reshape(local_rows, width)

        tok, cot = (over_rings(dot(ring_order, v).astype(BF16)) for v in (tokens, cotangent))
    else:
        slots = slot_rows[0]
    local_slot = slots - ri * ring_block
    owner = local_slot // local_rows
    owner_z, owner_x, owner_k = owner // 4, (owner // 2) % 2, owner % 2
    rank = rank_in_class(owner_x * 2 + owner_k)
    in_owner = local_slot % local_rows
    scan_place = (in_owner % batch_rows) * segments + owner_z * MB + in_owner // batch_rows
    here = zi * 4 + xi * 2 + ki
    mine = [lax.dynamic_index_in_dim(v, here, 0, False) for v in (owner_x, owner_k, rank)]
    send_place = (mine[1] ^ ti) * (2 * share) + (mine[0] ^ xi) * share + mine[2]
    in_group = (owner_x == xi) & (owner_k == ti)
    ranked = (
        jnp.arange(share, dtype=jnp.int32)[None, :, None] == rank[:, None, :]
    ) & in_group[:, None, :]
    arrival = jnp.sum(jnp.where(ranked, scan_place[:, None, :], 0), axis=2)
    arrival = arrival.reshape(zs, 2, 2, share)
    arrival = jnp.where(xi == 0, arrival, arrival[:, ::-1]).transpose(0, 2, 1, 3)
    arrived = arrival.reshape(1, group_rows)
    returned = jnp.where(ki == 0, arrival, arrival[:, ::-1]).transpose(1, 0, 2, 3)
    returned = returned.reshape(group_rows, 1)

    blocks = [to_blocks(tok), to_blocks(cot)]
    lengths = sequence_lengths.reshape(1, -1).astype(BF16)
    lengths = jnp.concatenate([lengths, jnp.zeros((1, ring_rows - lengths.shape[1]), BF16)], 1)
    note = jnp.concatenate([gain, lengths, jnp.zeros((share - 2, ring_rows), BF16)], 0)
    noted, plain = shape((share, width + LANES), BF16), shape((share, width), BF16)
    rows_out = whole(
        prep_kernel, "prep", [xi], (send_place[None], *blocks, note), [noted, noted, plain, plain]
    )
    group_tokens = lax.all_gather(
        jnp.concatenate([rows_out[0], swap(rows_out[1], "x", "tokens")], 0), ZK, axis=0, tiled=True
    )

    first = (zi * 2 + ki) * part

    def own_channels(value):
        return lax.dynamic_slice_in_dim(value, first, part, 1)

    rows_f = taps + 3 + states
    floats = own_channels(
        jnp.concatenate(
            [
                filter_weight, convolution_bias[None], step_bias[None], decay_log,
                skip_weight[None], jnp.zeros((-rows_f % 8, half_channels), F32),
            ],
            axis=0,
        )
    )
    params = jnp.concatenate([floats, swap(floats, "t", "params")], axis=1)
    layout = (rank_width, states, taps + 1, taps + 2, taps + 2 + states)
    select_t = lax.dynamic_slice_in_dim(select_weight, first, part, 0).T
    lows = jnp.concatenate([own_channels(step_weight), select_t], 0)
    lows = jnp.concatenate([lows, swap(lows, "t", "params_low")], axis=1)
    step_w, select_w = lows[:rank_width], lows[rank_width:]

    count = select_w.shape[0]
    half_out = [shape((count, group_rows // 2), F32)] * 2
    full = shape((group_rows, channels), F32)
    wide_low = shape((group_rows, width), BF16)
    normed, stream, act, sel_mine, sel_other, position, gain_row = whole(
        partial(front_kernel, (taps, sequence_lengths.shape[1])), "front", [ki, ti, zi],
        (after(group_tokens, gate_own), arrived, *ws, params, select_w),
        [wide_low, full, full, *half_out, shape((group_rows, LANES), F32), shape((8, width), F32)],
        [pltpu.VMEM((group_rows, width), BF16), pltpu.VMEM((group_rows, channels), BF16)],
        flops=4 * group_rows * width * channels,
    )
    total, rest, _ = sum_zk(sel_mine, sel_other, ((), outer_own, (wg[1], wg[2])))
    cot_keep, cot_send = after((rows_out[2], rows_out[3]), gate_own)
    group_cot = lax.all_gather(
        jnp.concatenate([cot_keep, swap(cot_send, "x", "cot")], 0), ZK, axis=0, tiled=True
    )
    upstream, gate, gated_grad = whole(
        late_kernel, "late", [zi], (group_cot, arrived, normed, *wg, *wo), [wide_low, full, full],
        flops=6 * group_rows * width * channels,
    )
    gated, gate_grad, act_grad, small_a, sel_mine, sel_other = mixer(
        layout, ki, position, act, gate, gated_grad, total, rest, step_w, params
    )

    half_rows = [shape((group_rows // 2, width), BF16)] * 2
    out_mine, out_other = whole(
        out_kernel, "out_rows", [zi], (returned, gated, *wo), half_rows,
        flops=2 * group_rows * width * channels,
    )
    pieces = whole(
        late_grad_kernel, "late_grad", [zi], (normed, upstream, after(gate_grad, out_mine), gated),
        [shape((2 * zs, part, ring_rows), BF16)] * 8,
        flops=4 * group_rows * width * channels,
    )
    late_diagonal = diagonal_grads(pieces[:4], pieces[4:], "late_g")
    total, rest, first_sum = sum_zk(sel_mine, sel_other, (out_mine, pieces))
    out_total = return_core(out_mine, out_other)
    late_first = first_grads(
        *after((pieces[:4], pieces[4:]), first_sum), "late_g"
    )
    near, far = return_rows(out_total)
    total = after(total, late_diagonal, out_total)
    back_place = send_place[:, None]
    if rings > 1:
        zero = jnp.zeros_like(tokens)
        rows = whole(
            output_kernel, "output", [xi], (back_place, near, far, zero), [shape(tokens.shape, BF16)]
        )[0]
        rows = from_blocks(over_rings(rows))
        output = (tokens.astype(F32) + dot(ring_order, rows, TN)).astype(BF16)
    else:
        output = whole(
            output_kernel, "output", [xi], (back_place, near, far, tokens), [shape(tokens.shape, BF16)]
        )[0]
    low, small_b, *stream_pieces = whole(
        partial(back_kernel, taps), "back", [ki, zi],
        (total, rest, position, stream, act_grad, params, select_w, normed),
        [shape((group_rows, channels), BF16), shape((count + 8, channels), BF16)]
        + [shape((2 * zs, part // 2, ring_rows), BF16)] * 8,
        [pltpu.VMEM((group_rows, channels), BF16), pltpu.VMEM((channels, group_rows), BF16)],
        flops=4 * group_rows * width * channels,
    )
    in_mine, in_other = whole(
        in_kernel, "in_rows", [zi], (returned, low, gate_grad, *ws, *wg),
        half_rows, [pltpu.VMEM((group_rows, 2 * channels), BF16)],
        flops=4 * group_rows * width * channels,
    )
    in_total = return_core(in_mine, in_other)
    late_second = second_grads(pieces[:4], pieces[4:], late_diagonal, "late_g")
    sides = after((stream_pieces[::2], stream_pieces[1::2]), in_total)
    stream_diagonal = diagonal_grads(*sides, "stream_g")
    stream_first = first_grads(*sides, "stream_g")
    stream_second = second_grads(*sides, stream_diagonal, "stream_g")
    late_sum = jnp.concatenate(
        [
            plus(pieces[0], late_first[0], late_second[0]),
            plus(pieces[4], late_first[1], late_second[1]),
        ],
        axis=1,
    )
    late_home = to_owners(late_sum)
    gate_home, outer_home = late_home[:, :part], late_home[:, part:]
    outer_home = outer_home.reshape(half_channels, ring_rows).astype(F32)
    if rings > 1:
        outer_home = lax.psum_scatter(outer_home, "r", scatter_dimension=1, tiled=True)
    stream_sum = jnp.concatenate(
        [
            plus(sides[0][0], stream_first[0], stream_second[0]),
            plus(sides[1][0], stream_first[1], stream_second[1]),
        ],
        axis=1,
    )
    stream_home = to_owners(after(stream_sum, late_home))
    near, far = return_rows(in_total)
    if rings > 1:
        zero = jnp.zeros_like(tokens)
        rows = whole(
            output_kernel, "rows_back", [xi], (back_place, near, far, zero), [shape(tokens.shape, BF16)]
        )[0]
        rows = dot(ring_order, from_blocks(over_rings(rows)), TN)
        own_x = tokens.astype(F32)
        inverse = lax.rsqrt(jnp.mean(own_x * own_x, axis=1, keepdims=True) + EPSILON)
        hat = own_x * inverse
        gain_rel = gain_row[:1].reshape(2, zs, 2, ring_rows)
        gain_abs = jnp.where(xi == 0, gain_rel, gain_rel[::-1]).transpose(1, 0, 2, 3)
        grad = rows * from_blocks(gain_abs.reshape(1, width))
        input_grad = cotangent.astype(F32) + inverse * (
            grad - hat * jnp.mean(grad * hat, axis=1, keepdims=True)
        )
    else:
        input_grad = whole(
            input_kernel, "input_grad", [xi],
            (back_place, near, far, tokens, cotangent, gain_row), [shape(tokens.shape, F32)],
        )[0]
    inner_home = jnp.stack(
        [v.reshape(half_channels, ring_rows).T for v in (stream_home, gate_home)], axis=1
    ).astype(F32)
    if rings > 1:
        inner_home = lax.psum_scatter(inner_home, "r", scatter_dimension=0, tiled=True)
    gain_grad = jnp.sum(inner_home * inner_weight.astype(F32), axis=(1, 2))
    gain_grad = (gain_grad + swap(gain_grad, "t", "gain")) / norm_gain.astype(F32)

    small = after(jnp.concatenate([small_a, small_b], axis=0), stream_diagonal)
    small = plus(small[:, :part], swap(small[:, part:], "t", "small"))
    small = after(small, late_second)
    small = plus(small, swap(small, "x", "small"))
    if rings > 1:
        small = lax.psum(small.astype(F32), "r").astype(BF16)
    gathered = []
    for step in range(zs):
        with jax.named_scope("small_z"):
            block = small if step == 0 else lax.ppermute(
                small, "z", [(i, (i + step) % zs) for i in range(zs)]
            )
        gathered += [block, swap(block, "k", "small")]
    one_row = shape((1, half_channels), F32)
    select_grad, step_w_grad, decay_grad, filter_grad, filter_b_grad, step_b_grad, skip_grad = whole(
        partial(small_kernel, (count, states, taps)), "small", [zi, ki], gathered,
        [
            shape((half_channels, count), F32), shape((rank_width, half_channels), F32),
            shape((states, half_channels), F32), shape((taps, half_channels), F32),
            one_row, one_row, one_row,
        ],
    )
    return (
        output,
        input_grad,
        gain_grad,
        inner_home,
        filter_grad,
        filter_b_grad[0],
        select_grad,
        step_w_grad,
        step_b_grad[0],
        decay_grad,
        skip_grad[0],
        outer_home,
    )


def solution(mesh):
    devices = mesh.devices
    split = Mesh(
        devices.reshape(devices.shape[0] // 16, 4, 2, 2, devices.shape[1]), DP + ("t",)
    )
    in_specs = (
        P(DP, None), P(DP, None), P(), P(DP, None), P(DP), P(DP, None, "t"), P(None, "t"), P("t"),
        P("t", None), P(None, "t"), P("t"), P(None, "t"), P("t"), P("t", DP),
    )
    out_specs = (
        P(DP, None), P(DP, None), P(DP), P(DP, None, "t"), P(None, "t"), P("t"), P("t", None),
        P(None, "t"), P("t"), P(None, "t"), P("t"), P("t", DP),
    )
    return jax.shard_map(body, mesh=split, in_specs=in_specs, out_specs=out_specs, check_vma=False)
```

```python
from functools import partial

import jax
import jax.numpy as jnp
from jax import lax
from jax.experimental import pallas as pl
from jax.experimental.pallas import tpu as pltpu
from jax.sharding import Mesh, PartitionSpec as P

MB = 2
EPSILON = 1e-05
ZK = ("z", "k")
DP = ("r", "z", "x", "k")
SWAP = [(0, 1), (1, 0)]
LOG2E = 1.4426950408889634
RESET_RATE = 1e30
LANES = 128
SUBLANES = 8
SIDE = 2
GROUP = 8
F32 = jnp.float32
BF16 = jnp.bfloat16
NT = ((1,), (1,))
TN = ((0,), (0,))


def dot(lhs, rhs, contract=((1,), (0,))):
    return lax.dot_general(lhs, rhs, (contract, ((), ())), preferred_element_type=F32)


def split_dot(lhs, rhs, contract=((1,), (0,))):
    high = lhs.astype(BF16)
    rest = (lhs - high.astype(F32)).astype(BF16)
    return dot(high, rhs, contract) + dot(rest, rhs, contract)


def shape(dims, dtype):
    return jax.ShapeDtypeStruct(dims, dtype)


def whole(kernel, name, scalars, arrays, outs, scratch=(), flops=0):
    scalars = [jnp.reshape(v, (1,)).astype(jnp.int32) for v in scalars]
    size = sum(v.size * v.dtype.itemsize for v in (*arrays, *outs))
    few, many, made = len(scalars), len(arrays), len(outs)

    def copied(*refs):
        inputs, refs_rest = refs[few : few + many], refs[few + many :]
        outputs, refs_rest = refs_rest[:made], refs_rest[made:]
        held, results = refs_rest[:many], refs_rest[many : many + made]
        *rest, semaphores = refs_rest[many + made :]
        loads = [
            pltpu.make_async_copy(source, target, semaphores.at[i])
            for i, (source, target) in enumerate(zip(inputs, held))
        ]
        stores = [
            pltpu.make_async_copy(source, target, semaphores.at[many + i])
            for i, (source, target) in enumerate(zip(results, outputs))
        ]
        for copy in loads:
            copy.start()
        for copy in loads:
            copy.wait()
        kernel(*refs[:few], *held, *results, *rest)
        for copy in stores:
            copy.start()
        for copy in stores:
            copy.wait()

    return pl.pallas_call(
        copied,
        in_specs=[pl.BlockSpec(memory_space=pltpu.SMEM)] * few
        + [pl.BlockSpec(memory_space=pltpu.HBM)] * many,
        out_specs=[pl.BlockSpec(memory_space=pltpu.HBM)] * made,
        out_shape=list(outs),
        scratch_shapes=[
            *(pltpu.VMEM(v.shape, v.dtype) for v in (*arrays, *outs)),
            *scratch,
            pltpu.SemaphoreType.DMA((many + made,)),
        ],
        compiler_params=pltpu.CompilerParams(vmem_limit_bytes=60 << 20),
        cost_estimate=pl.CostEstimate(flops=flops, bytes_accessed=size, transcendentals=0),
        name=name,
    )(*scalars, *arrays)


def row_matches(places, count):
    rows = lax.broadcasted_iota(jnp.int32, (count, places.shape[1]), 0)
    return (rows == places).astype(F32).astype(BF16)


def column_matches(places, count):
    columns = lax.broadcasted_iota(jnp.int32, (places.shape[0], count), 1)
    return (columns == places).astype(F32).astype(BF16)


def tiles(count, size):
    return [slice(i, i + size) for i in range(0, count, size)]


def prep_kernel(x_ref, place_ref, tok_ref, cot_ref, note_ref, tok_keep, tok_send, cot_keep, cot_send):
    share = tok_keep.shape[0]
    width = tok_ref.shape[1]
    half = width // 2
    order = row_matches(place_ref[...], 2 * share)
    for source, outs in ((tok_ref, (tok_keep, tok_send)), (cot_ref, (cot_keep, cot_send))):
        rows = dot(order, source[...])
        for side in (0, 1):
            part = rows[side * share : (side + 1) * share]
            for x in (0, 1):
                same = x_ref[0] == (x ^ side)
                for zk in range(half // LANES):
                    place = (zk // 2) * 4 + zk % 2
                    zero = part[:, place * LANES : (place + 1) * LANES]
                    one = part[:, (place + 2) * LANES : (place + 3) * LANES]
                    to = slice(x * half + zk * LANES, x * half + (zk + 1) * LANES)
                    outs[side][:, to] = jnp.where(same, zero, one).astype(BF16)
    tok_keep[:, width:] = note_ref[...]
    tok_send[:, width:] = note_ref[...]


def place_rows(x_ref, place_ref, near_ref, far_ref):
    share = near_ref.shape[0] // 2
    width = near_ref.shape[1]
    half = width // 2
    order = column_matches(place_ref[...], 4 * share)
    total = None
    for group in range(4):
        source = (near_ref, far_ref)[group // 2]
        rows = slice((group % 2) * share, (group % 2 + 1) * share)
        blocks = []
        for block in range(width // LANES):
            z, x, k = block // 4, (block // 2) % 2, block % 2
            same = x_ref[0] == (x ^ (group % 2))
            at = (z * 2 + k) * LANES
            first = source[rows, at : at + LANES].astype(F32)
            second = source[rows, half + at : half + at + LANES].astype(F32)
            blocks.append(jnp.where(same, first, second).astype(BF16))
        piece = dot(order[:, group * share : (group + 1) * share], jnp.concatenate(blocks, 1))
        total = piece if total is None else total + piece
    return total


def output_kernel(x_ref, place_ref, near_ref, far_ref, tok_ref, out_ref):
    rows = place_rows(x_ref, place_ref, near_ref, far_ref)
    out_ref[...] = (tok_ref[...].astype(F32) + rows).astype(BF16)


def input_kernel(x_ref, place_ref, near_ref, far_ref, tok_ref, cot_ref, gain_ref, out_ref):
    rows = place_rows(x_ref, place_ref, near_ref, far_ref)
    x = tok_ref[...].astype(F32)
    inverse = lax.rsqrt(jnp.mean(x * x, axis=1, keepdims=True) + EPSILON)
    hat = x * inverse
    half = gain_ref.shape[1] // 2
    gains = []
    for block in range(x.shape[1] // LANES):
        z, side, k = block // 4, (block // 2) % 2, block % 2
        at = (z * 2 + k) * LANES
        gains.append(
            jnp.where(
                x_ref[0] == side,
                gain_ref[0:1, at : at + LANES],
                gain_ref[0:1, half + at : half + at + LANES],
            )
        )
    grad = rows * jnp.concatenate(gains, 1)
    out_ref[...] = cot_ref[...].astype(F32) + inverse * (
        grad - hat * jnp.mean(grad * hat, axis=1, keepdims=True)
    )


def column_sum(rows_ref, pieces):
    own, by_x, by_t, *diagonal = pieces
    depth = own.shape[0]
    near, far = rows_ref[:, :depth], rows_ref[:, depth:]
    a = dot(near, own[...]) + dot(far, by_x[...])
    b = dot(near, by_t[...])
    for i, at in enumerate(tiles(depth, diagonal[0].shape[0])):
        b = b + dot(far[:, at], diagonal[i][...])
    return a, b


def z_block(z_ref, step, size):
    return lax.rem(z_ref[0] + (size - step), size)


def row_sum(z_ref, sides, out_refs):
    depth = sides[0][1][0].shape[0]
    rows = sides[0][0].shape[0] // 2
    block = 2 * LANES
    for base in range(0, 2 * depth, block):
        at = slice(base % depth, base % depth + block)
        value = None
        for lhs, (own, by_x, by_t, *diagonal) in sides:
            part = lhs.shape[1] // 2
            if base < depth:
                near, far = own[at, :], by_t[at, :]
            else:
                size = diagonal[0].shape[0]
                inner = slice(at.start % size, at.start % size + block)
                near, far = by_x[at, :], diagonal[at.start // size][inner, :]
            term = dot(lhs[:, :part], near, NT) + dot(lhs[:, part:], far, NT)
            value = term if value is None else value + term
        place = z_block(z_ref, at.start // block, depth // block) * block
        to = pl.ds(pl.multiple_of(base // depth * depth + place, block), block)
        for i, out in enumerate(out_refs):
            out[:, to] = value[i * rows : (i + 1) * rows].astype(BF16)


def reorder_rows(z_ref, order, source, out):
    block = 2 * LANES
    half = out.shape[1] // 2
    for base in range(0, 2 * half, block):
        step = base % half // block
        place = base // half * half + z_block(z_ref, step, half // block) * block
        at = pl.ds(pl.multiple_of(place, block), block)
        out[:, base : base + block] = dot(order, source[:, at]).astype(BF16)


def grad_pieces(z_ref, channels_t, rows_ref, outs):
    part = channels_t.shape[0] // 2
    depth = rows_ref.shape[1] // 2
    for at in tiles(2 * depth, 2 * LANES):
        value = dot(channels_t, rows_ref[:, at])
        near_out, far_out = (outs[0], outs[2]) if at.start < depth else (outs[1], outs[3])
        block = 2 * z_block(z_ref, (at.start % depth) // (2 * LANES), depth // (2 * LANES))
        for i in (0, 1):
            lanes = value[:, i * LANES : (i + 1) * LANES].astype(BF16)
            for refs, rows in ((near_out, lanes[:part]), (far_out, lanes[part:])):
                size = part // len(refs)
                for j, ref in enumerate(refs):
                    ref[block + i, :, :] = rows[j * size : (j + 1) * size]


def first_pack_kernel(z_ref, k_ref, stream, gate, outer, keep, send):
    count = keep.shape[0] // 3
    part = keep.shape[2]
    for i, source in enumerate((stream, gate, outer)):
        for step in range(count):
            z = lax.rem(z_ref[0] + step, count)
            for out, core in ((keep, k_ref[0]), (send, 1 - k_ref[0])):
                at = pl.ds(pl.multiple_of((z * 2 + core) * part, part), part)
                out[i * count + step] = source[:, at]


def second_pack_kernel(k_ref, kept, got, *outs):
    first = k_ref[0] == 0
    height = kept.shape[1]
    for i, out in enumerate(outs):
        mine, other = kept[i].astype(F32), got[i].astype(F32)
        out[:height, :] = jnp.where(first, mine, other).astype(BF16)
        out[height:, :] = jnp.where(first, other, mine).astype(BF16)


def down(value, count):
    if count == 0:
        return value
    return jnp.concatenate([jnp.zeros((count, value.shape[1]), value.dtype), value[:-count]], 0)


def up(value, count):
    if count == 0:
        return value
    return jnp.concatenate([value[count:], jnp.zeros((count, value.shape[1]), value.dtype)], 0)


def lag_masks(place, taps):
    return [None] + [place >= lag for lag in range(1, taps)]


def masked(value, mask):
    return value if mask is None else jnp.where(mask, value, 0.0)


def filter_sum(stream, masks, weights):
    taps = len(masks)
    total = weights[taps : taps + 1, :] + weights[taps - 1 : taps, :] * stream
    for lag in range(1, taps):
        total = total + weights[taps - 1 - lag : taps - lag, :] * masked(
            down(stream, SUBLANES * lag), masks[lag]
        )
    return total


def places(notes, rows, per_device):
    segments = len(notes) * MB
    zero = lax.broadcasted_iota(jnp.int32, (segments, LANES), 0) % MB
    lane = lax.broadcasted_iota(jnp.int32, (segments, LANES), 1)
    table = jnp.concatenate([v for v in notes for _ in range(MB)], 0)
    begin = jnp.zeros((segments, 1), F32)
    step = lax.broadcasted_iota(jnp.int32, (rows, LANES), 0) // segments
    step = step.astype(F32)
    latest = jnp.zeros((rows, LANES), F32)
    for i in range(per_device - 1):
        picked = jnp.where(lane == zero * per_device + i, table, 0.0)
        begin = begin + jnp.sum(picked, axis=1, keepdims=True)
        every = jnp.concatenate(
            [jnp.broadcast_to(begin, (segments, LANES))] * (rows // segments), 0
        )
        latest = jnp.where(every <= step, every, latest)
    return step - latest


def front_kernel(
    sizes, core_ref, tensor_ref, z_ref, x_ref, place_ref, own, by_x, by_t, low, high, par_ref, sel_ref,
    n_ref, stream_ref, act_ref, mine_ref, other_ref, pos_ref, gain_ref, nrm, act_low,
):
    taps, per_device = sizes
    rows = x_ref.shape[0]
    width = n_ref.shape[1]
    depth = width // 2
    part = own.shape[1]
    members = depth // LANES
    share = rows // (2 * members)
    note = slice(width, width + LANES)
    for side in (0, 1):
        for member in range(members):
            row = member * 2 * share + side * share
            at = side * depth + member * LANES
            gain_ref[0:1, at : at + LANES] = x_ref[row : row + 16, note].astype(F32)[0:1]
    notes = []
    for z in range(members // 2):
        two = [
            x_ref[m * 2 * share : m * 2 * share + 16, note].astype(F32)[1:2]
            for m in (2 * z, 2 * z + 1)
        ]
        notes.append(jnp.where(tensor_ref[0] == 0, two[0], two[1]))
    place = places(notes, rows, per_device)
    pos_ref[...] = place

    def norm(i, _):
        at = pl.ds(pl.multiple_of(i * 64, 64), 64)
        x = x_ref[at, :width].astype(F32)
        inverse = lax.rsqrt(jnp.mean(x * x, axis=1, keepdims=True) + EPSILON)
        nrm[at, :] = (x * inverse * gain_ref[0:1, :]).astype(BF16)
        return 0

    lax.fori_loop(0, rows // 64, norm, 0)
    reorder_rows(z_ref, row_matches(place_ref[...], rows), nrm, n_ref)
    near, far = column_sum(n_ref, (own, by_x, by_t, low, high))
    stream_ref[:, :part] = near
    stream_ref[:, part:] = far
    masks = lag_masks(place, taps)
    for at in tiles(2 * part, LANES):
        filtered = filter_sum(stream_ref[:, at], masks, par_ref[:, at])
        act = filtered * jax.nn.sigmoid(filtered)
        act_ref[:, at] = act
        act_low[:, at] = act.astype(BF16)
    selected = dot(sel_ref[...], act_low[...], NT)
    first = core_ref[0] == 0
    mine_ref[...] = jnp.where(first, selected[:, : rows // 2], selected[:, rows // 2 :])
    other_ref[...] = jnp.where(first, selected[:, rows // 2 :], selected[:, : rows // 2])


def late_kernel(z_ref, cot_ref, place_ref, n_ref, *refs):
    gate_pieces, out_pieces = refs[:4], refs[4:8]
    up_ref, gate_ref, gg_ref = refs[8:]
    part = gate_pieces[0].shape[1]
    reorder_rows(z_ref, row_matches(place_ref[...], cot_ref.shape[0]), cot_ref, up_ref)
    for source, out, pieces in ((n_ref, gate_ref, gate_pieces), (up_ref, gg_ref, out_pieces)):
        near, far = column_sum(source, pieces)
        out[:, :part] = near
        out[:, part:] = far


def out_kernel(z_ref, place_ref, gated_ref, *refs):
    order = column_matches(place_ref[...], gated_ref.shape[0])
    rows = dot(order, gated_ref[...]).astype(BF16)
    row_sum(z_ref, [(rows, refs[:4])], refs[4:])


def late_grad_kernel(z_ref, n_ref, up_ref, gate_grad_ref, gated_ref, *outs):
    for i, (source, rows_ref) in enumerate(((gate_grad_ref, n_ref), (gated_ref, up_ref))):
        grad_pieces(
            z_ref, source[...].astype(F32).T.astype(BF16), rows_ref, [[v] for v in outs[4 * i : 4 * i + 4]]
        )


def back_kernel(
    taps, core_ref, z_ref, total_ref, rest_ref, pos_ref, stream_ref, sact_ref, par_ref, sel_ref, n_ref,
    low_ref, small_ref, *refs,
):
    *outs, act_low, grad_t = refs
    rows, channels = stream_ref.shape
    first = core_ref[0] == 0
    total, rest = total_ref[...], rest_ref[...]
    selected_t = jnp.concatenate(
        [jnp.where(first, total, rest), jnp.where(first, rest, total)], 1
    )
    selected_low = selected_t.astype(BF16)
    count = selected_t.shape[0]
    padded = jnp.concatenate(
        [selected_t, jnp.zeros((-count % LANES, rows), F32)], 0
    )
    selected = padded.T.astype(BF16)
    masks = lag_masks(pos_ref[...], taps)
    spare = jnp.zeros((SUBLANES - taps - 1, LANES), F32)
    for at in tiles(channels, LANES):
        stream = stream_ref[:, at]
        weights = par_ref[:, at]
        filtered = filter_sum(stream, masks, weights)
        slope = jax.nn.sigmoid(filtered)
        act_low[:, at] = (filtered * slope).astype(BF16)
        select = jnp.concatenate(
            [sel_ref[:, at], jnp.zeros((-count % LANES, LANES), BF16)], 0
        )
        act_grad = sact_ref[:, at] + dot(selected, select)
        grad = act_grad * (slope * (1.0 + filtered * (1.0 - slope)))
        stream_grad = weights[taps - 1 : taps, :] * grad
        sums = [jnp.sum(grad * stream, axis=0, keepdims=True)]
        for lag in range(1, taps):
            part_grad = masked(grad, masks[lag])
            sums.append(
                jnp.sum(part_grad * down(stream, SUBLANES * lag), axis=0, keepdims=True)
            )
            stream_grad = stream_grad + weights[taps - 1 - lag : taps - lag, :] * up(
                part_grad, SUBLANES * lag
            )
        sums = sums[::-1] + [jnp.sum(grad, axis=0, keepdims=True), spare]
        small_ref[count:, at] = jnp.concatenate(sums, 0).astype(BF16)
        low_ref[:, at] = stream_grad.astype(BF16)
        grad_t[at, :] = stream_grad.T.astype(BF16)
    small_ref[:count, :] = dot(selected_low, act_low[...]).astype(BF16)
    own_low, own_high, by_x_high, by_t_low, x_way, t_way = outs
    grad_pieces(
        z_ref, grad_t[...], n_ref,
        [
            (own_low, own_high), (x_way.at[1], by_x_high),
            (by_t_low, t_way.at[1]), (x_way.at[0], t_way.at[0]),
        ],
    )


def in_kernel(z_ref, place_ref, low_ref, gate_grad_ref, *refs):
    stream_pieces, gate_pieces, outs, stage = refs[:5], refs[5:9], refs[9:11], refs[11]
    channels = low_ref.shape[1]
    order = column_matches(place_ref[...], low_ref.shape[0])
    stage[:, :channels] = dot(order, low_ref[...]).astype(BF16)
    stage[:, channels:] = dot(order, gate_grad_ref[...]).astype(BF16)
    row_sum(
        z_ref, [(stage[:, :channels], stream_pieces), (stage[:, channels:], gate_pieces)], outs
    )


def small_kernel(
    sizes, z_ref, k_ref, *refs,
):
    count, states, taps = sizes
    blocks = refs[:-7]
    select, step_w, decay, filters, filter_b, step_b, skip = refs[-7:]
    part = blocks[0].shape[1]
    zs = len(blocks) // 2
    rank = step_w.shape[0]
    for i, block in enumerate(blocks):
        core = k_ref[0] if i % 2 == 0 else 1 - k_ref[0]
        place = (z_block(z_ref, i // 2, zs) * 2 + core) * part
        at = pl.ds(pl.multiple_of(place, part), part)
        first = block[: states + 8, :].astype(F32)
        step_b[:, at] = first[0:1]
        skip[:, at] = first[1:2]
        decay[:, at] = first[8:]
        step_w[:, at] = block[states + 8 : states + 8 + rank, :].astype(F32)
        rest = block[states + 8 + rank :, :].astype(F32)
        filters[:, at] = rest[count : count + taps]
        filter_b[:, at] = rest[count + taps : count + taps + 1]
        chosen = jnp.concatenate([rest[:count], jnp.zeros((-count % LANES, part), F32)], 0)
        select[at, :] = chosen.T[:, :count]


def scan_kernel(
    layout, core_ref, pos_ref, act_ref, gate_ref, gg_ref, total_ref, rest_ref, sw_ref, par_ref,
    gated_ref, gateg_ref, sact_ref, small_ref, mine_ref, other_ref,
    bb, cb, hist, fac, ci_acc, co_acc, rate_s, reff_s, u_s, ds_s, y_s, s2_s, slope_s, decb, sel_t, rate_low, rank_t,
):
    rank_width, states, bias_row, decay_row, skip_row = layout
    rows, channels = act_ref.shape
    lanes = LANES
    steps = rows // SUBLANES
    wide = states * lanes
    first = core_ref[0] == 0
    spread = (
        lax.broadcasted_iota(jnp.int32, (states, wide), 1) // lanes
        == lax.broadcasted_iota(jnp.int32, (states, wide), 0)
    ).astype(F32).astype(BF16)
    total, rest = total_ref[...], rest_ref[...]
    sel_t[:, : rows // 2] = jnp.where(first, total, rest)
    sel_t[:, rows // 2 :] = jnp.where(first, rest, total)
    rate_low[...] = sel_t[:rank_width, :].T.astype(BF16)
    bb[...] = split_dot(sel_t[rank_width : rank_width + states, :], spread, TN)
    cb[...] = split_dot(sel_t[rank_width + states :, :], spread, TN)
    hist[0:SUBLANES, :] = jnp.zeros((SUBLANES, SIDE * wide), F32)
    ci_acc[...] = jnp.zeros_like(ci_acc)
    co_acc[...] = jnp.zeros_like(co_acc)
    rank_t[...] = jnp.zeros_like(rank_t)
    zero = jnp.zeros((8, lanes), F32)
    sides = range(SIDE)
    both = SIDE * lanes

    def cols(n):
        return slice(n * lanes, (n + 1) * lanes)

    def wide_cols(n, side):
        return slice((n * SIDE + side) * lanes, (n * SIDE + side + 1) * lanes)

    def side_cols(side):
        return slice(side * lanes, (side + 1) * lanes)

    def one_block(block, _):
        at = pl.ds(pl.multiple_of(block * both, both), both)
        decay = -jnp.exp(par_ref[decay_row : decay_row + states, at])
        for n in range(states):
            decb[8 * n : 8 * n + 8, :] = jnp.broadcast_to(decay[n : n + 1, :], (8, both))
        step_pre = dot(rate_low[...], sw_ref[:, at]) + par_ref[bias_row : bias_row + 1, at]
        rate = jnp.maximum(step_pre, 0.0) + jnp.log1p(jnp.exp(-jnp.abs(step_pre)))
        rate_s[...] = rate
        for side in sides:
            reff_s[:, side_cols(side)] = jnp.where(
                pos_ref[...] > 0.0, rate[:, side_cols(side)] * LOG2E, RESET_RATE
            )
        u_s[...] = rate * act_ref[:, at]
        slope_s[...] = jax.nn.sigmoid(step_pre)
        gate = gate_ref[:, at]
        ds_s[...] = gg_ref[:, at] * (gate * jax.nn.sigmoid(gate))

        for group in range(states // GROUP):
            names = range(group * GROUP, (group + 1) * GROUP)

            def forward(t, h, names=names, group=group):
                row = pl.ds(pl.multiple_of(t * 8, 8), 8)
                next_row = pl.ds(pl.multiple_of(t * 8 + 8, 8), 8)
                reff = [reff_s[row, side_cols(i)] for i in sides]
                u = [u_s[row, side_cols(i)] for i in sides]
                ds = [ds_s[row, side_cols(i)] for i in sides]
                y = [zero if group == 0 else y_s[row, side_cols(i)] for i in sides]
                fresh = []
                for n in names:
                    b, c = bb[row, cols(n)], cb[row, cols(n)]
                    out = co_acc[row, cols(n)]
                    for i in sides:
                        a = jnp.exp2(reff[i] * decb[8 * n : 8 * n + 8, side_cols(i)])
                        hn = a * h[len(fresh)] + b * u[i]
                        hist[next_row, wide_cols(n, i)] = hn
                        fac[row, wide_cols(n, i)] = a
                        y[i] = y[i] + c * hn
                        out = out + ds[i] * hn
                        fresh.append(hn)
                    co_acc[row, cols(n)] = out
                for i in sides:
                    y_s[row, side_cols(i)] = y[i]
                return tuple(fresh)

            lax.fori_loop(0, steps, forward, (zero,) * (GROUP * SIDE))

        act = act_ref[:, at]
        skip = par_ref[skip_row : skip_row + 1, at]
        scanned = y_s[...] + skip * act
        sig = jax.nn.sigmoid(gate)
        gated_ref[:, at] = (scanned * (gate * sig)).astype(BF16)
        gateg_ref[:, at] = (
            gg_ref[:, at] * scanned * (sig * (1.0 + gate * (1.0 - sig)))
        ).astype(BF16)

        sums = []
        for group in range(states // GROUP):
            names = range(group * GROUP, (group + 1) * GROUP)

            def backward(i, carried, names=names, group=group):
                g, dacc = carried
                t = steps - 1 - i
                row = pl.ds(pl.multiple_of(t * 8, 8), 8)
                ds = [ds_s[row, side_cols(k)] for k in sides]
                u = [u_s[row, side_cols(k)] for k in sides]
                rt = [rate_s[row, side_cols(k)] for k in sides]
                s1 = [zero if group == 0 else reff_s[row, side_cols(k)] for k in sides]
                s2 = [zero if group == 0 else s2_s[row, side_cols(k)] for k in sides]
                g_new, d_new = [], []
                for n in names:
                    b, c = bb[row, cols(n)], cb[row, cols(n)]
                    out = ci_acc[row, cols(n)]
                    for k in sides:
                        lam = c * ds[k] + g[len(g_new)]
                        q = lam * fac[row, wide_cols(n, k)]
                        hp = hist[row, wide_cols(n, k)] * q
                        s1[k] = s1[k] + hp * decb[8 * n : 8 * n + 8, side_cols(k)]
                        s2[k] = s2[k] + lam * b
                        out = out + lam * u[k]
                        d_new.append(dacc[len(g_new)] + hp * rt[k])
                        g_new.append(q)
                    ci_acc[row, cols(n)] = out
                for k in sides:
                    s2_s[row, side_cols(k)] = s2[k]
                    reff_s[row, side_cols(k)] = s1[k]
                return tuple(g_new), tuple(d_new)

            none = (zero,) * (GROUP * SIDE)
            _, dacc = lax.fori_loop(0, steps, backward, (none, none))
            for n in range(GROUP):
                row = jnp.concatenate(
                    [jnp.sum(dacc[n * SIDE + k], axis=0, keepdims=True) for k in sides], 1
                )
                name = group * GROUP + n
                sums.append(row * decb[8 * name : 8 * name + 1, :])

        act = act_ref[:, at]
        skip = par_ref[skip_row : skip_row + 1, at]
        s2_all = s2_s[...]
        dscan = ds_s[...]
        sact_ref[:, at] = rate_s[...] * s2_all + skip * dscan
        spre = (reff_s[...] + act * s2_all) * slope_s[...]
        spre_low = spre.astype(BF16)
        head = [jnp.sum(spre, axis=0, keepdims=True), jnp.sum(dscan * act, axis=0, keepdims=True)]
        head.append(jnp.zeros((6, both), F32))
        small_ref[: states + 8, at] = jnp.concatenate(head + sums, 0).astype(BF16)
        small_ref[states + 8 :, at] = dot(
            sel_t[:rank_width, :].astype(BF16), spre_low
        ).astype(BF16)
        rank_t[...] += dot(sw_ref[:, at], spre_low, NT)
        return 0

    lax.fori_loop(0, channels // both, one_block, 0)
    high, low = slice(0, rows // 2), slice(rows // 2, rows)
    for acc, base in ((ci_acc, rank_width), (co_acc, rank_width + states)):
        sel_t[base : base + states, :] = split_dot(acc[...], spread, NT).T
    sel_t[:rank_width, :] = rank_t[...]
    mine_ref[...] = jnp.where(first, sel_t[:, high], sel_t[:, low])
    other_ref[...] = jnp.where(first, sel_t[:, low], sel_t[:, high])


def mixer(layout, core, position, act, gate, gated_grad, total, rest, step_w, params):
    rows, channels = act.shape
    rank_width, states = layout[:2]
    count = total.shape[0]
    wide = states * LANES
    return whole(
        partial(scan_kernel, layout), "mixer", [core],
        (position, act, gate, gated_grad, total, rest, step_w, params),
        [
            shape((rows, channels), BF16), shape((rows, channels), BF16),
            shape((rows, channels), F32), shape((rank_width + states + 8, channels), BF16),
            shape((count, rows // 2), F32), shape((count, rows // 2), F32),
        ],
        [
            pltpu.VMEM((rows, wide), F32), pltpu.VMEM((rows, wide), F32),
            pltpu.VMEM((rows + 8, SIDE * wide), F32), pltpu.VMEM((rows, SIDE * wide), F32),
            pltpu.VMEM((rows, wide), F32), pltpu.VMEM((rows, wide), F32),
        ]
        + [pltpu.VMEM((rows, SIDE * LANES), F32)] * 7
        + [
            pltpu.VMEM((8 * states, SIDE * LANES), F32), pltpu.VMEM((count, rows), F32),
            pltpu.VMEM((rows, rank_width), BF16), pltpu.VMEM((rank_width, rows), F32),
        ],
        flops=20 * rows * channels * states,
    )


def step(*values):
    return lax.optimization_barrier(values)


def swap(value, axis, name="swap"):
    with jax.named_scope(f"{name}_{axis}"):
        return lax.ppermute(value, axis, SWAP)


def exchange_z(value, distance, name):
    size = lax.axis_size("z")
    with jax.named_scope(f"{name}_z"):
        return lax.ppermute(value, "z", [(i, i ^ distance) for i in range(size)])


def from_z(blocks, name):
    size = lax.axis_size("z")
    got = [blocks[0]]
    for shift in range(1, size):
        with jax.named_scope(f"{name}_z"):
            got.append(
                lax.ppermute(blocks[shift], "z", [(i, (i + shift) % size) for i in range(size)])
            )
    return got


def plus(value, *more):
    total = value.astype(F32)
    for v in more:
        total = total + v.astype(F32)
    return total.astype(BF16)


def to_owners(value):
    return lax.all_to_all(value, ZK, 0, 0, tiled=True)


def rank_in_class(keys):
    count = keys.shape[1]
    earlier = jnp.arange(count)[:, None] > jnp.arange(count)[None, :]
    same = (keys[:, :, None] == keys[:, None, :]) & earlier[None]
    return jnp.sum(same.astype(jnp.int32), axis=2)


def body(
    tokens, cotangent, owner_slot, sequence_lengths, norm_gain, inner_weight, filter_weight,
    convolution_bias, select_weight, step_weight, step_bias, decay_log, skip_weight, output_weight,
):
    rings = lax.axis_size("r")
    zs = lax.axis_size("z")
    members = zs * 4
    ri, zi, xi, ki, ti = (lax.axis_index(a) for a in ("r", "z", "x", "k", "t"))
    local_rows, width = tokens.shape
    rank_width = step_weight.shape[0]
    states = decay_log.shape[0]
    taps = filter_weight.shape[0]
    half_channels = inner_weight.shape[2]
    part = half_channels // (2 * zs)
    channels = 2 * part
    block_rows = inner_weight.shape[0]
    ring_rows = rings * block_rows
    depth = width // 2
    batch_rows = local_rows // MB
    group_rows = zs * local_rows
    segments = group_rows // batch_rows
    share = local_rows // 4

    def to_blocks(value):
        if rings == 1:
            return value
        value = value.reshape(-1, rings, members, block_rows)
        return value.transpose(0, 2, 1, 3).reshape(-1, width)

    def from_blocks(value):
        if rings == 1:
            return value
        value = value.reshape(-1, members, rings, block_rows)
        return value.transpose(0, 2, 1, 3).reshape(-1, width)

    inner = inner_weight
    outer = output_weight.T
    gain = norm_gain[None, :]
    if rings > 1:
        inner = lax.all_gather(inner, "r", axis=0, tiled=True)
        outer = lax.all_gather(outer, "r", axis=0, tiled=True)
        gain = lax.all_gather(gain, "r", axis=1, tiled=True)

    blocks_w = 3 * zs
    kept, sent = whole(
        first_pack_kernel, "pack", [zi, ki], (inner[:, 0], inner[:, 1], outer),
        [shape((blocks_w, ring_rows, part), BF16)] * 2,
    )

    slot_rows = owner_slot.reshape(rings, members, local_rows)
    tok, cot = tokens, cotangent
    ring_block = members * local_rows
    if rings > 1:
        per_ring = local_rows // rings
        flat = slot_rows.reshape(rings * members, local_rows)
        target = flat // ring_block
        place = target * per_ring + rank_in_class(target)
        chosen = jnp.arange(local_rows, dtype=jnp.int32)[None, :, None] == place[:, None, :]
        ordered = jnp.sum(jnp.where(chosen, flat[:, None, :], 0), axis=2)
        ordered = ordered.reshape(rings, members, rings, per_ring)
        ordered = lax.dynamic_index_in_dim(ordered, ri, 2, keepdims=False)
        slots = ordered.transpose(1, 0, 2).reshape(members, local_rows)
        own_place = lax.dynamic_index_in_dim(place, ri * members + zi * 4 + xi * 2 + ki, 0, False)
        ring_order = (
            jnp.arange(local_rows, dtype=jnp.int32)[:, None] == own_place[None, :]
        ).astype(BF16)

        def over_rings(value):
            value = value.reshape(rings, per_ring, width)
            return lax.all_to_all(value, "r", 0, 0, tiled=True).reshape(local_rows, width)

        tok, cot = (over_rings(dot(ring_order, v).astype(BF16)) for v in (tokens, cotangent))
    else:
        slots = slot_rows[0]
    local_slot = slots - ri * ring_block
    owner = local_slot // local_rows
    owner_z, owner_x, owner_k = owner // 4, (owner // 2) % 2, owner % 2
    rank = rank_in_class(owner_x * 2 + owner_k)
    in_owner = local_slot % local_rows
    scan_place = (in_owner % batch_rows) * segments + owner_z * MB + in_owner // batch_rows
    here = zi * 4 + xi * 2 + ki
    mine = [lax.dynamic_index_in_dim(v, here, 0, False) for v in (owner_x, owner_k, rank)]
    send_place = (mine[1] ^ ti) * (2 * share) + (mine[0] ^ xi) * share + mine[2]
    in_group = (owner_x == xi) & (owner_k == ti)
    ranked = (
        jnp.arange(share, dtype=jnp.int32)[None, :, None] == rank[:, None, :]
    ) & in_group[:, None, :]
    arrival = jnp.sum(jnp.where(ranked, scan_place[:, None, :], 0), axis=2)
    arrival = arrival.reshape(zs, 2, 2, share)
    arrival = jnp.where(xi == 0, arrival, arrival[:, ::-1]).transpose(0, 2, 1, 3)
    arrived = arrival.reshape(1, group_rows)
    returned = jnp.where(ki == 0, arrival, arrival[:, ::-1]).transpose(1, 0, 2, 3)
    returned = returned.reshape(group_rows, 1)

    blocks = [to_blocks(tok), to_blocks(cot)]
    lengths = sequence_lengths.reshape(1, -1).astype(BF16)
    lengths = jnp.concatenate([lengths, jnp.zeros((1, ring_rows - lengths.shape[1]), BF16)], 1)
    note = jnp.concatenate([gain, lengths, jnp.zeros((share - 2, ring_rows), BF16)], 0)
    noted, plain = shape((share, width + LANES), BF16), shape((share, width), BF16)
    blocks = step(kept, *blocks)[1:]
    rows_out = whole(
        prep_kernel, "prep", [xi], (send_place[None], *blocks, note), [noted, noted, plain, plain]
    )
    first = (zi * 2 + ki) * part

    def own_channels(value):
        return lax.dynamic_slice_in_dim(value, first, part, 1)

    rows_f = taps + 3 + states
    floats = own_channels(
        jnp.concatenate(
            [
                filter_weight, convolution_bias[None], step_bias[None], decay_log,
                skip_weight[None], jnp.zeros((-rows_f % 8, half_channels), F32),
            ],
            axis=0,
        )
    )
    layout = (rank_width, states, taps + 1, taps + 2, taps + 2 + states)
    select_t = lax.dynamic_slice_in_dim(select_weight, first, part, 0).T
    lows = jnp.concatenate([own_channels(step_weight), select_t], 0)
    count = select_t.shape[0]
    half_out = [shape((count, group_rows // 2), F32)] * 2
    half_rows = [shape((group_rows // 2, width), BF16)] * 2
    full = shape((group_rows, channels), F32)
    wide_low = shape((group_rows, width), BF16)
    half = depth // 2

    def gathered(keep, send):
        return lax.all_gather(jnp.concatenate([keep, send], 0), ZK, axis=0, tiled=True)

    tok_keep, tok_send, cot_keep, cot_send = rows_out
    (other_core,) = step(swap(sent, "k", "weights"))
    packed = whole(
        second_pack_kernel, "pack_cores", [ki], (kept, other_core),
        [shape((2 * ring_rows, part), BF16)] * blocks_w,
    )
    tok_got = swap(tok_send, "x", "tokens")
    group_tokens = gathered(tok_keep, tok_got)
    stream_own, floats_t, lows_t, *packed = step(
        jnp.concatenate(from_z(packed[:zs], "stream_w"), 0),
        swap(floats, "t", "params"), swap(lows, "t", "params_low"), *packed[zs:],
    )
    stream_x, stream_t, gate_own, *packed = step(
        swap(stream_own, "x", "stream_w"), swap(stream_own, "t", "stream_w"),
        jnp.concatenate(from_z(packed[:zs], "gate_w"), 0), *packed[zs:],
    )
    params = jnp.concatenate([floats, floats_t], axis=1)
    lows = jnp.concatenate([lows, lows_t], axis=1)
    step_w, select_w = lows[:rank_width], lows[rank_width:]
    stream_low, stream_high, outer_own, cot_got, gate_own, group_tokens = step(
        swap(stream_x[:half], "t", "stream_w_far"), swap(stream_t[half:], "x", "stream_w_far"),
        jnp.concatenate(from_z(packed, "outer_w"), 0), swap(cot_send, "x", "cot"),
        gate_own, group_tokens,
    )
    ws = (stream_own, stream_x, stream_t, stream_low, stream_high)
    group_cot = gathered(cot_keep, cot_got)
    normed, stream, act, sel_mine, sel_other, position, gain_row = whole(
        partial(front_kernel, (taps, sequence_lengths.shape[1])), "front", [ki, ti, zi],
        (group_tokens, arrived, *ws, params, select_w),
        [wide_low, full, full, *half_out, shape((group_rows, LANES), F32), shape((8, width), F32)],
        [pltpu.VMEM((group_rows, width), BF16), pltpu.VMEM((group_rows, channels), BF16)],
        flops=4 * group_rows * width * channels,
    )
    normed, stream, act, sel_mine, sel_other, gate_x, outer_t = step(
        normed, stream, act, sel_mine, sel_other,
        swap(gate_own, "x", "gate_w"), swap(outer_own, "t", "outer_w"),
    )
    sent = (sel_mine + swap(sel_other, "k", "select")).astype(BF16)
    got, gate_t, outer_x, sent = step(
        exchange_z(sent, 1, "select"), swap(gate_own, "t", "gate_w"),
        swap(outer_own, "x", "outer_w"), sent,
    )
    sent = plus(sent, got)
    got, gate_d, outer_d, sent = step(
        exchange_z(sent, 2, "select"), swap(gate_x, "t", "gate_w_far"),
        swap(outer_t, "x", "outer_w_far"), sent,
    )
    total = sent.astype(F32) + got.astype(F32)
    wg, wo = (gate_own, gate_x, gate_t, gate_d), (outer_own, outer_x, outer_t, outer_d)
    upstream, gate, gated_grad = whole(
        late_kernel, "late", [zi], (group_cot, arrived, normed, *wg, *wo), [wide_low, full, full],
        flops=6 * group_rows * width * channels,
    )
    rest = swap(total, "k", "select_rest")
    gated, gate_grad, act_grad, small_a, sel_mine, sel_other = mixer(
        layout, ki, position, act, gate, gated_grad, total, rest, step_w, params
    )

    out_mine, out_other = whole(
        out_kernel, "out_rows", [zi], (returned, gated, *wo), half_rows,
        flops=2 * group_rows * width * channels,
    )
    got, out_mine, out_other, gated, gate_grad = step(
        swap(sel_other, "k", "select"), out_mine, out_other, gated, gate_grad
    )
    sent = (sel_mine + got).astype(BF16)
    pieces = whole(
        late_grad_kernel, "late_grad", [zi], (normed, upstream, gate_grad, gated),
        [shape((2 * zs, part, ring_rows), BF16)] * 8,
        flops=4 * group_rows * width * channels,
    )
    got, out_got, sent, *pieces = step(
        exchange_z(sent, 1, "select"), swap(out_other, "k", "rows"), sent, *pieces
    )
    out_total = plus(out_mine, out_got)
    gate_g, outer_g = pieces[:4], pieces[4:]
    sent = plus(sent, got)
    got, gate_far, outer_far, sent, out_total, *pieces = step(
        exchange_z(sent, 2, "select"), swap(gate_g[3], "x", "gate_g_far"),
        swap(outer_g[3], "t", "outer_g_far"), sent, out_total, *pieces,
    )
    gate_g, outer_g = pieces[:4], pieces[4:]
    out_back = lax.psum_scatter(out_total, "z", scatter_dimension=0, tiled=True)
    total = sent.astype(F32) + got.astype(F32)
    rest = swap(total, "k", "select_rest")
    low, small_b, *stream_g = whole(
        partial(back_kernel, taps), "back", [ki, zi],
        (total, rest, position, stream, act_grad, params, select_w, normed),
        [shape((group_rows, channels), BF16), shape((count + 8, channels), BF16)]
        + [shape((2 * zs, part // 2, ring_rows), BF16)] * 4
        + [shape((2, 2 * zs, part // 2, ring_rows), BF16)] * 2,
        [pltpu.VMEM((group_rows, channels), BF16), pltpu.VMEM((channels, group_rows), BF16)],
        flops=4 * group_rows * width * channels,
    )
    small = jnp.concatenate([small_a, small_b], axis=0)
    gate_first, outer_first, low, small_got, small, *stream_g = step(
        swap(gate_g[1], "x", "gate_g"), swap(outer_g[2], "t", "outer_g"), low,
        swap(small[:, part:], "t", "small"), small, *stream_g,
    )
    small = plus(small[:, :part], small_got)
    in_mine, in_other = whole(
        in_kernel, "in_rows", [zi], (returned, low, gate_grad, *ws, *wg),
        half_rows, [pltpu.VMEM((group_rows, 2 * channels), BF16)],
        flops=4 * group_rows * width * channels,
    )
    in_total = plus(in_mine, swap(in_other, "k", "rows"))
    in_back = lax.psum_scatter(in_total, "z", scatter_dimension=0, tiled=True)
    gate_second, outer_second, small_got, small, _ = step(
        swap(plus(gate_g[2], gate_far), "t", "gate_g_sum"),
        swap(plus(outer_g[1], outer_far), "x", "outer_g_sum"),
        swap(small, "x", "small"), small, in_total,
    )
    small = plus(small, small_got)
    late_sum = jnp.concatenate(
        [plus(gate_g[0], gate_first, gate_second), plus(outer_g[0], outer_first, outer_second)],
        axis=1,
    )
    late_home = to_owners(late_sum)
    own_low, own_high, by_x_high, by_t_low, x_way, t_way = stream_g
    def near_rows(rows):
        return jnp.concatenate([rows[:share], swap(rows[share:], "x", "rows")], 0)

    x_way, t_way, small, out_near = step(
        swap(x_way, "x", "stream_g"), swap(t_way, "t", "stream_g"), small, near_rows(out_back),
    )
    if rings > 1:
        small = lax.psum(small.astype(F32), "r").astype(BF16)
    low_second, high_second, out_far, out_near, in_back, late_home, *gathered_small = step(
        swap(plus(by_t_low, x_way[0]), "t", "stream_g_sum"),
        swap(plus(by_x_high, t_way[0]), "x", "stream_g_sum"),
        swap(out_near, "t", "rows"), out_near, in_back, late_home, *from_z([small] * zs, "small"),
    )
    stream_sum = jnp.concatenate(
        [plus(own_low, x_way[1], low_second), plus(own_high, t_way[1], high_second)], axis=1
    )
    stream_home, in_near = step(to_owners(stream_sum), near_rows(in_back))
    in_far = swap(in_near, "t", "rows")
    small_blocks = [v for block in gathered_small for v in (block, swap(block, "k", "small"))]

    back_place = send_place[:, None]
    if rings > 1:
        def own_rows(near, far, name):
            rows = whole(
                output_kernel, name, [xi], (back_place, near, far, jnp.zeros_like(tokens)),
                [shape(tokens.shape, BF16)],
            )[0]
            return dot(ring_order, from_blocks(over_rings(rows)), TN)

        output = (tokens.astype(F32) + own_rows(out_near, out_far, "output")).astype(BF16)
        rows = own_rows(in_near, in_far, "rows_back")
        own_x = tokens.astype(F32)
        inverse = lax.rsqrt(jnp.mean(own_x * own_x, axis=1, keepdims=True) + EPSILON)
        hat = own_x * inverse
        gain_rel = gain_row[:1].reshape(2, zs, 2, ring_rows)
        gain_abs = jnp.where(xi == 0, gain_rel, gain_rel[::-1]).transpose(1, 0, 2, 3)
        grad = rows * from_blocks(gain_abs.reshape(1, width))
        input_grad = cotangent.astype(F32) + inverse * (
            grad - hat * jnp.mean(grad * hat, axis=1, keepdims=True)
        )
    else:
        output = whole(
            output_kernel, "output", [xi], (back_place, out_near, out_far, tokens),
            [shape(tokens.shape, BF16)],
        )[0]
        input_grad = whole(
            input_kernel, "input_grad", [xi],
            (back_place, in_near, in_far, tokens, cotangent, gain_row),
            [shape(tokens.shape, F32)],
        )[0]
    one_row = shape((1, half_channels), F32)
    select_grad, step_w_grad, decay_grad, filter_grad, filter_b_grad, step_b_grad, skip_grad = whole(
        partial(small_kernel, (count, states, taps)), "small", [zi, ki], small_blocks,
        [
            shape((half_channels, count), F32), shape((rank_width, half_channels), F32),
            shape((states, half_channels), F32), shape((taps, half_channels), F32),
            one_row, one_row, one_row,
        ],
    )
    gate_home, outer_home = late_home[:, :part], late_home[:, part:]
    outer_home = outer_home.reshape(half_channels, ring_rows).astype(F32)
    inner_home = jnp.stack(
        [v.reshape(half_channels, ring_rows).T for v in (stream_home, gate_home)], axis=1
    ).astype(F32)
    if rings > 1:
        outer_home = lax.psum_scatter(outer_home, "r", scatter_dimension=1, tiled=True)
        inner_home = lax.psum_scatter(inner_home, "r", scatter_dimension=0, tiled=True)
    gain_grad = jnp.sum(inner_home * inner_weight.astype(F32), axis=(1, 2))
    gain_grad = (gain_grad + swap(gain_grad, "t", "gain")) / norm_gain.astype(F32)
    return (
        output,
        input_grad,
        gain_grad,
        inner_home,
        filter_grad,
        filter_b_grad[0],
        select_grad,
        step_w_grad,
        step_b_grad[0],
        decay_grad,
        skip_grad[0],
        outer_home,
    )


def solution(mesh):
    devices = mesh.devices
    split = Mesh(
        devices.reshape(devices.shape[0] // 16, 4, 2, 2, devices.shape[1]), DP + ("t",)
    )
    in_specs = (
        P(DP, None), P(DP, None), P(), P(DP, None), P(DP), P(DP, None, "t"), P(None, "t"), P("t"),
        P("t", None), P(None, "t"), P("t"), P(None, "t"), P("t"), P("t", DP),
    )
    out_specs = (
        P(DP, None), P(DP, None), P(DP), P(DP, None, "t"), P(None, "t"), P("t"), P("t", None),
        P(None, "t"), P("t"), P(None, "t"), P("t"), P("t", DP),
    )
    return jax.shard_map(body, mesh=split, in_specs=in_specs, out_specs=out_specs, check_vma=False)
```

```python
from functools import partial

import jax
import jax.numpy as jnp
from jax import lax
from jax.experimental import pallas as pl
from jax.experimental.pallas import tpu as pltpu
from jax.sharding import Mesh, PartitionSpec as P

MB = 2
EPSILON = 1e-05
ZK = ("z", "k")
DP = ("r", "z", "x", "k")
SWAP = [(0, 1), (1, 0)]
LOG2E = 1.4426950408889634
RESET_RATE = 1e30
LANES = 128
MICROSECONDS = {
    "pack": 3, "pack_cores": 3, "prep": 2, "front": 8, "late": 8, "mixer": 24, "out_rows": 5,
    "late_grad": 6, "back": 7, "in_rows": 7, "output": 3, "input_grad": 4, "small": 3,
    "rows_back": 3,
}
SUBLANES = 8
SIDE = 2
GROUP = 8
CHUNK = 64
UNROLL = 2
F32 = jnp.float32
BF16 = jnp.bfloat16
NT = ((1,), (1,))
TN = ((0,), (0,))


def dot(lhs, rhs, contract=((1,), (0,))):
    return lax.dot_general(lhs, rhs, (contract, ((), ())), preferred_element_type=F32)


def split_dot(lhs, rhs, contract=((1,), (0,))):
    high = lhs.astype(BF16)
    rest = (lhs - high.astype(F32)).astype(BF16)
    return dot(high, rhs, contract) + dot(rest, rhs, contract)


def shape(dims, dtype):
    return jax.ShapeDtypeStruct(dims, dtype)


def whole(kernel, name, scalars, arrays, outs, scratch=()):
    scalars = [jnp.reshape(v, (1,)).astype(jnp.int32) for v in scalars]
    few, many, made = len(scalars), len(arrays), len(outs)

    def copied(*refs):
        inputs, refs_rest = refs[few : few + many], refs[few + many :]
        outputs, refs_rest = refs_rest[:made], refs_rest[made:]
        held, results = refs_rest[:many], refs_rest[many : many + made]
        *rest, semaphores = refs_rest[many + made :]
        loads = [
            pltpu.make_async_copy(source, target, semaphores.at[i])
            for i, (source, target) in enumerate(zip(inputs, held))
        ]
        stores = [
            pltpu.make_async_copy(source, target, semaphores.at[many + i])
            for i, (source, target) in enumerate(zip(results, outputs))
        ]
        for copy in loads:
            copy.start()
        for copy in loads:
            copy.wait()
        kernel(*refs[:few], *held, *results, *rest)
        for copy in stores:
            copy.start()
        for copy in stores:
            copy.wait()

    return pl.pallas_call(
        copied,
        in_specs=[pl.BlockSpec(memory_space=pltpu.SMEM)] * few
        + [pl.BlockSpec(memory_space=pltpu.HBM)] * many,
        out_specs=[pl.BlockSpec(memory_space=pltpu.HBM)] * made,
        out_shape=list(outs),
        scratch_shapes=[
            *(pltpu.VMEM(v.shape, v.dtype) for v in (*arrays, *outs)),
            *scratch,
            pltpu.SemaphoreType.DMA((many + made,)),
        ],
        compiler_params=pltpu.CompilerParams(vmem_limit_bytes=60 << 20),
        cost_estimate=pl.CostEstimate(
            flops=0, bytes_accessed=MICROSECONDS[name] * 3690000, transcendentals=0
        ),
        name=name,
    )(*scalars, *arrays)


def row_matches(places, count):
    rows = lax.broadcasted_iota(jnp.int32, (count, places.shape[1]), 0)
    return (rows == places).astype(F32).astype(BF16)


def column_matches(places, count):
    columns = lax.broadcasted_iota(jnp.int32, (places.shape[0], count), 1)
    return (columns == places).astype(F32).astype(BF16)


def tiles(count, size):
    return [slice(i, i + size) for i in range(0, count, size)]


def prep_kernel(x_ref, place_ref, tok_ref, cot_ref, note_ref, tok_keep, tok_send, cot_keep, cot_send):
    share = tok_keep.shape[0]
    width = tok_ref.shape[1]
    half = width // 2
    order = row_matches(place_ref[...], 2 * share)
    for source, outs in ((tok_ref, (tok_keep, tok_send)), (cot_ref, (cot_keep, cot_send))):
        rows = dot(order, source[...])
        for side in (0, 1):
            part = rows[side * share : (side + 1) * share]
            for x in (0, 1):
                same = x_ref[0] == (x ^ side)
                for zk in range(half // LANES):
                    place = (zk // 2) * 4 + zk % 2
                    zero = part[:, place * LANES : (place + 1) * LANES]
                    one = part[:, (place + 2) * LANES : (place + 3) * LANES]
                    to = slice(x * half + zk * LANES, x * half + (zk + 1) * LANES)
                    outs[side][:, to] = jnp.where(same, zero, one).astype(BF16)
    tok_keep[:, width:] = note_ref[...]
    tok_send[:, width:] = note_ref[...]


def place_rows(x_ref, place_ref, near_ref, far_ref):
    share = near_ref.shape[0] // 2
    width = near_ref.shape[1]
    half = width // 2
    order = column_matches(place_ref[...], 4 * share)
    total = None
    for group in range(4):
        source = (near_ref, far_ref)[group // 2]
        rows = slice((group % 2) * share, (group % 2 + 1) * share)
        blocks = []
        for block in range(width // LANES):
            z, x, k = block // 4, (block // 2) % 2, block % 2
            same = x_ref[0] == (x ^ (group % 2))
            at = (z * 2 + k) * LANES
            first = source[rows, at : at + LANES].astype(F32)
            second = source[rows, half + at : half + at + LANES].astype(F32)
            blocks.append(jnp.where(same, first, second).astype(BF16))
        piece = dot(order[:, group * share : (group + 1) * share], jnp.concatenate(blocks, 1))
        total = piece if total is None else total + piece
    return total


def output_kernel(x_ref, place_ref, near_ref, far_ref, tok_ref, out_ref):
    rows = place_rows(x_ref, place_ref, near_ref, far_ref)
    out_ref[...] = (tok_ref[...].astype(F32) + rows).astype(BF16)


def input_kernel(x_ref, place_ref, near_ref, far_ref, tok_ref, cot_ref, gain_ref, out_ref):
    rows = place_rows(x_ref, place_ref, near_ref, far_ref)
    x = tok_ref[...].astype(F32)
    inverse = lax.rsqrt(jnp.mean(x * x, axis=1, keepdims=True) + EPSILON)
    hat = x * inverse
    half = gain_ref.shape[1] // 2
    gains = []
    for block in range(x.shape[1] // LANES):
        z, side, k = block // 4, (block // 2) % 2, block % 2
        at = (z * 2 + k) * LANES
        gains.append(
            jnp.where(
                x_ref[0] == side,
                gain_ref[0:1, at : at + LANES],
                gain_ref[0:1, half + at : half + at + LANES],
            )
        )
    grad = rows * jnp.concatenate(gains, 1)
    out_ref[...] = cot_ref[...].astype(F32) + inverse * (
        grad - hat * jnp.mean(grad * hat, axis=1, keepdims=True)
    )


def column_sum(rows_ref, pieces):
    own, by_x, by_t, *diagonal = pieces
    depth = own.shape[0]
    near, far = rows_ref[:, :depth], rows_ref[:, depth:]
    a = dot(near, own[...]) + dot(far, by_x[...])
    b = dot(near, by_t[...])
    for i, at in enumerate(tiles(depth, diagonal[0].shape[0])):
        b = b + dot(far[:, at], diagonal[i][...])
    return a, b


def z_block(z_ref, step, size):
    return lax.rem(z_ref[0] + (size - step), size)


def row_sum(z_ref, sides, out_refs):
    depth = sides[0][1][0].shape[0]
    rows = sides[0][0].shape[0] // 2
    block = 2 * LANES
    for base in range(0, 2 * depth, block):
        at = slice(base % depth, base % depth + block)
        value = None
        for lhs, (own, by_x, by_t, *diagonal) in sides:
            part = lhs.shape[1] // 2
            if base < depth:
                near, far = own[at, :], by_t[at, :]
            else:
                size = diagonal[0].shape[0]
                inner = slice(at.start % size, at.start % size + block)
                near, far = by_x[at, :], diagonal[at.start // size][inner, :]
            term = dot(lhs[:, :part], near, NT) + dot(lhs[:, part:], far, NT)
            value = term if value is None else value + term
        place = z_block(z_ref, at.start // block, depth // block) * block
        to = pl.ds(pl.multiple_of(base // depth * depth + place, block), block)
        for i, out in enumerate(out_refs):
            out[:, to] = value[i * rows : (i + 1) * rows].astype(BF16)


def reorder_rows(z_ref, order, source, out):
    block = 2 * LANES
    half = out.shape[1] // 2
    for base in range(0, 2 * half, block):
        step = base % half // block
        place = base // half * half + z_block(z_ref, step, half // block) * block
        at = pl.ds(pl.multiple_of(place, block), block)
        out[:, base : base + block] = dot(order, source[:, at]).astype(BF16)


def grad_pieces(z_ref, channels_t, rows_ref, outs):
    part = channels_t.shape[0] // 2
    depth = rows_ref.shape[1] // 2
    for at in tiles(2 * depth, 2 * LANES):
        value = dot(channels_t, rows_ref[:, at])
        near_out, far_out = (outs[0], outs[2]) if at.start < depth else (outs[1], outs[3])
        block = 2 * z_block(z_ref, (at.start % depth) // (2 * LANES), depth // (2 * LANES))
        for i in (0, 1):
            lanes = value[:, i * LANES : (i + 1) * LANES].astype(BF16)
            for refs, rows in ((near_out, lanes[:part]), (far_out, lanes[part:])):
                size = part // len(refs)
                for j, ref in enumerate(refs):
                    ref[block + i, :, :] = rows[j * size : (j + 1) * size]


def first_pack_kernel(z_ref, k_ref, stream, gate, outer, keep, send):
    count = keep.shape[0] // 3
    part = keep.shape[2]
    for i, source in enumerate((stream, gate, outer)):
        for step in range(count):
            z = lax.rem(z_ref[0] + step, count)
            for out, core in ((keep, k_ref[0]), (send, 1 - k_ref[0])):
                at = pl.ds(pl.multiple_of((z * 2 + core) * part, part), part)
                out[i * count + step] = source[:, at]


def second_pack_kernel(k_ref, kept, got, *outs):
    first = k_ref[0] == 0
    height = kept.shape[1]
    for i, out in enumerate(outs):
        mine, other = kept[i].astype(F32), got[i].astype(F32)
        out[:height, :] = jnp.where(first, mine, other).astype(BF16)
        out[height:, :] = jnp.where(first, other, mine).astype(BF16)


def down(value, count):
    if count == 0:
        return value
    return jnp.concatenate([jnp.zeros((count, value.shape[1]), value.dtype), value[:-count]], 0)


def up(value, count):
    if count == 0:
        return value
    return jnp.concatenate([value[count:], jnp.zeros((count, value.shape[1]), value.dtype)], 0)


def lag_masks(place, taps):
    return [None] + [place >= lag for lag in range(1, taps)]


def masked(value, mask):
    return value if mask is None else jnp.where(mask, value, 0.0)


def filter_sum(stream, masks, weights):
    taps = len(masks)
    total = weights[taps : taps + 1, :] + weights[taps - 1 : taps, :] * stream
    for lag in range(1, taps):
        total = total + weights[taps - 1 - lag : taps - lag, :] * masked(
            down(stream, SUBLANES * lag), masks[lag]
        )
    return total


def places(notes, rows, per_device):
    segments = len(notes) * MB
    zero = lax.broadcasted_iota(jnp.int32, (segments, LANES), 0) % MB
    lane = lax.broadcasted_iota(jnp.int32, (segments, LANES), 1)
    table = jnp.concatenate([v for v in notes for _ in range(MB)], 0)
    begin = jnp.zeros((segments, 1), F32)
    step = lax.broadcasted_iota(jnp.int32, (rows, LANES), 0) // segments
    step = step.astype(F32)
    latest = jnp.zeros((rows, LANES), F32)
    for i in range(per_device - 1):
        picked = jnp.where(lane == zero * per_device + i, table, 0.0)
        begin = begin + jnp.sum(picked, axis=1, keepdims=True)
        every = jnp.concatenate(
            [jnp.broadcast_to(begin, (segments, LANES))] * (rows // segments), 0
        )
        latest = jnp.where(every <= step, every, latest)
    return step - latest


def front_kernel(
    sizes, core_ref, tensor_ref, z_ref, x_ref, place_ref, own, by_x, by_t, low, high, par_ref, sel_ref,
    n_ref, stream_ref, act_ref, mine_ref, other_ref, pos_ref, gain_ref, nrm, act_low,
):
    taps, per_device = sizes
    rows = x_ref.shape[0]
    width = n_ref.shape[1]
    depth = width // 2
    part = own.shape[1]
    members = depth // LANES
    share = rows // (2 * members)
    note = slice(width, width + LANES)
    for side in (0, 1):
        for member in range(members):
            row = member * 2 * share + side * share
            at = side * depth + member * LANES
            gain_ref[0:1, at : at + LANES] = x_ref[row : row + 16, note].astype(F32)[0:1]
    notes = []
    for z in range(members // 2):
        two = [
            x_ref[m * 2 * share : m * 2 * share + 16, note].astype(F32)[1:2]
            for m in (2 * z, 2 * z + 1)
        ]
        notes.append(jnp.where(tensor_ref[0] == 0, two[0], two[1]))
    place = places(notes, rows, per_device)
    pos_ref[...] = place

    def norm(i, _):
        at = pl.ds(pl.multiple_of(i * 64, 64), 64)
        x = x_ref[at, :width].astype(F32)
        inverse = lax.rsqrt(jnp.mean(x * x, axis=1, keepdims=True) + EPSILON)
        nrm[at, :] = (x * inverse * gain_ref[0:1, :]).astype(BF16)
        return 0

    lax.fori_loop(0, rows // 64, norm, 0)
    reorder_rows(z_ref, row_matches(place_ref[...], rows), nrm, n_ref)
    near, far = column_sum(n_ref, (own, by_x, by_t, low, high))
    stream_ref[:, :part] = near
    stream_ref[:, part:] = far
    masks = lag_masks(place, taps)
    for at in tiles(2 * part, LANES):
        filtered = filter_sum(stream_ref[:, at], masks, par_ref[:, at])
        act = filtered * jax.nn.sigmoid(filtered)
        act_ref[:, at] = act
        act_low[:, at] = act.astype(BF16)
    selected = dot(sel_ref[...], act_low[...], NT)
    first = core_ref[0] == 0
    mine_ref[...] = jnp.where(first, selected[:, : rows // 2], selected[:, rows // 2 :])
    other_ref[...] = jnp.where(first, selected[:, rows // 2 :], selected[:, : rows // 2])


def late_kernel(z_ref, cot_ref, place_ref, n_ref, *refs):
    gate_pieces, out_pieces = refs[:4], refs[4:8]
    up_ref, gate_ref, gg_ref = refs[8:]
    part = gate_pieces[0].shape[1]
    reorder_rows(z_ref, row_matches(place_ref[...], cot_ref.shape[0]), cot_ref, up_ref)
    for source, out, pieces in ((n_ref, gate_ref, gate_pieces), (up_ref, gg_ref, out_pieces)):
        near, far = column_sum(source, pieces)
        out[:, :part] = near
        out[:, part:] = far


def out_kernel(z_ref, place_ref, gated_ref, *refs):
    order = column_matches(place_ref[...], gated_ref.shape[0])
    rows = dot(order, gated_ref[...]).astype(BF16)
    row_sum(z_ref, [(rows, refs[:4])], refs[4:])


def late_grad_kernel(z_ref, n_ref, up_ref, gate_grad_ref, gated_ref, *outs):
    for i, (source, rows_ref) in enumerate(((gate_grad_ref, n_ref), (gated_ref, up_ref))):
        grad_pieces(
            z_ref, source[...].astype(F32).T.astype(BF16), rows_ref, [[v] for v in outs[4 * i : 4 * i + 4]]
        )


def back_kernel(
    taps, core_ref, z_ref, total_ref, rest_ref, pos_ref, stream_ref, sact_ref, par_ref, sel_ref, n_ref,
    low_ref, small_ref, *refs,
):
    *outs, act_low, grad_t = refs
    rows, channels = stream_ref.shape
    first = core_ref[0] == 0
    total, rest = total_ref[...], rest_ref[...]
    selected_t = jnp.concatenate(
        [jnp.where(first, total, rest), jnp.where(first, rest, total)], 1
    )
    selected_low = selected_t.astype(BF16)
    count = selected_t.shape[0]
    padded = jnp.concatenate(
        [selected_t, jnp.zeros((-count % LANES, rows), F32)], 0
    )
    selected = padded.T.astype(BF16)
    masks = lag_masks(pos_ref[...], taps)
    spare = jnp.zeros((SUBLANES - taps - 1, LANES), F32)
    for at in tiles(channels, LANES):
        stream = stream_ref[:, at]
        weights = par_ref[:, at]
        filtered = filter_sum(stream, masks, weights)
        slope = jax.nn.sigmoid(filtered)
        act_low[:, at] = (filtered * slope).astype(BF16)
        select = jnp.concatenate(
            [sel_ref[:, at], jnp.zeros((-count % LANES, LANES), BF16)], 0
        )
        act_grad = sact_ref[:, at] + dot(selected, select)
        grad = act_grad * (slope * (1.0 + filtered * (1.0 - slope)))
        stream_grad = weights[taps - 1 : taps, :] * grad
        sums = [jnp.sum(grad * stream, axis=0, keepdims=True)]
        for lag in range(1, taps):
            part_grad = masked(grad, masks[lag])
            sums.append(
                jnp.sum(part_grad * down(stream, SUBLANES * lag), axis=0, keepdims=True)
            )
            stream_grad = stream_grad + weights[taps - 1 - lag : taps - lag, :] * up(
                part_grad, SUBLANES * lag
            )
        sums = sums[::-1] + [jnp.sum(grad, axis=0, keepdims=True), spare]
        small_ref[count:, at] = jnp.concatenate(sums, 0).astype(BF16)
        low_ref[:, at] = stream_grad.astype(BF16)
        grad_t[at, :] = stream_grad.T.astype(BF16)
    small_ref[:count, :] = dot(selected_low, act_low[...]).astype(BF16)
    own_low, own_high, by_x_high, by_t_low, x_way, t_way = outs
    grad_pieces(
        z_ref, grad_t[...], n_ref,
        [
            (own_low, own_high), (x_way.at[1], by_x_high),
            (by_t_low, t_way.at[1]), (x_way.at[0], t_way.at[0]),
        ],
    )


def in_kernel(z_ref, place_ref, low_ref, gate_grad_ref, *refs):
    stream_pieces, gate_pieces, outs, stage = refs[:5], refs[5:9], refs[9:11], refs[11]
    channels = low_ref.shape[1]
    order = column_matches(place_ref[...], low_ref.shape[0])
    stage[:, :channels] = dot(order, low_ref[...]).astype(BF16)
    stage[:, channels:] = dot(order, gate_grad_ref[...]).astype(BF16)
    row_sum(
        z_ref, [(stage[:, :channels], stream_pieces), (stage[:, channels:], gate_pieces)], outs
    )


def small_kernel(
    sizes, z_ref, k_ref, *refs,
):
    count, states, taps = sizes
    blocks = refs[:-7]
    select, step_w, decay, filters, filter_b, step_b, skip = refs[-7:]
    part = blocks[0].shape[1]
    zs = len(blocks) // 2
    rank = step_w.shape[0]
    for i, block in enumerate(blocks):
        core = k_ref[0] if i % 2 == 0 else 1 - k_ref[0]
        place = (z_block(z_ref, i // 2, zs) * 2 + core) * part
        at = pl.ds(pl.multiple_of(place, part), part)
        first = block[: states + 8, :].astype(F32)
        step_b[:, at] = first[0:1]
        skip[:, at] = first[1:2]
        decay[:, at] = first[8:]
        step_w[:, at] = block[states + 8 : states + 8 + rank, :].astype(F32)
        rest = block[states + 8 + rank :, :].astype(F32)
        filters[:, at] = rest[count : count + taps]
        filter_b[:, at] = rest[count + taps : count + taps + 1]
        select[:, at] = rest[:count]


def scan_kernel(
    layout, core_ref, pos_ref, act_ref, gate_ref, gg_ref, total_ref, rest_ref, sw_ref, par_ref,
    gated_ref, gateg_ref, sact_ref, small_ref, mine_ref, other_ref,
    bb, cb, hist, fac, ci_acc, co_acc, rate_s, reff_s, u_s, ds_s, y_s, s2_s, slope_s, spre_low, decb, sel_t, rate_low, rank_t,
):
    rank_width, states, bias_row, decay_row, skip_row = layout
    rows, channels = act_ref.shape
    lanes = LANES
    steps = rows // SUBLANES
    wide = states * lanes
    first = core_ref[0] == 0
    spread = (
        lax.broadcasted_iota(jnp.int32, (states, wide), 1) // lanes
        == lax.broadcasted_iota(jnp.int32, (states, wide), 0)
    ).astype(F32).astype(BF16)
    total, rest = total_ref[...], rest_ref[...]
    sel_t[:, : rows // 2] = jnp.where(first, total, rest)
    sel_t[:, rows // 2 :] = jnp.where(first, rest, total)
    rate_low[...] = sel_t[:rank_width, :].T.astype(BF16)
    twice = jnp.concatenate([spread, spread], 0)
    for out, base in ((bb, rank_width), (cb, rank_width + states)):
        value = sel_t[base : base + states, :]
        high = value.astype(BF16).astype(F32)
        parts = jnp.concatenate([high, value - high], 0).astype(BF16)
        out[...] = dot(parts, twice, TN)
    hist[0:SUBLANES, :] = jnp.zeros((SUBLANES, SIDE * wide), F32)
    ci_acc[...] = jnp.zeros_like(ci_acc)
    co_acc[...] = jnp.zeros_like(co_acc)
    rank_t[...] = jnp.zeros_like(rank_t)
    zero = jnp.zeros((8, lanes), F32)
    sides = range(SIDE)
    both = SIDE * lanes

    def cols(n):
        return slice(n * lanes, (n + 1) * lanes)

    def wide_cols(n, side):
        return slice((n * SIDE + side) * lanes, (n * SIDE + side + 1) * lanes)

    def side_cols(side):
        return slice(side * lanes, (side + 1) * lanes)

    def one_block(block, _):
        at = pl.ds(pl.multiple_of(block * both, both), both)
        decay = -jnp.exp(par_ref[decay_row : decay_row + states, at])
        for n in range(states):
            decb[8 * n : 8 * n + 8, :] = jnp.broadcast_to(decay[n : n + 1, :], (8, both))
        rate_s[...] = dot(rate_low[...], sw_ref[:, at]) + par_ref[bias_row : bias_row + 1, at]

        def before(i, _):
            row = pl.ds(pl.multiple_of(i * CHUNK, CHUNK), CHUNK)
            step_pre = rate_s[row, :]
            small = jnp.exp(-jnp.abs(step_pre))
            rate = jnp.maximum(step_pre, 0.0) + jnp.log1p(small)
            inverse = 1.0 / (1.0 + small)
            slope_s[row, :] = jnp.where(step_pre >= 0.0, inverse, small * inverse)
            rate_s[row, :] = rate
            keep = pos_ref[row, :] > 0.0
            for side in sides:
                reff_s[row, side_cols(side)] = jnp.where(
                    keep, rate[:, side_cols(side)] * LOG2E, RESET_RATE
                )
            u_s[row, :] = rate * act_ref[row, at]
            gate = gate_ref[row, at]
            ds_s[row, :] = gg_ref[row, at] * (gate * jax.nn.sigmoid(gate))
            return 0

        lax.fori_loop(0, rows // CHUNK, before, 0)

        for group in range(states // GROUP):
            names = range(group * GROUP, (group + 1) * GROUP)

            def forward(t, h, names=names, group=group):
                row = pl.ds(pl.multiple_of(t * 8, 8), 8)
                next_row = pl.ds(pl.multiple_of(t * 8 + 8, 8), 8)
                reff = [reff_s[row, side_cols(i)] for i in sides]
                u = [u_s[row, side_cols(i)] for i in sides]
                ds = [ds_s[row, side_cols(i)] for i in sides]
                y = [zero if group == 0 else y_s[row, side_cols(i)] for i in sides]
                fresh = []
                for n in names:
                    b, c = bb[row, cols(n)], cb[row, cols(n)]
                    out = co_acc[row, cols(n)]
                    for i in sides:
                        a = jnp.exp2(reff[i] * decb[8 * n : 8 * n + 8, side_cols(i)])
                        hn = a * h[len(fresh)] + b * u[i]
                        hist[next_row, wide_cols(n, i)] = hn
                        fac[row, wide_cols(n, i)] = a
                        y[i] = y[i] + c * hn
                        out = out + ds[i] * hn
                        fresh.append(hn)
                    co_acc[row, cols(n)] = out
                for i in sides:
                    y_s[row, side_cols(i)] = y[i]
                return tuple(fresh)

            lax.fori_loop(0, steps, forward, (zero,) * (GROUP * SIDE), unroll=UNROLL)

        skip = par_ref[skip_row : skip_row + 1, at]

        def between(i, _):
            row = pl.ds(pl.multiple_of(i * CHUNK, CHUNK), CHUNK)
            scanned = y_s[row, :] + skip * act_ref[row, at]
            gate = gate_ref[row, at]
            sig = jax.nn.sigmoid(gate)
            gated_ref[row, at] = (scanned * (gate * sig)).astype(BF16)
            gateg_ref[row, at] = (
                gg_ref[row, at] * scanned * (sig * (1.0 + gate * (1.0 - sig)))
            ).astype(BF16)
            return 0

        lax.fori_loop(0, rows // CHUNK, between, 0)

        sums = []
        for group in range(states // GROUP):
            names = range(group * GROUP, (group + 1) * GROUP)

            def backward(i, carried, names=names, group=group):
                g, dacc = carried
                t = steps - 1 - i
                row = pl.ds(pl.multiple_of(t * 8, 8), 8)
                ds = [ds_s[row, side_cols(k)] for k in sides]
                u = [u_s[row, side_cols(k)] for k in sides]
                rt = [rate_s[row, side_cols(k)] for k in sides]
                s1 = [zero if group == 0 else reff_s[row, side_cols(k)] for k in sides]
                s2 = [zero if group == 0 else s2_s[row, side_cols(k)] for k in sides]
                g_new, d_new = [], []
                for n in names:
                    b, c = bb[row, cols(n)], cb[row, cols(n)]
                    out = ci_acc[row, cols(n)]
                    for k in sides:
                        lam = c * ds[k] + g[len(g_new)]
                        q = lam * fac[row, wide_cols(n, k)]
                        hp = hist[row, wide_cols(n, k)] * q
                        s1[k] = s1[k] + hp * decb[8 * n : 8 * n + 8, side_cols(k)]
                        s2[k] = s2[k] + lam * b
                        out = out + lam * u[k]
                        d_new.append(dacc[len(g_new)] + hp * rt[k])
                        g_new.append(q)
                    ci_acc[row, cols(n)] = out
                for k in sides:
                    s2_s[row, side_cols(k)] = s2[k]
                    reff_s[row, side_cols(k)] = s1[k]
                return tuple(g_new), tuple(d_new)

            none = (zero,) * (GROUP * SIDE)
            _, dacc = lax.fori_loop(0, steps, backward, (none, none), unroll=UNROLL)
            for n in range(GROUP):
                row = jnp.concatenate(
                    [jnp.sum(dacc[n * SIDE + k], axis=0, keepdims=True) for k in sides], 1
                )
                name = group * GROUP + n
                sums.append(row * decb[8 * name : 8 * name + 1, :])

        def behind(i, carried):
            row = pl.ds(pl.multiple_of(i * CHUNK, CHUNK), CHUNK)
            act, dscan, s2_all = act_ref[row, at], ds_s[row, :], s2_s[row, :]
            sact_ref[row, at] = rate_s[row, :] * s2_all + skip * dscan
            spre = (reff_s[row, :] + act * s2_all) * slope_s[row, :]
            spre_low[row, :] = spre.astype(BF16)
            totals = []
            for total, value in zip(carried, (spre, dscan * act)):
                for j in range(CHUNK // SUBLANES):
                    total = total + value[j * SUBLANES : (j + 1) * SUBLANES]
                totals.append(total)
            return tuple(totals)

        empty = jnp.zeros((SUBLANES, both), F32)
        head = [
            jnp.sum(v, axis=0, keepdims=True)
            for v in lax.fori_loop(0, rows // CHUNK, behind, (empty, empty))
        ]
        head.append(jnp.zeros((6, both), F32))
        small_ref[: states + 8, at] = jnp.concatenate(head + sums, 0).astype(BF16)
        small_ref[states + 8 :, at] = dot(
            sel_t[:rank_width, :].astype(BF16), spre_low[...]
        ).astype(BF16)
        rank_t[...] += dot(sw_ref[:, at], spre_low[...], NT)
        return 0

    lax.fori_loop(0, channels // both, one_block, 0)
    high, low = slice(0, rows // 2), slice(rows // 2, rows)
    for acc, base in ((ci_acc, rank_width), (co_acc, rank_width + states)):
        sel_t[base : base + states, :] = dot(acc[...].astype(BF16), spread, NT).T
    sel_t[:rank_width, :] = rank_t[...]
    mine_ref[...] = jnp.where(first, sel_t[:, high], sel_t[:, low])
    other_ref[...] = jnp.where(first, sel_t[:, low], sel_t[:, high])


def mixer(layout, core, position, act, gate, gated_grad, total, rest, step_w, params):
    rows, channels = act.shape
    rank_width, states = layout[:2]
    count = total.shape[0]
    wide = states * LANES
    return whole(
        partial(scan_kernel, layout), "mixer", [core],
        (position, act, gate, gated_grad, total, rest, step_w, params),
        [
            shape((rows, channels), BF16), shape((rows, channels), BF16),
            shape((rows, channels), F32), shape((rank_width + states + 8, channels), BF16),
            shape((count, rows // 2), F32), shape((count, rows // 2), F32),
        ],
        [
            pltpu.VMEM((rows, wide), F32), pltpu.VMEM((rows, wide), F32),
            pltpu.VMEM((rows + 8, SIDE * wide), F32), pltpu.VMEM((rows, SIDE * wide), F32),
            pltpu.VMEM((rows, wide), F32), pltpu.VMEM((rows, wide), F32),
        ]
        + [pltpu.VMEM((rows, SIDE * LANES), F32)] * 7
        + [
            pltpu.VMEM((rows, SIDE * LANES), BF16),
            pltpu.VMEM((8 * states, SIDE * LANES), F32), pltpu.VMEM((count, rows), F32),
            pltpu.VMEM((rows, rank_width), BF16), pltpu.VMEM((rank_width, rows), F32),
        ],
    )


def step(*values):
    return lax.optimization_barrier(values)


def swap(value, axis, name="swap"):
    with jax.named_scope(f"{name}_{axis}"):
        return lax.ppermute(value, axis, SWAP)


def exchange_z(value, distance, name):
    size = lax.axis_size("z")
    with jax.named_scope(f"{name}_z"):
        return lax.ppermute(value, "z", [(i, i ^ distance) for i in range(size)])


def from_z(blocks, name):
    size = lax.axis_size("z")
    got = [blocks[0]]
    for shift in range(1, size):
        with jax.named_scope(f"{name}_z"):
            got.append(
                lax.ppermute(blocks[shift], "z", [(i, (i + shift) % size) for i in range(size)])
            )
    return got


def plus(value, *more):
    total = value.astype(F32)
    for v in more:
        total = total + v.astype(F32)
    return total.astype(BF16)


def to_owners(value):
    return lax.all_to_all(value, ZK, 0, 0, tiled=True)


def rank_in_class(keys):
    count = keys.shape[1]
    earlier = jnp.arange(count)[:, None] > jnp.arange(count)[None, :]
    same = (keys[:, :, None] == keys[:, None, :]) & earlier[None]
    return jnp.sum(same.astype(jnp.int32), axis=2)


def body(
    tokens, cotangent, owner_slot, sequence_lengths, norm_gain, inner_weight, filter_weight,
    convolution_bias, select_weight, step_weight, step_bias, decay_log, skip_weight, output_weight,
):
    rings = lax.axis_size("r")
    zs = lax.axis_size("z")
    members = zs * 4
    ri, zi, xi, ki, ti = (lax.axis_index(a) for a in ("r", "z", "x", "k", "t"))
    local_rows, width = tokens.shape
    rank_width = step_weight.shape[0]
    states = decay_log.shape[0]
    taps = filter_weight.shape[0]
    half_channels = inner_weight.shape[2]
    part = half_channels // (2 * zs)
    channels = 2 * part
    block_rows = inner_weight.shape[0]
    ring_rows = rings * block_rows
    depth = width // 2
    batch_rows = local_rows // MB
    group_rows = zs * local_rows
    segments = group_rows // batch_rows
    share = local_rows // 4

    def to_blocks(value):
        if rings == 1:
            return value
        value = value.reshape(-1, rings, members, block_rows)
        return value.transpose(0, 2, 1, 3).reshape(-1, width)

    def from_blocks(value):
        if rings == 1:
            return value
        value = value.reshape(-1, members, rings, block_rows)
        return value.transpose(0, 2, 1, 3).reshape(-1, width)

    inner = inner_weight
    outer = output_weight.T
    gain = norm_gain[None, :]
    if rings > 1:
        inner = lax.all_gather(inner, "r", axis=0, tiled=True)
        outer = lax.all_gather(outer, "r", axis=0, tiled=True)
        gain = lax.all_gather(gain, "r", axis=1, tiled=True)

    blocks_w = 3 * zs
    kept, sent = whole(
        first_pack_kernel, "pack", [zi, ki], (inner[:, 0], inner[:, 1], outer),
        [shape((blocks_w, ring_rows, part), BF16)] * 2,
    )

    slot_rows = owner_slot.reshape(rings, members, local_rows)
    tok, cot = tokens, cotangent
    ring_block = members * local_rows
    if rings > 1:
        per_ring = local_rows // rings
        flat = slot_rows.reshape(rings * members, local_rows)
        target = flat // ring_block
        place = target * per_ring + rank_in_class(target)
        chosen = jnp.arange(local_rows, dtype=jnp.int32)[None, :, None] == place[:, None, :]
        ordered = jnp.sum(jnp.where(chosen, flat[:, None, :], 0), axis=2)
        ordered = ordered.reshape(rings, members, rings, per_ring)
        ordered = lax.dynamic_index_in_dim(ordered, ri, 2, keepdims=False)
        slots = ordered.transpose(1, 0, 2).reshape(members, local_rows)
        own_place = lax.dynamic_index_in_dim(place, ri * members + zi * 4 + xi * 2 + ki, 0, False)
        ring_order = (
            jnp.arange(local_rows, dtype=jnp.int32)[:, None] == own_place[None, :]
        ).astype(BF16)

        def over_rings(value):
            value = value.reshape(rings, per_ring, width)
            return lax.all_to_all(value, "r", 0, 0, tiled=True).reshape(local_rows, width)

        tok, cot = (over_rings(dot(ring_order, v).astype(BF16)) for v in (tokens, cotangent))
    else:
        slots = slot_rows[0]
    local_slot = slots - ri * ring_block
    owner = local_slot // local_rows
    owner_z, owner_x, owner_k = owner // 4, (owner // 2) % 2, owner % 2
    rank = rank_in_class(owner_x * 2 + owner_k)
    in_owner = local_slot % local_rows
    scan_place = (in_owner % batch_rows) * segments + owner_z * MB + in_owner // batch_rows
    here = zi * 4 + xi * 2 + ki
    mine = [lax.dynamic_index_in_dim(v, here, 0, False) for v in (owner_x, owner_k, rank)]
    send_place = (mine[1] ^ ti) * (2 * share) + (mine[0] ^ xi) * share + mine[2]
    in_group = (owner_x == xi) & (owner_k == ti)
    ranked = (
        jnp.arange(share, dtype=jnp.int32)[None, :, None] == rank[:, None, :]
    ) & in_group[:, None, :]
    arrival = jnp.sum(jnp.where(ranked, scan_place[:, None, :], 0), axis=2)
    arrival = arrival.reshape(zs, 2, 2, share)
    arrival = jnp.where(xi == 0, arrival, arrival[:, ::-1]).transpose(0, 2, 1, 3)
    arrived = arrival.reshape(1, group_rows)
    returned = jnp.where(ki == 0, arrival, arrival[:, ::-1]).transpose(1, 0, 2, 3)
    returned = returned.reshape(group_rows, 1)

    blocks = [to_blocks(tok), to_blocks(cot)]
    lengths = sequence_lengths.reshape(1, -1).astype(BF16)
    lengths = jnp.concatenate([lengths, jnp.zeros((1, ring_rows - lengths.shape[1]), BF16)], 1)
    note = jnp.concatenate([gain, lengths, jnp.zeros((share - 2, ring_rows), BF16)], 0)
    noted, plain = shape((share, width + LANES), BF16), shape((share, width), BF16)
    blocks = step(kept, *blocks)[1:]
    rows_out = whole(
        prep_kernel, "prep", [xi], (send_place[None], *blocks, note), [noted, noted, plain, plain]
    )
    first = (zi * 2 + ki) * part

    def own_channels(value):
        return lax.dynamic_slice_in_dim(value, first, part, 1)

    rows_f = taps + 3 + states
    floats = own_channels(
        jnp.concatenate(
            [
                filter_weight, convolution_bias[None], step_bias[None], decay_log,
                skip_weight[None], jnp.zeros((-rows_f % 8, half_channels), F32),
            ],
            axis=0,
        )
    )
    layout = (rank_width, states, taps + 1, taps + 2, taps + 2 + states)
    select_t = lax.dynamic_slice_in_dim(select_weight, first, part, 0).T
    lows = jnp.concatenate([own_channels(step_weight), select_t], 0)
    count = select_t.shape[0]
    half_out = [shape((count, group_rows // 2), F32)] * 2
    half_rows = [shape((group_rows // 2, width), BF16)] * 2
    full = shape((group_rows, channels), F32)
    wide_low = shape((group_rows, width), BF16)
    half = depth // 2

    def gathered(keep, send):
        return lax.all_gather(jnp.concatenate([keep, send], 0), ZK, axis=0, tiled=True)

    tok_keep, tok_send, cot_keep, cot_send = rows_out
    (other_core,) = step(swap(sent, "k", "weights"))
    packed = whole(
        second_pack_kernel, "pack_cores", [ki], (kept, other_core),
        [shape((2 * ring_rows, part), BF16)] * blocks_w,
    )
    tok_got = swap(tok_send, "x", "tokens")
    group_tokens = gathered(tok_keep, tok_got)
    stream_own, floats_t, lows_t, *packed = step(
        jnp.concatenate(from_z(packed[:zs], "stream_w"), 0),
        swap(floats, "t", "params"), swap(lows, "t", "params_low"), *packed[zs:],
    )
    stream_x, stream_t, gate_own, *packed = step(
        swap(stream_own, "x", "stream_w"), swap(stream_own, "t", "stream_w"),
        jnp.concatenate(from_z(packed[:zs], "gate_w"), 0), *packed[zs:],
    )
    params = jnp.concatenate([floats, floats_t], axis=1)
    lows = jnp.concatenate([lows, lows_t], axis=1)
    step_w, select_w = lows[:rank_width], lows[rank_width:]
    stream_low, stream_high, outer_own, cot_got, gate_own, group_tokens = step(
        swap(stream_x[:half], "t", "stream_w_far"), swap(stream_t[half:], "x", "stream_w_far"),
        jnp.concatenate(from_z(packed, "outer_w"), 0), swap(cot_send, "x", "cot"),
        gate_own, group_tokens,
    )
    ws = (stream_own, stream_x, stream_t, stream_low, stream_high)
    group_cot = gathered(cot_keep, cot_got)
    normed, stream, act, sel_mine, sel_other, position, gain_row = whole(
        partial(front_kernel, (taps, sequence_lengths.shape[1])), "front", [ki, ti, zi],
        (group_tokens, arrived, *ws, params, select_w),
        [wide_low, full, full, *half_out, shape((group_rows, LANES), F32), shape((8, width), F32)],
        [pltpu.VMEM((group_rows, width), BF16), pltpu.VMEM((group_rows, channels), BF16)],
    )
    normed, stream, act, sel_mine, sel_other, gate_x, outer_t = step(
        normed, stream, act, sel_mine, sel_other,
        swap(gate_own, "x", "gate_w"), swap(outer_own, "t", "outer_w"),
    )
    sent = (sel_mine + swap(sel_other, "k", "select")).astype(BF16)
    got, gate_t, outer_x, sent = step(
        exchange_z(sent, 1, "select"), swap(gate_own, "t", "gate_w"),
        swap(outer_own, "x", "outer_w"), sent,
    )
    sent = plus(sent, got)
    got, gate_d, outer_d, sent = step(
        exchange_z(sent, 2, "select"), swap(gate_x, "t", "gate_w_far"),
        swap(outer_t, "x", "outer_w_far"), sent,
    )
    total = sent.astype(F32) + got.astype(F32)
    wg, wo = (gate_own, gate_x, gate_t, gate_d), (outer_own, outer_x, outer_t, outer_d)
    upstream, gate, gated_grad = whole(
        late_kernel, "late", [zi], (group_cot, arrived, normed, *wg, *wo), [wide_low, full, full],
    )
    rest = swap(total, "k", "select_rest")
    gated, gate_grad, act_grad, small_a, sel_mine, sel_other = mixer(
        layout, ki, position, act, gate, gated_grad, total, rest, step_w, params
    )

    out_mine, out_other = whole(
        out_kernel, "out_rows", [zi], (returned, gated, *wo), half_rows,
    )
    got, out_mine, out_other, gated, gate_grad = step(
        swap(sel_other, "k", "select"), out_mine, out_other, gated, gate_grad
    )
    sent = (sel_mine + got).astype(BF16)
    pieces = whole(
        late_grad_kernel, "late_grad", [zi], (normed, upstream, gate_grad, gated),
        [shape((2 * zs, part, ring_rows), BF16)] * 8,
    )
    got, out_got, sent, *pieces = step(
        exchange_z(sent, 1, "select"), swap(out_other, "k", "rows"), sent, *pieces
    )
    out_total = plus(out_mine, out_got)
    gate_g, outer_g = pieces[:4], pieces[4:]
    sent = plus(sent, got)
    got, sent, out_total, *pieces = step(
        exchange_z(sent, 2, "select"), sent, out_total, *pieces
    )
    gate_g, outer_g = pieces[:4], pieces[4:]
    out_back = lax.psum_scatter(out_total, "z", scatter_dimension=0, tiled=True)
    total = sent.astype(F32) + got.astype(F32)
    rest = swap(total, "k", "select_rest")
    low, small_b, *stream_g = whole(
        partial(back_kernel, taps), "back", [ki, zi],
        (total, rest, position, stream, act_grad, params, select_w, normed),
        [shape((group_rows, channels), BF16), shape((count + 8, channels), BF16)]
        + [shape((2 * zs, part // 2, ring_rows), BF16)] * 4
        + [shape((2, 2 * zs, part // 2, ring_rows), BF16)] * 2,
        [pltpu.VMEM((group_rows, channels), BF16), pltpu.VMEM((channels, group_rows), BF16)],
    )
    gate_far, outer_far, low, small_b, *more = step(
        swap(gate_g[3], "x", "gate_g_far"), swap(outer_g[3], "t", "outer_g_far"), low, small_b,
        *pieces, *stream_g,
    )
    pieces, stream_g = more[:8], more[8:]
    gate_g, outer_g = pieces[:4], pieces[4:]
    in_mine, in_other = whole(
        in_kernel, "in_rows", [zi], (returned, low, gate_grad, *ws, *wg),
        half_rows, [pltpu.VMEM((group_rows, 2 * channels), BF16)],
    )
    in_total = plus(in_mine, swap(in_other, "k", "rows"))
    in_back = lax.psum_scatter(in_total, "z", scatter_dimension=0, tiled=True)
    gate_first, outer_first, _, out_back, *pieces = step(
        swap(gate_g[1], "x", "gate_g"), swap(outer_g[2], "t", "outer_g"), in_total, out_back,
        *pieces,
    )
    gate_g, outer_g = pieces[:4], pieces[4:]
    small = jnp.concatenate([small_a, small_b], axis=0)
    gate_second, outer_second, small_got, small, in_back, *stream_g = step(
        swap(plus(gate_g[2], gate_far), "t", "gate_g_sum"),
        swap(plus(outer_g[1], outer_far), "x", "outer_g_sum"),
        swap(small[:, part:], "t", "small"), small, in_back, *stream_g,
    )
    late_sum = jnp.concatenate(
        [plus(gate_g[0], gate_first, gate_second), plus(outer_g[0], outer_first, outer_second)],
        axis=1,
    )
    late_home = to_owners(late_sum)
    own_low, own_high, by_x_high, by_t_low, x_way, t_way = stream_g
    small = plus(small[:, :part], small_got)

    def near_rows(rows):
        return jnp.concatenate([rows[:share], swap(rows[share:], "x", "rows")], 0)

    x_way, t_way, small_got, small, out_near = step(
        swap(x_way, "x", "stream_g"), swap(t_way, "t", "stream_g"), swap(small, "x", "small"),
        small, near_rows(out_back),
    )
    small = plus(small, small_got)
    if rings > 1:
        small = lax.psum(small.astype(F32), "r").astype(BF16)
    low_second, high_second, out_far, out_near, in_near, late_home, *gathered_small = step(
        swap(plus(by_t_low, x_way[0]), "t", "stream_g_sum"),
        swap(plus(by_x_high, t_way[0]), "x", "stream_g_sum"),
        swap(out_near, "t", "rows"), out_near, near_rows(in_back), late_home,
        *from_z([small] * zs, "small"),
    )
    stream_sum = jnp.concatenate(
        [plus(own_low, x_way[1], low_second), plus(own_high, t_way[1], high_second)], axis=1
    )
    stream_home, in_far, in_near = step(
        to_owners(stream_sum), swap(in_near, "t", "rows"), in_near
    )
    small_blocks = [v for block in gathered_small for v in (block, swap(block, "k", "small"))]

    back_place = send_place[:, None]
    if rings > 1:
        def own_rows(near, far, name):
            rows = whole(
                output_kernel, name, [xi], (back_place, near, far, jnp.zeros_like(tokens)),
                [shape(tokens.shape, BF16)],
            )[0]
            return dot(ring_order, from_blocks(over_rings(rows)), TN)

        output = (tokens.astype(F32) + own_rows(out_near, out_far, "output")).astype(BF16)
        rows = own_rows(in_near, in_far, "rows_back")
        own_x = tokens.astype(F32)
        inverse = lax.rsqrt(jnp.mean(own_x * own_x, axis=1, keepdims=True) + EPSILON)
        hat = own_x * inverse
        gain_rel = gain_row[:1].reshape(2, zs, 2, ring_rows)
        gain_abs = jnp.where(xi == 0, gain_rel, gain_rel[::-1]).transpose(1, 0, 2, 3)
        grad = rows * from_blocks(gain_abs.reshape(1, width))
        input_grad = cotangent.astype(F32) + inverse * (
            grad - hat * jnp.mean(grad * hat, axis=1, keepdims=True)
        )
    else:
        output = whole(
            output_kernel, "output", [xi], (back_place, out_near, out_far, tokens),
            [shape(tokens.shape, BF16)],
        )[0]
        input_grad = whole(
            input_kernel, "input_grad", [xi],
            (back_place, in_near, in_far, tokens, cotangent, gain_row),
            [shape(tokens.shape, F32)],
        )[0]
    one_row = shape((1, half_channels), F32)
    select_grad, step_w_grad, decay_grad, filter_grad, filter_b_grad, step_b_grad, skip_grad = whole(
        partial(small_kernel, (count, states, taps)), "small", [zi, ki], small_blocks,
        [
            shape((count, half_channels), F32), shape((rank_width, half_channels), F32),
            shape((states, half_channels), F32), shape((taps, half_channels), F32),
            one_row, one_row, one_row,
        ],
    )
    gate_home, outer_home = late_home[:, :part], late_home[:, part:]
    outer_home = outer_home.reshape(half_channels, ring_rows).astype(F32)
    inner_home = jnp.stack(
        [v.reshape(half_channels, ring_rows).T for v in (stream_home, gate_home)], axis=1
    ).astype(F32)
    if rings > 1:
        outer_home = lax.psum_scatter(outer_home, "r", scatter_dimension=1, tiled=True)
        inner_home = lax.psum_scatter(inner_home, "r", scatter_dimension=0, tiled=True)
    gain_grad = jnp.sum(inner_home * inner_weight.astype(F32), axis=(1, 2))
    gain_grad = (gain_grad + swap(gain_grad, "t", "gain")) / norm_gain.astype(F32)
    return (
        output,
        input_grad,
        gain_grad,
        inner_home,
        filter_grad,
        filter_b_grad[0],
        select_grad.T,
        step_w_grad,
        step_b_grad[0],
        decay_grad,
        skip_grad[0],
        outer_home,
    )


def solution(mesh):
    devices = mesh.devices
    split = Mesh(
        devices.reshape(devices.shape[0] // 16, 4, 2, 2, devices.shape[1]), DP + ("t",)
    )
    in_specs = (
        P(DP, None), P(DP, None), P(), P(DP, None), P(DP), P(DP, None, "t"), P(None, "t"), P("t"),
        P("t", None), P(None, "t"), P("t"), P(None, "t"), P("t"), P("t", DP),
    )
    out_specs = (
        P(DP, None), P(DP, None), P(DP), P(DP, None, "t"), P(None, "t"), P("t"), P("t", None),
        P(None, "t"), P("t"), P(None, "t"), P("t"), P("t", DP),
    )
    return jax.shard_map(body, mesh=split, in_specs=in_specs, out_specs=out_specs, check_vma=False)
```

```python
from functools import partial
from inspect import isgeneratorfunction

import jax
import jax.numpy as jnp
from jax import lax
from jax.experimental import pallas as pl
from jax.experimental.pallas import tpu as pltpu
from jax.sharding import Mesh, PartitionSpec as P

MB = 2
EPSILON = 1e-05
ZK = ("z", "k")
DP = ("r", "z", "x", "k")
SWAP = [(0, 1), (1, 0)]
LOG2E = 1.4426950408889634
RESET_RATE = 1e30
LANES = 128
MICROSECONDS = {
    "pack": 3, "pack_cores": 3, "prep": 2, "front": 8, "late": 8, "mixer": 24, "out_rows": 5,
    "late_grad": 6, "back": 7, "in_rows": 7, "output": 3, "input_grad": 4, "small": 3,
    "rows_back": 3,
}
SUBLANES = 8
SIDE = 2
GROUP = 8
CHUNK = 64
UNROLL = 2
LOAD, STORE = 0, 1
F32 = jnp.float32
BF16 = jnp.bfloat16
NT = ((1,), (1,))
TN = ((0,), (0,))


def dot(lhs, rhs, contract=((1,), (0,))):
    return lax.dot_general(lhs, rhs, (contract, ((), ())), preferred_element_type=F32)


def split_dot(lhs, rhs, contract=((1,), (0,))):
    high = lhs.astype(BF16)
    rest = (lhs - high.astype(F32)).astype(BF16)
    return dot(high, rhs, contract) + dot(rest, rhs, contract)


def shape(dims, dtype):
    return jax.ShapeDtypeStruct(dims, dtype)


def whole(kernel, name, scalars, arrays, outs, scratch=()):
    scalars = [jnp.reshape(v, (1,)).astype(jnp.int32) for v in scalars]
    few, many, made = len(scalars), len(arrays), len(outs)

    def copied(*refs):
        inputs, refs_rest = refs[few : few + many], refs[few + many :]
        outputs, refs_rest = refs_rest[:made], refs_rest[made:]
        held, results = refs_rest[:many], refs_rest[many : many + made]
        *rest, semaphores = refs_rest[many + made :]
        loads = [
            pltpu.make_async_copy(source, target, semaphores.at[i])
            for i, (source, target) in enumerate(zip(inputs, held))
        ]
        stores = [
            pltpu.make_async_copy(source, target, semaphores.at[many + i])
            for i, (source, target) in enumerate(zip(results, outputs))
        ]
        for copy in loads:
            copy.start()
        asked = {LOAD: set(), STORE: set()}

        def ask(kind, numbers):
            for i in numbers:
                if i not in asked[kind]:
                    asked[kind].add(i)
                    loads[i].wait() if kind == LOAD else stores[i].start()

        lazy = isgeneratorfunction(getattr(kernel, "func", kernel))
        if not lazy:
            ask(LOAD, range(many))
        parts = kernel(*refs[:few], *held, *results, *rest)
        for kind, numbers in parts if lazy else ():
            ask(kind, numbers)
        ask(LOAD, range(many))
        ask(STORE, range(made))
        for copy in stores:
            copy.wait()

    return pl.pallas_call(
        copied,
        in_specs=[pl.BlockSpec(memory_space=pltpu.SMEM)] * few
        + [pl.BlockSpec(memory_space=pltpu.HBM)] * many,
        out_specs=[pl.BlockSpec(memory_space=pltpu.HBM)] * made,
        out_shape=list(outs),
        scratch_shapes=[
            *(pltpu.VMEM(v.shape, v.dtype) for v in (*arrays, *outs)),
            *scratch,
            pltpu.SemaphoreType.DMA((many + made,)),
        ],
        compiler_params=pltpu.CompilerParams(vmem_limit_bytes=60 << 20),
        cost_estimate=pl.CostEstimate(
            flops=0, bytes_accessed=MICROSECONDS[name] * 3690000, transcendentals=0
        ),
        name=name,
    )(*scalars, *arrays)


def row_matches(places, count):
    rows = lax.broadcasted_iota(jnp.int32, (count, places.shape[1]), 0)
    return (rows == places).astype(F32).astype(BF16)


def column_matches(places, count):
    columns = lax.broadcasted_iota(jnp.int32, (places.shape[0], count), 1)
    return (columns == places).astype(F32).astype(BF16)


def tiles(count, size):
    return [slice(i, i + size) for i in range(0, count, size)]


def prep_kernel(x_ref, place_ref, tok_ref, cot_ref, note_ref, tok_keep, tok_send, cot_keep, cot_send):
    share = tok_keep.shape[0]
    width = tok_ref.shape[1]
    half = width // 2
    order = row_matches(place_ref[...], 2 * share)
    for source, outs in ((tok_ref, (tok_keep, tok_send)), (cot_ref, (cot_keep, cot_send))):
        rows = dot(order, source[...])
        for side in (0, 1):
            part = rows[side * share : (side + 1) * share]
            for x in (0, 1):
                same = x_ref[0] == (x ^ side)
                for zk in range(half // LANES):
                    place = (zk // 2) * 4 + zk % 2
                    zero = part[:, place * LANES : (place + 1) * LANES]
                    one = part[:, (place + 2) * LANES : (place + 3) * LANES]
                    to = slice(x * half + zk * LANES, x * half + (zk + 1) * LANES)
                    outs[side][:, to] = jnp.where(same, zero, one).astype(BF16)
    tok_keep[:, width:] = note_ref[...]
    tok_send[:, width:] = note_ref[...]


def place_rows(x_ref, place_ref, near_ref, far_ref):
    share = near_ref.shape[0] // 2
    width = near_ref.shape[1]
    half = width // 2
    order = column_matches(place_ref[...], 4 * share)
    total = None
    for group in range(4):
        source = (near_ref, far_ref)[group // 2]
        rows = slice((group % 2) * share, (group % 2 + 1) * share)
        blocks = []
        for block in range(width // LANES):
            z, x, k = block // 4, (block // 2) % 2, block % 2
            same = x_ref[0] == (x ^ (group % 2))
            at = (z * 2 + k) * LANES
            first = source[rows, at : at + LANES].astype(F32)
            second = source[rows, half + at : half + at + LANES].astype(F32)
            blocks.append(jnp.where(same, first, second).astype(BF16))
        piece = dot(order[:, group * share : (group + 1) * share], jnp.concatenate(blocks, 1))
        total = piece if total is None else total + piece
    return total


def output_kernel(x_ref, place_ref, near_ref, far_ref, tok_ref, out_ref):
    rows = place_rows(x_ref, place_ref, near_ref, far_ref)
    out_ref[...] = (tok_ref[...].astype(F32) + rows).astype(BF16)


def input_kernel(x_ref, place_ref, near_ref, far_ref, tok_ref, cot_ref, gain_ref, out_ref):
    rows = place_rows(x_ref, place_ref, near_ref, far_ref)
    x = tok_ref[...].astype(F32)
    inverse = lax.rsqrt(jnp.mean(x * x, axis=1, keepdims=True) + EPSILON)
    hat = x * inverse
    half = gain_ref.shape[1] // 2
    gains = []
    for block in range(x.shape[1] // LANES):
        z, side, k = block // 4, (block // 2) % 2, block % 2
        at = (z * 2 + k) * LANES
        gains.append(
            jnp.where(
                x_ref[0] == side,
                gain_ref[0:1, at : at + LANES],
                gain_ref[0:1, half + at : half + at + LANES],
            )
        )
    grad = rows * jnp.concatenate(gains, 1)
    out_ref[...] = cot_ref[...].astype(F32) + inverse * (
        grad - hat * jnp.mean(grad * hat, axis=1, keepdims=True)
    )


def column_sum(rows_ref, pieces):
    own, by_x, by_t, *diagonal = pieces
    depth = own.shape[0]
    near, far = rows_ref[:, :depth], rows_ref[:, depth:]
    a = dot(near, own[...]) + dot(far, by_x[...])
    b = dot(near, by_t[...])
    for i, at in enumerate(tiles(depth, diagonal[0].shape[0])):
        b = b + dot(far[:, at], diagonal[i][...])
    return a, b


def z_block(z_ref, step, size):
    return lax.rem(z_ref[0] + (size - step), size)


def row_sum(z_ref, sides, out_refs):
    depth = sides[0][1][0].shape[0]
    rows = sides[0][0].shape[0] // 2
    block = 2 * LANES
    for base in range(0, 2 * depth, block):
        at = slice(base % depth, base % depth + block)
        value = None
        for lhs, (own, by_x, by_t, *diagonal) in sides:
            part = lhs.shape[1] // 2
            if base < depth:
                near, far = own[at, :], by_t[at, :]
            else:
                size = diagonal[0].shape[0]
                inner = slice(at.start % size, at.start % size + block)
                near, far = by_x[at, :], diagonal[at.start // size][inner, :]
            term = dot(lhs[:, :part], near, NT) + dot(lhs[:, part:], far, NT)
            value = term if value is None else value + term
        place = z_block(z_ref, at.start // block, depth // block) * block
        to = pl.ds(pl.multiple_of(base // depth * depth + place, block), block)
        for i, out in enumerate(out_refs):
            out[:, to] = value[i * rows : (i + 1) * rows].astype(BF16)


def reorder_rows(z_ref, order, source, out):
    block = 2 * LANES
    half = out.shape[1] // 2
    for base in range(0, 2 * half, block):
        step = base % half // block
        place = base // half * half + z_block(z_ref, step, half // block) * block
        at = pl.ds(pl.multiple_of(place, block), block)
        out[:, base : base + block] = dot(order, source[:, at]).astype(BF16)


def grad_pieces(z_ref, channels_t, rows_ref, outs):
    part = channels_t.shape[0] // 2
    depth = rows_ref.shape[1] // 2
    for at in tiles(2 * depth, 2 * LANES):
        value = dot(channels_t, rows_ref[:, at])
        near_out, far_out = (outs[0], outs[2]) if at.start < depth else (outs[1], outs[3])
        block = 2 * z_block(z_ref, (at.start % depth) // (2 * LANES), depth // (2 * LANES))
        for i in (0, 1):
            lanes = value[:, i * LANES : (i + 1) * LANES].astype(BF16)
            for refs, rows in ((near_out, lanes[:part]), (far_out, lanes[part:])):
                size = part // len(refs)
                for j, ref in enumerate(refs):
                    ref[block + i, :, :] = rows[j * size : (j + 1) * size]


def first_pack_kernel(z_ref, k_ref, stream, gate, outer, keep, send):
    count = keep.shape[0] // 3
    part = keep.shape[2]
    for i, source in enumerate((stream, gate, outer)):
        for step in range(count):
            z = lax.rem(z_ref[0] + step, count)
            for out, core in ((keep, k_ref[0]), (send, 1 - k_ref[0])):
                at = pl.ds(pl.multiple_of((z * 2 + core) * part, part), part)
                out[i * count + step] = source[:, at]


def second_pack_kernel(k_ref, kept, got, *outs):
    first = k_ref[0] == 0
    height = kept.shape[1]
    for i, out in enumerate(outs):
        mine, other = kept[i].astype(F32), got[i].astype(F32)
        out[:height, :] = jnp.where(first, mine, other).astype(BF16)
        out[height:, :] = jnp.where(first, other, mine).astype(BF16)


def down(value, count):
    if count == 0:
        return value
    return jnp.concatenate([jnp.zeros((count, value.shape[1]), value.dtype), value[:-count]], 0)


def up(value, count):
    if count == 0:
        return value
    return jnp.concatenate([value[count:], jnp.zeros((count, value.shape[1]), value.dtype)], 0)


def lag_masks(place, taps):
    return [None] + [place >= lag for lag in range(1, taps)]


def masked(value, mask):
    return value if mask is None else jnp.where(mask, value, 0.0)


def filter_sum(stream, masks, weights):
    taps = len(masks)
    total = weights[taps : taps + 1, :] + weights[taps - 1 : taps, :] * stream
    for lag in range(1, taps):
        total = total + weights[taps - 1 - lag : taps - lag, :] * masked(
            down(stream, SUBLANES * lag), masks[lag]
        )
    return total


def places(notes, rows, per_device):
    segments = len(notes) * MB
    zero = lax.broadcasted_iota(jnp.int32, (segments, LANES), 0) % MB
    lane = lax.broadcasted_iota(jnp.int32, (segments, LANES), 1)
    table = jnp.concatenate([v for v in notes for _ in range(MB)], 0)
    begin = jnp.zeros((segments, 1), F32)
    step = lax.broadcasted_iota(jnp.int32, (rows, LANES), 0) // segments
    step = step.astype(F32)
    latest = jnp.zeros((rows, LANES), F32)
    for i in range(per_device - 1):
        picked = jnp.where(lane == zero * per_device + i, table, 0.0)
        begin = begin + jnp.sum(picked, axis=1, keepdims=True)
        every = jnp.concatenate(
            [jnp.broadcast_to(begin, (segments, LANES))] * (rows // segments), 0
        )
        latest = jnp.where(every <= step, every, latest)
    return step - latest


def front_kernel(
    sizes, core_ref, tensor_ref, z_ref, x_ref, place_ref, own, by_x, by_t, low, high, par_ref, sel_ref,
    n_ref, stream_ref, act_ref, mine_ref, other_ref, pos_ref, gain_ref, nrm, act_low,
):
    yield LOAD, (0, 1)
    taps, per_device = sizes
    rows = x_ref.shape[0]
    width = n_ref.shape[1]
    depth = width // 2
    part = own.shape[1]
    members = depth // LANES
    share = rows // (2 * members)
    note = slice(width, width + LANES)
    for side in (0, 1):
        for member in range(members):
            row = member * 2 * share + side * share
            at = side * depth + member * LANES
            gain_ref[0:1, at : at + LANES] = x_ref[row : row + 16, note].astype(F32)[0:1]
    notes = []
    for z in range(members // 2):
        two = [
            x_ref[m * 2 * share : m * 2 * share + 16, note].astype(F32)[1:2]
            for m in (2 * z, 2 * z + 1)
        ]
        notes.append(jnp.where(tensor_ref[0] == 0, two[0], two[1]))
    place = places(notes, rows, per_device)
    pos_ref[...] = place

    def norm(i, _):
        at = pl.ds(pl.multiple_of(i * 64, 64), 64)
        x = x_ref[at, :width].astype(F32)
        inverse = lax.rsqrt(jnp.mean(x * x, axis=1, keepdims=True) + EPSILON)
        nrm[at, :] = (x * inverse * gain_ref[0:1, :]).astype(BF16)
        return 0

    lax.fori_loop(0, rows // 64, norm, 0)
    reorder_rows(z_ref, row_matches(place_ref[...], rows), nrm, n_ref)
    yield STORE, (0, 5, 6)
    yield LOAD, (2, 3, 4, 5, 6)
    near, far = column_sum(n_ref, (own, by_x, by_t, low, high))
    stream_ref[:, :part] = near
    stream_ref[:, part:] = far
    yield STORE, (1,)
    yield LOAD, (7, 8)
    masks = lag_masks(place, taps)
    for at in tiles(2 * part, LANES):
        filtered = filter_sum(stream_ref[:, at], masks, par_ref[:, at])
        act = filtered * jax.nn.sigmoid(filtered)
        act_ref[:, at] = act
        act_low[:, at] = act.astype(BF16)
    yield STORE, (2,)
    selected = dot(sel_ref[...], act_low[...], NT)
    first = core_ref[0] == 0
    mine_ref[...] = jnp.where(first, selected[:, : rows // 2], selected[:, rows // 2 :])
    other_ref[...] = jnp.where(first, selected[:, rows // 2 :], selected[:, : rows // 2])


def late_kernel(z_ref, cot_ref, place_ref, n_ref, *refs):
    gate_pieces, out_pieces = refs[:4], refs[4:8]
    up_ref, gate_ref, gg_ref = refs[8:]
    part = gate_pieces[0].shape[1]
    yield LOAD, (0, 1)
    reorder_rows(z_ref, row_matches(place_ref[...], cot_ref.shape[0]), cot_ref, up_ref)
    yield STORE, (0,)
    for i, (source, out, pieces) in enumerate(
        ((n_ref, gate_ref, gate_pieces), (up_ref, gg_ref, out_pieces))
    ):
        yield LOAD, (2, *range(3 + 4 * i, 7 + 4 * i))
        near, far = column_sum(source, pieces)
        out[:, :part] = near
        out[:, part:] = far
        yield STORE, (1 + i,)


def out_kernel(z_ref, place_ref, gated_ref, *refs):
    yield LOAD, (0, 1)
    order = column_matches(place_ref[...], gated_ref.shape[0])
    rows = dot(order, gated_ref[...]).astype(BF16)
    yield LOAD, (2, 3, 4, 5)
    row_sum(z_ref, [(rows, refs[:4])], refs[4:])


def late_grad_kernel(z_ref, n_ref, up_ref, gate_grad_ref, gated_ref, *outs):
    gate_own, gate_t, outer_own, outer_x, x_way, t_way = outs
    for source, rows_ref, pieces, needs, ends in (
        (gate_grad_ref, n_ref, (gate_own, x_way.at[1], gate_t, x_way.at[0]), (2, 0), (4, 1, 0)),
        (gated_ref, up_ref, (outer_own, outer_x, t_way.at[1], t_way.at[0]), (3, 1), (5, 3, 2)),
    ):
        yield LOAD, needs[:1]
        channels_t = source[...].astype(F32).T.astype(BF16)
        yield LOAD, needs[1:]
        grad_pieces(z_ref, channels_t, rows_ref, [[v] for v in pieces])
        yield STORE, ends


def back_kernel(
    taps, core_ref, z_ref, total_ref, rest_ref, pos_ref, stream_ref, sact_ref, par_ref, sel_ref, n_ref,
    low_ref, small_ref, *refs,
):
    *outs, act_low, grad_t = refs
    yield LOAD, (0, 1, 2, 3, 4, 5, 6)
    rows, channels = stream_ref.shape
    first = core_ref[0] == 0
    total, rest = total_ref[...], rest_ref[...]
    selected_t = jnp.concatenate(
        [jnp.where(first, total, rest), jnp.where(first, rest, total)], 1
    )
    selected_low = selected_t.astype(BF16)
    count = selected_t.shape[0]
    padded = jnp.concatenate(
        [selected_t, jnp.zeros((-count % LANES, rows), F32)], 0
    )
    selected = padded.T.astype(BF16)
    masks = lag_masks(pos_ref[...], taps)
    spare = jnp.zeros((SUBLANES - taps - 1, LANES), F32)
    for at in tiles(channels, LANES):
        stream = stream_ref[:, at]
        weights = par_ref[:, at]
        filtered = filter_sum(stream, masks, weights)
        slope = jax.nn.sigmoid(filtered)
        act_low[:, at] = (filtered * slope).astype(BF16)
        select = jnp.concatenate(
            [sel_ref[:, at], jnp.zeros((-count % LANES, LANES), BF16)], 0
        )
        act_grad = sact_ref[:, at] + dot(selected, select)
        grad = act_grad * (slope * (1.0 + filtered * (1.0 - slope)))
        stream_grad = weights[taps - 1 : taps, :] * grad
        sums = [jnp.sum(grad * stream, axis=0, keepdims=True)]
        for lag in range(1, taps):
            part_grad = masked(grad, masks[lag])
            sums.append(
                jnp.sum(part_grad * down(stream, SUBLANES * lag), axis=0, keepdims=True)
            )
            stream_grad = stream_grad + weights[taps - 1 - lag : taps - lag, :] * up(
                part_grad, SUBLANES * lag
            )
        sums = sums[::-1] + [jnp.sum(grad, axis=0, keepdims=True), spare]
        small_ref[count:, at] = jnp.concatenate(sums, 0).astype(BF16)
        low_ref[:, at] = stream_grad.astype(BF16)
        grad_t[at, :] = stream_grad.T.astype(BF16)
    yield STORE, (0,)
    small_ref[:count, :] = dot(selected_low, act_low[...]).astype(BF16)
    yield STORE, (1,)
    yield LOAD, (7,)
    own_low, own_high, by_x_high, by_t_low, x_way, t_way = outs
    grad_pieces(
        z_ref, grad_t[...], n_ref,
        [
            (own_low, own_high), (x_way.at[1], by_x_high),
            (by_t_low, t_way.at[1]), (x_way.at[0], t_way.at[0]),
        ],
    )


def in_kernel(z_ref, place_ref, low_ref, gate_grad_ref, *refs):
    stream_pieces, gate_pieces, outs, stage = refs[:5], refs[5:9], refs[9:11], refs[11]
    channels = low_ref.shape[1]
    yield LOAD, (0, 1, 2)
    order = column_matches(place_ref[...], low_ref.shape[0])
    stage[:, :channels] = dot(order, low_ref[...]).astype(BF16)
    stage[:, channels:] = dot(order, gate_grad_ref[...]).astype(BF16)
    yield LOAD, range(3, 12)
    row_sum(
        z_ref, [(stage[:, :channels], stream_pieces), (stage[:, channels:], gate_pieces)], outs
    )


def small_kernel(
    sizes, z_ref, k_ref, *refs,
):
    count, states, taps = sizes
    blocks = refs[:-7]
    select, step_w, decay, filters, filter_b, step_b, skip = refs[-7:]
    part = blocks[0].shape[1]
    zs = len(blocks) // 2
    rank = step_w.shape[0]
    for i, block in enumerate(blocks):
        core = k_ref[0] if i % 2 == 0 else 1 - k_ref[0]
        place = (z_block(z_ref, i // 2, zs) * 2 + core) * part
        at = pl.ds(pl.multiple_of(place, part), part)
        first = block[: states + 8, :].astype(F32)
        step_b[:, at] = first[0:1]
        skip[:, at] = first[1:2]
        decay[:, at] = first[8:]
        step_w[:, at] = block[states + 8 : states + 8 + rank, :].astype(F32)
        rest = block[states + 8 + rank :, :].astype(F32)
        filters[:, at] = rest[count : count + taps]
        filter_b[:, at] = rest[count + taps : count + taps + 1]
        select[:, at] = rest[:count]


def scan_kernel(
    layout, core_ref, pos_ref, act_ref, gate_ref, gg_ref, total_ref, rest_ref, sw_ref, par_ref,
    gated_ref, gateg_ref, sact_ref, small_ref, mine_ref, other_ref,
    bb, cb, hist, fac, ci_acc, co_acc, rate_s, reff_s, u_s, ds_s, y_s, s2_s, slope_s, spre_low, decb, sel_t, rate_low, rank_t,
):
    rank_width, states, bias_row, decay_row, skip_row = layout
    rows, channels = act_ref.shape
    lanes = LANES
    steps = rows // SUBLANES
    wide = states * lanes
    first = core_ref[0] == 0
    spread = (
        lax.broadcasted_iota(jnp.int32, (states, wide), 1) // lanes
        == lax.broadcasted_iota(jnp.int32, (states, wide), 0)
    ).astype(F32).astype(BF16)
    yield LOAD, (4, 5)
    total, rest = total_ref[...], rest_ref[...]
    sel_t[:, : rows // 2] = jnp.where(first, total, rest)
    sel_t[:, rows // 2 :] = jnp.where(first, rest, total)
    rate_low[...] = sel_t[:rank_width, :].T.astype(BF16)
    twice = jnp.concatenate([spread, spread], 0)
    for out, base in ((bb, rank_width), (cb, rank_width + states)):
        value = sel_t[base : base + states, :]
        high = value.astype(BF16).astype(F32)
        parts = jnp.concatenate([high, value - high], 0).astype(BF16)
        out[...] = dot(parts, twice, TN)
    hist[0:SUBLANES, :] = jnp.zeros((SUBLANES, SIDE * wide), F32)
    ci_acc[...] = jnp.zeros_like(ci_acc)
    co_acc[...] = jnp.zeros_like(co_acc)
    rank_t[...] = jnp.zeros_like(rank_t)
    zero = jnp.zeros((8, lanes), F32)
    sides = range(SIDE)
    both = SIDE * lanes

    def cols(n):
        return slice(n * lanes, (n + 1) * lanes)

    def wide_cols(n, side):
        return slice((n * SIDE + side) * lanes, (n * SIDE + side + 1) * lanes)

    def side_cols(side):
        return slice(side * lanes, (side + 1) * lanes)

    def one_block(block, _):
        at = pl.ds(pl.multiple_of(block * both, both), both)
        decay = -jnp.exp(par_ref[decay_row : decay_row + states, at])
        for n in range(states):
            decb[8 * n : 8 * n + 8, :] = jnp.broadcast_to(decay[n : n + 1, :], (8, both))
        rate_s[...] = dot(rate_low[...], sw_ref[:, at]) + par_ref[bias_row : bias_row + 1, at]

        def before(i, _):
            row = pl.ds(pl.multiple_of(i * CHUNK, CHUNK), CHUNK)
            step_pre = rate_s[row, :]
            small = jnp.exp(-jnp.abs(step_pre))
            rate = jnp.maximum(step_pre, 0.0) + jnp.log1p(small)
            inverse = 1.0 / (1.0 + small)
            slope_s[row, :] = jnp.where(step_pre >= 0.0, inverse, small * inverse)
            rate_s[row, :] = rate
            keep = pos_ref[row, :] > 0.0
            for side in sides:
                reff_s[row, side_cols(side)] = jnp.where(
                    keep, rate[:, side_cols(side)] * LOG2E, RESET_RATE
                )
            u_s[row, :] = rate * act_ref[row, at]
            gate = gate_ref[row, at]
            ds_s[row, :] = gg_ref[row, at] * (gate * jax.nn.sigmoid(gate))
            return 0

        lax.fori_loop(0, rows // CHUNK, before, 0)

        for group in range(states // GROUP):
            names = range(group * GROUP, (group + 1) * GROUP)

            def forward(t, h, names=names, group=group):
                row = pl.ds(pl.multiple_of(t * 8, 8), 8)
                next_row = pl.ds(pl.multiple_of(t * 8 + 8, 8), 8)
                reff = [reff_s[row, side_cols(i)] for i in sides]
                u = [u_s[row, side_cols(i)] for i in sides]
                ds = [ds_s[row, side_cols(i)] for i in sides]
                y = [zero if group == 0 else y_s[row, side_cols(i)] for i in sides]
                fresh = []
                for n in names:
                    b, c = bb[row, cols(n)], cb[row, cols(n)]
                    out = co_acc[row, cols(n)]
                    for i in sides:
                        a = jnp.exp2(reff[i] * decb[8 * n : 8 * n + 8, side_cols(i)])
                        hn = a * h[len(fresh)] + b * u[i]
                        hist[next_row, wide_cols(n, i)] = hn
                        fac[row, wide_cols(n, i)] = a
                        y[i] = y[i] + c * hn
                        out = out + ds[i] * hn
                        fresh.append(hn)
                    co_acc[row, cols(n)] = out
                for i in sides:
                    y_s[row, side_cols(i)] = y[i]
                return tuple(fresh)

            lax.fori_loop(0, steps, forward, (zero,) * (GROUP * SIDE), unroll=UNROLL)

        skip = par_ref[skip_row : skip_row + 1, at]

        def between(i, _):
            row = pl.ds(pl.multiple_of(i * CHUNK, CHUNK), CHUNK)
            scanned = y_s[row, :] + skip * act_ref[row, at]
            gate = gate_ref[row, at]
            sig = jax.nn.sigmoid(gate)
            gated_ref[row, at] = (scanned * (gate * sig)).astype(BF16)
            gateg_ref[row, at] = (
                gg_ref[row, at] * scanned * (sig * (1.0 + gate * (1.0 - sig)))
            ).astype(BF16)
            return 0

        lax.fori_loop(0, rows // CHUNK, between, 0)

        sums = []
        for group in range(states // GROUP):
            names = range(group * GROUP, (group + 1) * GROUP)

            def backward(i, carried, names=names, group=group):
                g, dacc = carried
                t = steps - 1 - i
                row = pl.ds(pl.multiple_of(t * 8, 8), 8)
                ds = [ds_s[row, side_cols(k)] for k in sides]
                u = [u_s[row, side_cols(k)] for k in sides]
                rt = [rate_s[row, side_cols(k)] for k in sides]
                s1 = [zero if group == 0 else reff_s[row, side_cols(k)] for k in sides]
                s2 = [zero if group == 0 else s2_s[row, side_cols(k)] for k in sides]
                g_new, d_new = [], []
                for n in names:
                    b, c = bb[row, cols(n)], cb[row, cols(n)]
                    out = ci_acc[row, cols(n)]
                    for k in sides:
                        lam = c * ds[k] + g[len(g_new)]
                        q = lam * fac[row, wide_cols(n, k)]
                        hp = hist[row, wide_cols(n, k)] * q
                        s1[k] = s1[k] + hp * decb[8 * n : 8 * n + 8, side_cols(k)]
                        s2[k] = s2[k] + lam * b
                        out = out + lam * u[k]
                        d_new.append(dacc[len(g_new)] + hp * rt[k])
                        g_new.append(q)
                    ci_acc[row, cols(n)] = out
                for k in sides:
                    s2_s[row, side_cols(k)] = s2[k]
                    reff_s[row, side_cols(k)] = s1[k]
                return tuple(g_new), tuple(d_new)

            none = (zero,) * (GROUP * SIDE)
            _, dacc = lax.fori_loop(0, steps, backward, (none, none), unroll=UNROLL)
            for n in range(GROUP):
                row = jnp.concatenate(
                    [jnp.sum(dacc[n * SIDE + k], axis=0, keepdims=True) for k in sides], 1
                )
                name = group * GROUP + n
                sums.append(row * decb[8 * name : 8 * name + 1, :])

        def behind(i, carried):
            row = pl.ds(pl.multiple_of(i * CHUNK, CHUNK), CHUNK)
            act, dscan, s2_all = act_ref[row, at], ds_s[row, :], s2_s[row, :]
            sact_ref[row, at] = rate_s[row, :] * s2_all + skip * dscan
            spre = (reff_s[row, :] + act * s2_all) * slope_s[row, :]
            spre_low[row, :] = spre.astype(BF16)
            totals = []
            for total, value in zip(carried, (spre, dscan * act)):
                for j in range(CHUNK // SUBLANES):
                    total = total + value[j * SUBLANES : (j + 1) * SUBLANES]
                totals.append(total)
            return tuple(totals)

        empty = jnp.zeros((SUBLANES, both), F32)
        head = [
            jnp.sum(v, axis=0, keepdims=True)
            for v in lax.fori_loop(0, rows // CHUNK, behind, (empty, empty))
        ]
        head.append(jnp.zeros((6, both), F32))
        small_ref[: states + 8, at] = jnp.concatenate(head + sums, 0).astype(BF16)
        small_ref[states + 8 :, at] = dot(
            sel_t[:rank_width, :].astype(BF16), spre_low[...]
        ).astype(BF16)
        rank_t[...] += dot(sw_ref[:, at], spre_low[...], NT)
        return 0

    yield LOAD, (0, 1, 2, 3, 6, 7)
    lax.fori_loop(0, channels // both, one_block, 0)
    yield STORE, (0, 1, 2, 3)
    high, low = slice(0, rows // 2), slice(rows // 2, rows)
    for acc, base in ((ci_acc, rank_width), (co_acc, rank_width + states)):
        sel_t[base : base + states, :] = dot(acc[...].astype(BF16), spread, NT).T
    sel_t[:rank_width, :] = rank_t[...]
    mine_ref[...] = jnp.where(first, sel_t[:, high], sel_t[:, low])
    other_ref[...] = jnp.where(first, sel_t[:, low], sel_t[:, high])


def mixer(layout, core, position, act, gate, gated_grad, total, rest, step_w, params):
    rows, channels = act.shape
    rank_width, states = layout[:2]
    count = total.shape[0]
    wide = states * LANES
    return whole(
        partial(scan_kernel, layout), "mixer", [core],
        (position, act, gate, gated_grad, total, rest, step_w, params),
        [
            shape((rows, channels), BF16), shape((rows, channels), BF16),
            shape((rows, channels), F32), shape((rank_width + states + 8, channels), BF16),
            shape((count, rows // 2), F32), shape((count, rows // 2), F32),
        ],
        [
            pltpu.VMEM((rows, wide), F32), pltpu.VMEM((rows, wide), F32),
            pltpu.VMEM((rows + 8, SIDE * wide), F32), pltpu.VMEM((rows, SIDE * wide), F32),
            pltpu.VMEM((rows, wide), F32), pltpu.VMEM((rows, wide), F32),
        ]
        + [pltpu.VMEM((rows, SIDE * LANES), F32)] * 7
        + [
            pltpu.VMEM((rows, SIDE * LANES), BF16),
            pltpu.VMEM((8 * states, SIDE * LANES), F32), pltpu.VMEM((count, rows), F32),
            pltpu.VMEM((rows, rank_width), BF16), pltpu.VMEM((rank_width, rows), F32),
        ],
    )


def step(*values):
    return lax.optimization_barrier(values)


def swap(value, axis, name="swap"):
    with jax.named_scope(f"{name}_{axis}"):
        return lax.ppermute(value, axis, SWAP)


def exchange_z(value, distance, name):
    size = lax.axis_size("z")
    with jax.named_scope(f"{name}_z"):
        return lax.ppermute(value, "z", [(i, i ^ distance) for i in range(size)])


def from_z(blocks, name):
    size = lax.axis_size("z")
    got = [blocks[0]]
    for shift in range(1, size):
        with jax.named_scope(f"{name}_z"):
            got.append(
                lax.ppermute(blocks[shift], "z", [(i, (i + shift) % size) for i in range(size)])
            )
    return got


def plus(value, *more):
    total = value.astype(F32)
    for v in more:
        total = total + v.astype(F32)
    return total.astype(BF16)


def to_owners(value):
    return lax.all_to_all(value, ZK, 0, 0, tiled=True)


def rank_in_class(keys):
    count = keys.shape[1]
    earlier = jnp.arange(count)[:, None] > jnp.arange(count)[None, :]
    same = (keys[:, :, None] == keys[:, None, :]) & earlier[None]
    return jnp.sum(same.astype(jnp.int32), axis=2)


def body(
    tokens, cotangent, owner_slot, sequence_lengths, norm_gain, inner_weight, filter_weight,
    convolution_bias, select_weight, step_weight, step_bias, decay_log, skip_weight, output_weight,
):
    rings = lax.axis_size("r")
    zs = lax.axis_size("z")
    members = zs * 4
    ri, zi, xi, ki, ti = (lax.axis_index(a) for a in ("r", "z", "x", "k", "t"))
    local_rows, width = tokens.shape
    rank_width = step_weight.shape[0]
    states = decay_log.shape[0]
    taps = filter_weight.shape[0]
    half_channels = inner_weight.shape[2]
    part = half_channels // (2 * zs)
    channels = 2 * part
    block_rows = inner_weight.shape[0]
    ring_rows = rings * block_rows
    depth = width // 2
    batch_rows = local_rows // MB
    group_rows = zs * local_rows
    segments = group_rows // batch_rows
    share = local_rows // 4

    def to_blocks(value):
        if rings == 1:
            return value
        value = value.reshape(-1, rings, members, block_rows)
        return value.transpose(0, 2, 1, 3).reshape(-1, width)

    def from_blocks(value):
        if rings == 1:
            return value
        value = value.reshape(-1, members, rings, block_rows)
        return value.transpose(0, 2, 1, 3).reshape(-1, width)

    inner = inner_weight
    outer = output_weight.T
    gain = norm_gain[None, :]
    if rings > 1:
        inner = lax.all_gather(inner, "r", axis=0, tiled=True)
        outer = lax.all_gather(outer, "r", axis=0, tiled=True)
        gain = lax.all_gather(gain, "r", axis=1, tiled=True)

    blocks_w = 3 * zs
    kept, sent = whole(
        first_pack_kernel, "pack", [zi, ki], (inner[:, 0], inner[:, 1], outer),
        [shape((blocks_w, ring_rows, part), BF16)] * 2,
    )

    slot_rows = owner_slot.reshape(rings, members, local_rows)
    tok, cot = tokens, cotangent
    ring_block = members * local_rows
    if rings > 1:
        per_ring = local_rows // rings
        flat = slot_rows.reshape(rings * members, local_rows)
        target = flat // ring_block
        place = target * per_ring + rank_in_class(target)
        chosen = jnp.arange(local_rows, dtype=jnp.int32)[None, :, None] == place[:, None, :]
        ordered = jnp.sum(jnp.where(chosen, flat[:, None, :], 0), axis=2)
        ordered = ordered.reshape(rings, members, rings, per_ring)
        ordered = lax.dynamic_index_in_dim(ordered, ri, 2, keepdims=False)
        slots = ordered.transpose(1, 0, 2).reshape(members, local_rows)
        own_place = lax.dynamic_index_in_dim(place, ri * members + zi * 4 + xi * 2 + ki, 0, False)
        ring_order = (
            jnp.arange(local_rows, dtype=jnp.int32)[:, None] == own_place[None, :]
        ).astype(BF16)

        def over_rings(value):
            value = value.reshape(rings, per_ring, width)
            return lax.all_to_all(value, "r", 0, 0, tiled=True).reshape(local_rows, width)

        tok, cot = (over_rings(dot(ring_order, v).astype(BF16)) for v in (tokens, cotangent))
    else:
        slots = slot_rows[0]
    local_slot = slots - ri * ring_block
    owner = local_slot // local_rows
    owner_z, owner_x, owner_k = owner // 4, (owner // 2) % 2, owner % 2
    rank = rank_in_class(owner_x * 2 + owner_k)
    in_owner = local_slot % local_rows
    scan_place = (in_owner % batch_rows) * segments + owner_z * MB + in_owner // batch_rows
    here = zi * 4 + xi * 2 + ki
    mine = [lax.dynamic_index_in_dim(v, here, 0, False) for v in (owner_x, owner_k, rank)]
    send_place = (mine[1] ^ ti) * (2 * share) + (mine[0] ^ xi) * share + mine[2]
    in_group = (owner_x == xi) & (owner_k == ti)
    ranked = (
        jnp.arange(share, dtype=jnp.int32)[None, :, None] == rank[:, None, :]
    ) & in_group[:, None, :]
    arrival = jnp.sum(jnp.where(ranked, scan_place[:, None, :], 0), axis=2)
    arrival = arrival.reshape(zs, 2, 2, share)
    arrival = jnp.where(xi == 0, arrival, arrival[:, ::-1]).transpose(0, 2, 1, 3)
    arrived = arrival.reshape(1, group_rows)
    returned = jnp.where(ki == 0, arrival, arrival[:, ::-1]).transpose(1, 0, 2, 3)
    returned = returned.reshape(group_rows, 1)

    blocks = [to_blocks(tok), to_blocks(cot)]
    lengths = sequence_lengths.reshape(1, -1).astype(BF16)
    lengths = jnp.concatenate([lengths, jnp.zeros((1, ring_rows - lengths.shape[1]), BF16)], 1)
    note = jnp.concatenate([gain, lengths, jnp.zeros((share - 2, ring_rows), BF16)], 0)
    noted, plain = shape((share, width + LANES), BF16), shape((share, width), BF16)
    first = (zi * 2 + ki) * part

    def own_channels(value):
        return lax.dynamic_slice_in_dim(value, first, part, 1)

    rows_f = taps + 3 + states
    floats = own_channels(
        jnp.concatenate(
            [
                filter_weight, convolution_bias[None], step_bias[None], decay_log,
                skip_weight[None], jnp.zeros((-rows_f % 8, half_channels), F32),
            ],
            axis=0,
        )
    )
    layout = (rank_width, states, taps + 1, taps + 2, taps + 2 + states)
    select_t = lax.dynamic_slice_in_dim(select_weight, first, part, 0).T
    lows = jnp.concatenate([own_channels(step_weight), select_t], 0)
    count = select_t.shape[0]
    half_out = [shape((count, group_rows // 2), F32)] * 2
    half_rows = [shape((group_rows // 2, width), BF16)] * 2
    full = shape((group_rows, channels), F32)
    wide_low = shape((group_rows, width), BF16)
    half = depth // 2

    def gathered(keep, send):
        return lax.all_gather(jnp.concatenate([keep, send], 0), ZK, axis=0, tiled=True)

    (other_core,) = step(swap(sent, "k", "weights"))
    packed = whole(
        second_pack_kernel, "pack_cores", [ki], (kept, other_core),
        [shape((2 * ring_rows, part), BF16)] * blocks_w,
    )
    *packed, tok, cot = step(*packed, *blocks)
    tok_keep, tok_send, cot_keep, cot_send = whole(
        prep_kernel, "prep", [xi], (send_place[None], tok, cot, note), [noted, noted, plain, plain]
    )
    stream_own, floats_t, lows_t, tok_keep, tok_send, cot_keep, cot_send, *packed = step(
        jnp.concatenate(from_z(packed[:zs], "stream_w"), 0),
        swap(floats, "t", "params"), swap(lows, "t", "params_low"),
        tok_keep, tok_send, cot_keep, cot_send, *packed[zs:],
    )
    tok_got, stream_own = step(swap(tok_send, "x", "tokens"), stream_own)
    group_tokens = gathered(tok_keep, tok_got)
    params = jnp.concatenate([floats, floats_t], axis=1)
    lows = jnp.concatenate([lows, lows_t], axis=1)
    stream_x, stream_t, gate_own, params, step_w, select_w, arrived, returned, *packed = step(
        swap(stream_own, "x", "stream_w"), swap(stream_own, "t", "stream_w"),
        jnp.concatenate(from_z(packed[:zs], "gate_w"), 0), params, lows[:rank_width],
        lows[rank_width:], arrived, returned, *packed[zs:],
    )
    stream_low, stream_high, outer_own, cot_got, gate_own, group_tokens = step(
        swap(stream_x[:half], "t", "stream_w_far"), swap(stream_t[half:], "x", "stream_w_far"),
        jnp.concatenate(from_z(packed, "outer_w"), 0), swap(cot_send, "x", "cot"),
        gate_own, group_tokens,
    )
    ws = (stream_own, stream_x, stream_t, stream_low, stream_high)
    group_cot = gathered(cot_keep, cot_got)
    normed, stream, act, sel_mine, sel_other, position, gain_row = whole(
        partial(front_kernel, (taps, sequence_lengths.shape[1])), "front", [ki, ti, zi],
        (group_tokens, arrived, *ws, params, select_w),
        [wide_low, full, full, *half_out, shape((group_rows, LANES), F32), shape((8, width), F32)],
        [pltpu.VMEM((group_rows, width), BF16), pltpu.VMEM((group_rows, channels), BF16)],
    )
    normed, stream, act, sel_mine, sel_other, gate_x, outer_t = step(
        normed, stream, act, sel_mine, sel_other,
        swap(gate_own, "x", "gate_w"), swap(outer_own, "t", "outer_w"),
    )
    sent = (sel_mine + swap(sel_other, "k", "select")).astype(BF16)
    got, gate_t, outer_x, sent = step(
        exchange_z(sent, 1, "select"), swap(gate_own, "t", "gate_w"),
        swap(outer_own, "x", "outer_w"), sent,
    )
    sent = plus(sent, got)
    got, gate_d, outer_d, sent = step(
        exchange_z(sent, 2, "select"), swap(gate_x, "t", "gate_w_far"),
        swap(outer_t, "x", "outer_w_far"), sent,
    )
    total = sent.astype(F32) + got.astype(F32)
    wg, wo = (gate_own, gate_x, gate_t, gate_d), (outer_own, outer_x, outer_t, outer_d)
    upstream, gate, gated_grad = whole(
        late_kernel, "late", [zi], (group_cot, arrived, normed, *wg, *wo), [wide_low, full, full],
    )
    rest = swap(total, "k", "select_rest")
    gated, gate_grad, act_grad, small_a, sel_mine, sel_other = mixer(
        layout, ki, position, act, gate, gated_grad, total, rest, step_w, params
    )

    out_mine, out_other = whole(
        out_kernel, "out_rows", [zi], (returned, gated, *wo), half_rows,
    )
    got, out_mine, out_other, gated, gate_grad = step(
        swap(sel_other, "k", "select"), out_mine, out_other, gated, gate_grad
    )
    sent = (sel_mine + got).astype(BF16)
    pieces = whole(
        late_grad_kernel, "late_grad", [zi], (normed, upstream, gate_grad, gated),
        [shape((2 * zs, part, ring_rows), BF16)] * 4
        + [shape((2, 2 * zs, part, ring_rows), BF16)] * 2,
    )
    got, out_got, sent, *pieces = step(
        exchange_z(sent, 1, "select"), swap(out_other, "k", "rows"), sent, *pieces
    )
    out_total = plus(out_mine, out_got)
    sent = plus(sent, got)
    got, sent, out_total, *pieces = step(
        exchange_z(sent, 2, "select"), sent, out_total, *pieces
    )
    out_back = lax.psum_scatter(out_total, "z", scatter_dimension=0, tiled=True)
    total = sent.astype(F32) + got.astype(F32)
    rest = swap(total, "k", "select_rest")
    low, small_b, *stream_g = whole(
        partial(back_kernel, taps), "back", [ki, zi],
        (total, rest, position, stream, act_grad, params, select_w, normed),
        [shape((group_rows, channels), BF16), shape((count + 8, channels), BF16)]
        + [shape((2 * zs, part // 2, ring_rows), BF16)] * 4
        + [shape((2, 2 * zs, part // 2, ring_rows), BF16)] * 2,
        [pltpu.VMEM((group_rows, channels), BF16), pltpu.VMEM((channels, group_rows), BF16)],
    )
    gate_own_g, gate_t_g, outer_own_g, outer_x_g, x_way_l, t_way_l = pieces
    in_mine, in_other = whole(
        in_kernel, "in_rows", [zi], (returned, low, gate_grad, *ws, *wg),
        half_rows, [pltpu.VMEM((group_rows, 2 * channels), BF16)],
    )
    x_way_l, t_way_l, in_mine, in_other, out_back, small_b, *stream_g = step(
        swap(x_way_l, "x", "late_g"), swap(t_way_l, "t", "late_g"), in_mine, in_other, out_back,
        small_b, *stream_g,
    )
    in_total = plus(in_mine, swap(in_other, "k", "rows"))
    in_back = lax.psum_scatter(in_total, "z", scatter_dimension=0, tiled=True)
    small = jnp.concatenate([small_a, small_b], axis=0)
    gate_second, outer_second, small_got, small, *stream_g = step(
        swap(plus(gate_t_g, x_way_l[0]), "t", "gate_g_sum"),
        swap(plus(outer_x_g, t_way_l[0]), "x", "outer_g_sum"),
        swap(small[:, part:], "t", "small"), small, *stream_g,
    )
    late_sum = jnp.concatenate(
        [plus(gate_own_g, x_way_l[1], gate_second), plus(outer_own_g, t_way_l[1], outer_second)],
        axis=1,
    )
    late_home = to_owners(late_sum)
    own_low, own_high, by_x_high, by_t_low, x_way, t_way = stream_g
    small = plus(small[:, :part], small_got)

    def near_rows(rows):
        return jnp.concatenate([rows[:share], swap(rows[share:], "x", "rows")], 0)

    x_way, t_way, small_got, small, out_near, in_near = step(
        swap(x_way, "x", "stream_g"), swap(t_way, "t", "stream_g"), swap(small, "x", "small"),
        small, near_rows(out_back), near_rows(in_back),
    )
    small = plus(small, small_got)
    if rings > 1:
        small = lax.psum(small.astype(F32), "r").astype(BF16)
    low_second, high_second, out_far, in_far, *gathered_small = step(
        swap(plus(by_t_low, x_way[0]), "t", "stream_g_sum"),
        swap(plus(by_x_high, t_way[0]), "x", "stream_g_sum"),
        swap(out_near, "t", "rows"), swap(in_near, "t", "rows"),
        *from_z([small] * zs, "small"),
    )
    stream_sum = jnp.concatenate(
        [plus(own_low, x_way[1], low_second), plus(own_high, t_way[1], high_second)], axis=1
    )
    stream_home = to_owners(stream_sum)
    small_blocks = [v for block in gathered_small for v in (block, swap(block, "k", "small"))]

    back_place = send_place[:, None]
    if rings > 1:
        def own_rows(near, far, name):
            rows = whole(
                output_kernel, name, [xi], (back_place, near, far, jnp.zeros_like(tokens)),
                [shape(tokens.shape, BF16)],
            )[0]
            return dot(ring_order, from_blocks(over_rings(rows)), TN)

        output = (tokens.astype(F32) + own_rows(out_near, out_far, "output")).astype(BF16)
        rows = own_rows(in_near, in_far, "rows_back")
        own_x = tokens.astype(F32)
        inverse = lax.rsqrt(jnp.mean(own_x * own_x, axis=1, keepdims=True) + EPSILON)
        hat = own_x * inverse
        gain_rel = gain_row[:1].reshape(2, zs, 2, ring_rows)
        gain_abs = jnp.where(xi == 0, gain_rel, gain_rel[::-1]).transpose(1, 0, 2, 3)
        grad = rows * from_blocks(gain_abs.reshape(1, width))
        input_grad = cotangent.astype(F32) + inverse * (
            grad - hat * jnp.mean(grad * hat, axis=1, keepdims=True)
        )
    else:
        output = whole(
            output_kernel, "output", [xi], (back_place, out_near, out_far, tokens),
            [shape(tokens.shape, BF16)],
        )[0]
        input_grad = whole(
            input_kernel, "input_grad", [xi],
            (back_place, in_near, in_far, tokens, cotangent, gain_row),
            [shape(tokens.shape, F32)],
        )[0]
    one_row = shape((1, half_channels), F32)
    select_grad, step_w_grad, decay_grad, filter_grad, filter_b_grad, step_b_grad, skip_grad = whole(
        partial(small_kernel, (count, states, taps)), "small", [zi, ki], small_blocks,
        [
            shape((count, half_channels), F32), shape((rank_width, half_channels), F32),
            shape((states, half_channels), F32), shape((taps, half_channels), F32),
            one_row, one_row, one_row,
        ],
    )
    late_home, stream_home, output, input_grad, select_grad = step(
        late_home, stream_home, output, input_grad, select_grad
    )
    gate_home, outer_home = late_home[:, :part], late_home[:, part:]
    outer_home = outer_home.reshape(half_channels, ring_rows).astype(F32)
    inner_home = jnp.stack(
        [v.reshape(half_channels, ring_rows).T for v in (stream_home, gate_home)], axis=1
    ).astype(F32)
    if rings > 1:
        outer_home = lax.psum_scatter(outer_home, "r", scatter_dimension=1, tiled=True)
        inner_home = lax.psum_scatter(inner_home, "r", scatter_dimension=0, tiled=True)
    gain_grad = jnp.sum(inner_home * inner_weight.astype(F32), axis=(1, 2))
    gain_grad = (gain_grad + swap(gain_grad, "t", "gain")) / norm_gain.astype(F32)
    return (
        output,
        input_grad,
        gain_grad,
        inner_home,
        filter_grad,
        filter_b_grad[0],
        select_grad.T,
        step_w_grad,
        step_b_grad[0],
        decay_grad,
        skip_grad[0],
        outer_home,
    )


def solution(mesh):
    devices = mesh.devices
    split = Mesh(
        devices.reshape(devices.shape[0] // 16, 4, 2, 2, devices.shape[1]), DP + ("t",)
    )
    in_specs = (
        P(DP, None), P(DP, None), P(), P(DP, None), P(DP), P(DP, None, "t"), P(None, "t"), P("t"),
        P("t", None), P(None, "t"), P("t"), P(None, "t"), P("t"), P("t", DP),
    )
    out_specs = (
        P(DP, None), P(DP, None), P(DP), P(DP, None, "t"), P(None, "t"), P("t"), P("t", None),
        P(None, "t"), P("t"), P(None, "t"), P("t"), P("t", DP),
    )
    return jax.shard_map(body, mesh=split, in_specs=in_specs, out_specs=out_specs, check_vma=False)
```

```python
from functools import partial
from inspect import isgeneratorfunction

import jax
import jax.numpy as jnp
from jax import lax
from jax.experimental import pallas as pl
from jax.experimental.pallas import tpu as pltpu
from jax.sharding import Mesh, PartitionSpec as P

MB = 2
EPSILON = 1e-05
ZK = ("z", "k")
DP = ("r", "z", "x", "k")
SWAP = [(0, 1), (1, 0)]
LOG2E = 1.4426950408889634
RESET_RATE = 1e30
LANES = 128
MICROSECONDS = {
    "pack": 3, "pack_cores": 3, "prep": 2, "front": 8, "late": 8, "mixer": 24, "out_rows": 5,
    "late_grad": 6, "back": 7, "in_rows": 7, "output": 3, "input_grad": 4, "small": 3,
    "rows_back": 3,
}
SUBLANES = 8
SIDE = 2
GROUP = 8
CHUNK = 64
UNROLL = 4
LOAD, STORE = 0, 1
F32 = jnp.float32
BF16 = jnp.bfloat16
NT = ((1,), (1,))
TN = ((0,), (0,))


def dot(lhs, rhs, contract=((1,), (0,))):
    return lax.dot_general(lhs, rhs, (contract, ((), ())), preferred_element_type=F32)


def split_dot(lhs, rhs, contract=((1,), (0,))):
    high = lhs.astype(BF16)
    rest = (lhs - high.astype(F32)).astype(BF16)
    return dot(high, rhs, contract) + dot(rest, rhs, contract)


def shape(dims, dtype):
    return jax.ShapeDtypeStruct(dims, dtype)


def whole(kernel, name, scalars, arrays, outs, scratch=()):
    scalars = [jnp.reshape(v, (1,)).astype(jnp.int32) for v in scalars]
    few, many, made = len(scalars), len(arrays), len(outs)

    def copied(*refs):
        inputs, refs_rest = refs[few : few + many], refs[few + many :]
        outputs, refs_rest = refs_rest[:made], refs_rest[made:]
        held, results = refs_rest[:many], refs_rest[many : many + made]
        *rest, semaphores = refs_rest[many + made :]
        loads = [
            pltpu.make_async_copy(source, target, semaphores.at[i])
            for i, (source, target) in enumerate(zip(inputs, held))
        ]
        stores = [
            pltpu.make_async_copy(source, target, semaphores.at[many + i])
            for i, (source, target) in enumerate(zip(results, outputs))
        ]
        for copy in loads:
            copy.start()
        asked = {LOAD: set(), STORE: set()}

        def ask(kind, numbers):
            for i in numbers:
                if i not in asked[kind]:
                    asked[kind].add(i)
                    loads[i].wait() if kind == LOAD else stores[i].start()

        lazy = isgeneratorfunction(getattr(kernel, "func", kernel))
        if not lazy:
            ask(LOAD, range(many))
        parts = kernel(*refs[:few], *held, *results, *rest)
        for kind, numbers in parts if lazy else ():
            ask(kind, numbers)
        ask(LOAD, range(many))
        ask(STORE, range(made))
        for copy in stores:
            copy.wait()

    return pl.pallas_call(
        copied,
        in_specs=[pl.BlockSpec(memory_space=pltpu.SMEM)] * few
        + [pl.BlockSpec(memory_space=pltpu.HBM)] * many,
        out_specs=[pl.BlockSpec(memory_space=pltpu.HBM)] * made,
        out_shape=list(outs),
        scratch_shapes=[
            *(pltpu.VMEM(v.shape, v.dtype) for v in (*arrays, *outs)),
            *scratch,
            pltpu.SemaphoreType.DMA((many + made,)),
        ],
        compiler_params=pltpu.CompilerParams(vmem_limit_bytes=60 << 20),
        cost_estimate=pl.CostEstimate(
            flops=0, bytes_accessed=MICROSECONDS[name] * 3690000, transcendentals=0
        ),
        name=name,
    )(*scalars, *arrays)


def row_matches(places, count):
    rows = lax.broadcasted_iota(jnp.int32, (count, places.shape[1]), 0)
    return (rows == places).astype(F32).astype(BF16)


def column_matches(places, count):
    columns = lax.broadcasted_iota(jnp.int32, (places.shape[0], count), 1)
    return (columns == places).astype(F32).astype(BF16)


def tiles(count, size):
    return [slice(i, i + size) for i in range(0, count, size)]


def prep_kernel(x_ref, place_ref, tok_ref, cot_ref, note_ref, tok_keep, tok_send, cot_keep, cot_send):
    share = tok_keep.shape[0]
    width = tok_ref.shape[1]
    half = width // 2
    order = row_matches(place_ref[...], 2 * share)
    for source, outs in ((tok_ref, (tok_keep, tok_send)), (cot_ref, (cot_keep, cot_send))):
        rows = dot(order, source[...])
        for side in (0, 1):
            part = rows[side * share : (side + 1) * share]
            for x in (0, 1):
                same = x_ref[0] == (x ^ side)
                for zk in range(half // LANES):
                    place = (zk // 2) * 4 + zk % 2
                    zero = part[:, place * LANES : (place + 1) * LANES]
                    one = part[:, (place + 2) * LANES : (place + 3) * LANES]
                    to = slice(x * half + zk * LANES, x * half + (zk + 1) * LANES)
                    outs[side][:, to] = jnp.where(same, zero, one).astype(BF16)
    tok_keep[:, width:] = note_ref[...]
    tok_send[:, width:] = note_ref[...]


def place_rows(x_ref, place_ref, near_ref, far_ref):
    share = near_ref.shape[0] // 2
    width = near_ref.shape[1]
    half = width // 2
    order = column_matches(place_ref[...], 4 * share)
    total = None
    for group in range(4):
        source = (near_ref, far_ref)[group // 2]
        rows = slice((group % 2) * share, (group % 2 + 1) * share)
        blocks = []
        for block in range(width // LANES):
            z, x, k = block // 4, (block // 2) % 2, block % 2
            same = x_ref[0] == (x ^ (group % 2))
            at = (z * 2 + k) * LANES
            first = source[rows, at : at + LANES].astype(F32)
            second = source[rows, half + at : half + at + LANES].astype(F32)
            blocks.append(jnp.where(same, first, second).astype(BF16))
        piece = dot(order[:, group * share : (group + 1) * share], jnp.concatenate(blocks, 1))
        total = piece if total is None else total + piece
    return total


def output_kernel(x_ref, place_ref, near_ref, far_ref, tok_ref, out_ref):
    rows = place_rows(x_ref, place_ref, near_ref, far_ref)
    out_ref[...] = (tok_ref[...].astype(F32) + rows).astype(BF16)


def input_kernel(x_ref, place_ref, near_ref, far_ref, tok_ref, cot_ref, gain_ref, out_ref):
    rows = place_rows(x_ref, place_ref, near_ref, far_ref)
    x = tok_ref[...].astype(F32)
    inverse = lax.rsqrt(jnp.mean(x * x, axis=1, keepdims=True) + EPSILON)
    hat = x * inverse
    half = gain_ref.shape[1] // 2
    gains = []
    for block in range(x.shape[1] // LANES):
        z, side, k = block // 4, (block // 2) % 2, block % 2
        at = (z * 2 + k) * LANES
        gains.append(
            jnp.where(
                x_ref[0] == side,
                gain_ref[0:1, at : at + LANES],
                gain_ref[0:1, half + at : half + at + LANES],
            )
        )
    grad = rows * jnp.concatenate(gains, 1)
    out_ref[...] = cot_ref[...].astype(F32) + inverse * (
        grad - hat * jnp.mean(grad * hat, axis=1, keepdims=True)
    )


def column_sum(rows_ref, pieces):
    own, by_x, by_t, *diagonal = pieces
    depth = own.shape[0]
    near, far = rows_ref[:, :depth], rows_ref[:, depth:]
    a = dot(near, own[...]) + dot(far, by_x[...])
    b = dot(near, by_t[...])
    for i, at in enumerate(tiles(depth, diagonal[0].shape[0])):
        b = b + dot(far[:, at], diagonal[i][...])
    return a, b


def z_block(z_ref, step, size):
    return lax.rem(z_ref[0] + (size - step), size)


def row_sum(z_ref, sides, out_refs):
    depth = sides[0][1][0].shape[0]
    rows = sides[0][0].shape[0] // 2
    block = 2 * LANES
    for base in range(0, 2 * depth, block):
        at = slice(base % depth, base % depth + block)
        value = None
        for lhs, (own, by_x, by_t, *diagonal) in sides:
            part = lhs.shape[1] // 2
            if base < depth:
                near, far = own[at, :], by_t[at, :]
            else:
                size = diagonal[0].shape[0]
                inner = slice(at.start % size, at.start % size + block)
                near, far = by_x[at, :], diagonal[at.start // size][inner, :]
            term = dot(lhs[:, :part], near, NT) + dot(lhs[:, part:], far, NT)
            value = term if value is None else value + term
        place = z_block(z_ref, at.start // block, depth // block) * block
        to = pl.ds(pl.multiple_of(base // depth * depth + place, block), block)
        for i, out in enumerate(out_refs):
            out[:, to] = value[i * rows : (i + 1) * rows].astype(BF16)


def reorder_rows(z_ref, order, source, out):
    block = 2 * LANES
    half = out.shape[1] // 2
    for base in range(0, 2 * half, block):
        step = base % half // block
        place = base // half * half + z_block(z_ref, step, half // block) * block
        at = pl.ds(pl.multiple_of(place, block), block)
        out[:, base : base + block] = dot(order, source[:, at]).astype(BF16)


def grad_pieces(z_ref, channels_t, rows_ref, outs):
    part = channels_t.shape[0] // 2
    depth = rows_ref.shape[1] // 2
    for at in tiles(2 * depth, 2 * LANES):
        value = dot(channels_t, rows_ref[:, at])
        near_out, far_out = (outs[0], outs[2]) if at.start < depth else (outs[1], outs[3])
        block = 2 * z_block(z_ref, (at.start % depth) // (2 * LANES), depth // (2 * LANES))
        for i in (0, 1):
            lanes = value[:, i * LANES : (i + 1) * LANES].astype(BF16)
            for refs, rows in ((near_out, lanes[:part]), (far_out, lanes[part:])):
                size = part // len(refs)
                for j, ref in enumerate(refs):
                    ref[block + i, :, :] = rows[j * size : (j + 1) * size]


def first_pack_kernel(z_ref, k_ref, stream, gate, outer, keep, send):
    count = keep.shape[0] // 3
    part = keep.shape[2]
    for i, source in enumerate((stream, gate, outer)):
        for step in range(count):
            z = lax.rem(z_ref[0] + step, count)
            for out, core in ((keep, k_ref[0]), (send, 1 - k_ref[0])):
                at = pl.ds(pl.multiple_of((z * 2 + core) * part, part), part)
                out[i * count + step] = source[:, at]


def second_pack_kernel(k_ref, kept, got, *outs):
    first = k_ref[0] == 0
    height = kept.shape[1]
    for i, out in enumerate(outs):
        mine, other = kept[i].astype(F32), got[i].astype(F32)
        out[:height, :] = jnp.where(first, mine, other).astype(BF16)
        out[height:, :] = jnp.where(first, other, mine).astype(BF16)


def down(value, count):
    if count == 0:
        return value
    return jnp.concatenate([jnp.zeros((count, value.shape[1]), value.dtype), value[:-count]], 0)


def up(value, count):
    if count == 0:
        return value
    return jnp.concatenate([value[count:], jnp.zeros((count, value.shape[1]), value.dtype)], 0)


def lag_masks(place, taps):
    return [None] + [place >= lag for lag in range(1, taps)]


def masked(value, mask):
    return value if mask is None else jnp.where(mask, value, 0.0)


def filter_sum(stream, masks, weights):
    taps = len(masks)
    total = weights[taps : taps + 1, :] + weights[taps - 1 : taps, :] * stream
    for lag in range(1, taps):
        total = total + weights[taps - 1 - lag : taps - lag, :] * masked(
            down(stream, SUBLANES * lag), masks[lag]
        )
    return total


def places(notes, rows, per_device):
    segments = len(notes) * MB
    zero = lax.broadcasted_iota(jnp.int32, (segments, LANES), 0) % MB
    lane = lax.broadcasted_iota(jnp.int32, (segments, LANES), 1)
    table = jnp.concatenate([v for v in notes for _ in range(MB)], 0)
    begin = jnp.zeros((segments, 1), F32)
    step = lax.broadcasted_iota(jnp.int32, (rows, LANES), 0) // segments
    step = step.astype(F32)
    latest = jnp.zeros((rows, LANES), F32)
    for i in range(per_device - 1):
        picked = jnp.where(lane == zero * per_device + i, table, 0.0)
        begin = begin + jnp.sum(picked, axis=1, keepdims=True)
        every = jnp.concatenate(
            [jnp.broadcast_to(begin, (segments, LANES))] * (rows // segments), 0
        )
        latest = jnp.where(every <= step, every, latest)
    return step - latest


def front_kernel(
    sizes, core_ref, tensor_ref, z_ref, x_ref, place_ref, own, by_x, by_t, low, high, par_ref, sel_ref,
    n_ref, stream_ref, act_ref, mine_ref, other_ref, pos_ref, gain_ref, nrm, act_low,
):
    yield LOAD, (0, 1)
    taps, per_device = sizes
    rows = x_ref.shape[0]
    width = n_ref.shape[1]
    depth = width // 2
    part = own.shape[1]
    members = depth // LANES
    share = rows // (2 * members)
    note = slice(width, width + LANES)
    for side in (0, 1):
        for member in range(members):
            row = member * 2 * share + side * share
            at = side * depth + member * LANES
            gain_ref[0:1, at : at + LANES] = x_ref[row : row + 16, note].astype(F32)[0:1]
    notes = []
    for z in range(members // 2):
        two = [
            x_ref[m * 2 * share : m * 2 * share + 16, note].astype(F32)[1:2]
            for m in (2 * z, 2 * z + 1)
        ]
        notes.append(jnp.where(tensor_ref[0] == 0, two[0], two[1]))
    place = places(notes, rows, per_device)
    pos_ref[...] = place

    def norm(i, _):
        at = pl.ds(pl.multiple_of(i * 64, 64), 64)
        x = x_ref[at, :width].astype(F32)
        inverse = lax.rsqrt(jnp.mean(x * x, axis=1, keepdims=True) + EPSILON)
        nrm[at, :] = (x * inverse * gain_ref[0:1, :]).astype(BF16)
        return 0

    lax.fori_loop(0, rows // 64, norm, 0)
    reorder_rows(z_ref, row_matches(place_ref[...], rows), nrm, n_ref)
    yield STORE, (0, 5, 6)
    yield LOAD, (2, 3, 4, 5, 6)
    near, far = column_sum(n_ref, (own, by_x, by_t, low, high))
    stream_ref[:, :part] = near
    stream_ref[:, part:] = far
    yield STORE, (1,)
    yield LOAD, (7, 8)
    masks = lag_masks(place, taps)
    for at in tiles(2 * part, LANES):
        filtered = filter_sum(stream_ref[:, at], masks, par_ref[:, at])
        act = filtered * jax.nn.sigmoid(filtered)
        act_ref[:, at] = act
        act_low[:, at] = act.astype(BF16)
    yield STORE, (2,)
    selected = dot(sel_ref[...], act_low[...], NT)
    first = core_ref[0] == 0
    mine_ref[...] = jnp.where(first, selected[:, : rows // 2], selected[:, rows // 2 :])
    other_ref[...] = jnp.where(first, selected[:, rows // 2 :], selected[:, : rows // 2])


def late_kernel(z_ref, cot_ref, place_ref, n_ref, *refs):
    gate_pieces, out_pieces = refs[:4], refs[4:8]
    up_ref, gate_ref, gg_ref = refs[8:]
    part = gate_pieces[0].shape[1]
    yield LOAD, (0, 1)
    reorder_rows(z_ref, row_matches(place_ref[...], cot_ref.shape[0]), cot_ref, up_ref)
    yield STORE, (0,)
    for i, (source, out, pieces) in enumerate(
        ((n_ref, gate_ref, gate_pieces), (up_ref, gg_ref, out_pieces))
    ):
        yield LOAD, (2, *range(3 + 4 * i, 7 + 4 * i))
        near, far = column_sum(source, pieces)
        out[:, :part] = near
        out[:, part:] = far
        yield STORE, (1 + i,)


def out_kernel(z_ref, place_ref, gated_ref, *refs):
    yield LOAD, (0, 1)
    order = column_matches(place_ref[...], gated_ref.shape[0])
    rows = dot(order, gated_ref[...]).astype(BF16)
    yield LOAD, (2, 3, 4, 5)
    row_sum(z_ref, [(rows, refs[:4])], refs[4:])


def late_grad_kernel(z_ref, n_ref, up_ref, gate_grad_ref, gated_ref, *outs):
    gate_own, gate_t, outer_own, outer_x, x_way, t_way = outs
    for source, rows_ref, pieces, needs, ends in (
        (gate_grad_ref, n_ref, (gate_own, x_way.at[1], gate_t, x_way.at[0]), (2, 0), (4, 1, 0)),
        (gated_ref, up_ref, (outer_own, outer_x, t_way.at[1], t_way.at[0]), (3, 1), (5, 3, 2)),
    ):
        yield LOAD, needs[:1]
        channels_t = source[...].astype(F32).T.astype(BF16)
        yield LOAD, needs[1:]
        grad_pieces(z_ref, channels_t, rows_ref, [[v] for v in pieces])
        yield STORE, ends


def back_kernel(
    taps, core_ref, z_ref, total_ref, rest_ref, pos_ref, stream_ref, sact_ref, par_ref, sel_ref, n_ref,
    low_ref, small_ref, *refs,
):
    *outs, act_low, grad_t = refs
    yield LOAD, (0, 1, 2, 3, 4, 5, 6)
    rows, channels = stream_ref.shape
    first = core_ref[0] == 0
    total, rest = total_ref[...], rest_ref[...]
    selected_t = jnp.concatenate(
        [jnp.where(first, total, rest), jnp.where(first, rest, total)], 1
    )
    selected_low = selected_t.astype(BF16)
    count = selected_t.shape[0]
    padded = jnp.concatenate(
        [selected_t, jnp.zeros((-count % LANES, rows), F32)], 0
    )
    selected = padded.T.astype(BF16)
    masks = lag_masks(pos_ref[...], taps)
    spare = jnp.zeros((SUBLANES - taps - 1, LANES), F32)
    for at in tiles(channels, LANES):
        stream = stream_ref[:, at]
        weights = par_ref[:, at]
        filtered = filter_sum(stream, masks, weights)
        slope = jax.nn.sigmoid(filtered)
        act_low[:, at] = (filtered * slope).astype(BF16)
        select = jnp.concatenate(
            [sel_ref[:, at], jnp.zeros((-count % LANES, LANES), BF16)], 0
        )
        act_grad = sact_ref[:, at] + dot(selected, select)
        grad = act_grad * (slope * (1.0 + filtered * (1.0 - slope)))
        stream_grad = weights[taps - 1 : taps, :] * grad
        sums = [jnp.sum(grad * stream, axis=0, keepdims=True)]
        for lag in range(1, taps):
            part_grad = masked(grad, masks[lag])
            sums.append(
                jnp.sum(part_grad * down(stream, SUBLANES * lag), axis=0, keepdims=True)
            )
            stream_grad = stream_grad + weights[taps - 1 - lag : taps - lag, :] * up(
                part_grad, SUBLANES * lag
            )
        sums = sums[::-1] + [jnp.sum(grad, axis=0, keepdims=True), spare]
        small_ref[count:, at] = jnp.concatenate(sums, 0).astype(BF16)
        low_ref[:, at] = stream_grad.astype(BF16)
        grad_t[at, :] = stream_grad.T.astype(BF16)
    yield STORE, (0,)
    small_ref[:count, :] = dot(selected_low, act_low[...]).astype(BF16)
    yield STORE, (1,)
    yield LOAD, (7,)
    own_low, own_high, by_x_high, by_t_low, x_way, t_way = outs
    grad_pieces(
        z_ref, grad_t[...], n_ref,
        [
            (own_low, own_high), (x_way.at[1], by_x_high),
            (by_t_low, t_way.at[1]), (x_way.at[0], t_way.at[0]),
        ],
    )


def in_kernel(z_ref, place_ref, low_ref, gate_grad_ref, *refs):
    stream_pieces, gate_pieces, outs, stage = refs[:5], refs[5:9], refs[9:11], refs[11]
    channels = low_ref.shape[1]
    yield LOAD, (0, 1, 2)
    order = column_matches(place_ref[...], low_ref.shape[0])
    stage[:, :channels] = dot(order, low_ref[...]).astype(BF16)
    stage[:, channels:] = dot(order, gate_grad_ref[...]).astype(BF16)
    yield LOAD, range(3, 12)
    row_sum(
        z_ref, [(stage[:, :channels], stream_pieces), (stage[:, channels:], gate_pieces)], outs
    )


def small_kernel(sizes, z_ref, x_ref, k_ref, mine, other, *outs):
    count, states, taps, zs = sizes
    select, step_w, decay, filters, filter_b, step_b, skip = outs
    part = mine.shape[1]
    rank = step_w.shape[0]
    half = mine.shape[0] // (2 * zs)
    first_x = x_ref[0] == 0
    for source, core in ((mine, k_ref[0]), (other, 1 - k_ref[0])):
        for shift in range(zs):
            near = source[shift * half : (shift + 1) * half, :].astype(F32)
            far = source[(zs + shift) * half : (zs + shift + 1) * half, :].astype(F32)
            block = jnp.concatenate(
                [jnp.where(first_x, near, far), jnp.where(first_x, far, near)], 0
            )
            place = (z_block(z_ref, shift, zs) * 2 + core) * part
            at = pl.ds(pl.multiple_of(place, part), part)
            step_b[:, at] = block[0:1]
            skip[:, at] = block[1:2]
            decay[:, at] = block[8 : states + 8]
            step_w[:, at] = block[states + 8 : states + 8 + rank]
            rest = block[states + 8 + rank :]
            filters[:, at] = rest[count : count + taps]
            filter_b[:, at] = rest[count + taps : count + taps + 1]
            select[:, at] = rest[:count]


def scan_kernel(
    layout, core_ref, pos_ref, act_ref, gate_ref, gg_ref, total_ref, rest_ref, sw_ref, par_ref,
    gated_ref, gateg_ref, sact_ref, small_ref, mine_ref, other_ref,
    bb, cb, hist, fac, ci_acc, co_acc, rate_s, reff_s, u_s, ds_s, y_s, s2_s, slope_s, spre_low, decb, sel_t, rate_low, rank_t,
):
    rank_width, states, bias_row, decay_row, skip_row = layout
    rows, channels = act_ref.shape
    lanes = LANES
    steps = rows // SUBLANES
    wide = states * lanes
    first = core_ref[0] == 0
    spread = (
        lax.broadcasted_iota(jnp.int32, (states, wide), 1) // lanes
        == lax.broadcasted_iota(jnp.int32, (states, wide), 0)
    ).astype(F32).astype(BF16)
    yield LOAD, (4, 5)
    total, rest = total_ref[...], rest_ref[...]
    sel_t[:, : rows // 2] = jnp.where(first, total, rest)
    sel_t[:, rows // 2 :] = jnp.where(first, rest, total)
    rate_low[...] = sel_t[:rank_width, :].T.astype(BF16)
    twice = jnp.concatenate([spread, spread], 0)
    for out, base in ((bb, rank_width), (cb, rank_width + states)):
        value = sel_t[base : base + states, :]
        high = value.astype(BF16).astype(F32)
        parts = jnp.concatenate([high, value - high], 0).astype(BF16)
        out[...] = dot(parts, twice, TN)
    hist[0:SUBLANES, :] = jnp.zeros((SUBLANES, SIDE * wide), F32)
    ci_acc[...] = jnp.zeros_like(ci_acc)
    co_acc[...] = jnp.zeros_like(co_acc)
    rank_t[...] = jnp.zeros_like(rank_t)
    zero = jnp.zeros((8, lanes), F32)
    sides = range(SIDE)
    both = SIDE * lanes

    def cols(n):
        return slice(n * lanes, (n + 1) * lanes)

    def wide_cols(n, side):
        return slice((n * SIDE + side) * lanes, (n * SIDE + side + 1) * lanes)

    def side_cols(side):
        return slice(side * lanes, (side + 1) * lanes)

    def one_block(block, _):
        at = pl.ds(pl.multiple_of(block * both, both), both)
        decay = -jnp.exp(par_ref[decay_row : decay_row + states, at])
        for n in range(states):
            decb[8 * n : 8 * n + 8, :] = jnp.broadcast_to(decay[n : n + 1, :], (8, both))
        rate_s[...] = dot(rate_low[...], sw_ref[:, at]) + par_ref[bias_row : bias_row + 1, at]

        def before(i, _):
            row = pl.ds(pl.multiple_of(i * CHUNK, CHUNK), CHUNK)
            step_pre = rate_s[row, :]
            small = jnp.exp(-jnp.abs(step_pre))
            rate = jnp.maximum(step_pre, 0.0) + jnp.log1p(small)
            inverse = 1.0 / (1.0 + small)
            slope_s[row, :] = jnp.where(step_pre >= 0.0, inverse, small * inverse)
            rate_s[row, :] = rate
            keep = pos_ref[row, :] > 0.0
            for side in sides:
                reff_s[row, side_cols(side)] = jnp.where(
                    keep, rate[:, side_cols(side)] * LOG2E, RESET_RATE
                )
            u_s[row, :] = rate * act_ref[row, at]
            gate = gate_ref[row, at]
            ds_s[row, :] = gg_ref[row, at] * (gate * jax.nn.sigmoid(gate))
            return 0

        lax.fori_loop(0, rows // CHUNK, before, 0)

        for group in range(states // GROUP):
            names = range(group * GROUP, (group + 1) * GROUP)

            def forward(t, h, names=names, group=group):
                row = pl.ds(pl.multiple_of(t * 8, 8), 8)
                next_row = pl.ds(pl.multiple_of(t * 8 + 8, 8), 8)
                reff = [reff_s[row, side_cols(i)] for i in sides]
                u = [u_s[row, side_cols(i)] for i in sides]
                ds = [ds_s[row, side_cols(i)] for i in sides]
                y = [zero if group == 0 else y_s[row, side_cols(i)] for i in sides]
                fresh = []
                for n in names:
                    b, c = bb[row, cols(n)], cb[row, cols(n)]
                    out = co_acc[row, cols(n)]
                    for i in sides:
                        a = jnp.exp2(reff[i] * decb[8 * n : 8 * n + 8, side_cols(i)])
                        hn = a * h[len(fresh)] + b * u[i]
                        hist[next_row, wide_cols(n, i)] = hn
                        fac[row, wide_cols(n, i)] = a
                        y[i] = y[i] + c * hn
                        out = out + ds[i] * hn
                        fresh.append(hn)
                    co_acc[row, cols(n)] = out
                for i in sides:
                    y_s[row, side_cols(i)] = y[i]
                return tuple(fresh)

            lax.fori_loop(0, steps, forward, (zero,) * (GROUP * SIDE), unroll=UNROLL)

        skip = par_ref[skip_row : skip_row + 1, at]

        def between(i, _):
            row = pl.ds(pl.multiple_of(i * CHUNK, CHUNK), CHUNK)
            scanned = y_s[row, :] + skip * act_ref[row, at]
            gate = gate_ref[row, at]
            sig = jax.nn.sigmoid(gate)
            gated_ref[row, at] = (scanned * (gate * sig)).astype(BF16)
            gateg_ref[row, at] = (
                gg_ref[row, at] * scanned * (sig * (1.0 + gate * (1.0 - sig)))
            ).astype(BF16)
            return 0

        lax.fori_loop(0, rows // CHUNK, between, 0)

        sums = []
        for group in range(states // GROUP):
            names = range(group * GROUP, (group + 1) * GROUP)

            def backward(i, carried, names=names, group=group):
                g, dacc = carried
                t = steps - 1 - i
                row = pl.ds(pl.multiple_of(t * 8, 8), 8)
                ds = [ds_s[row, side_cols(k)] for k in sides]
                u = [u_s[row, side_cols(k)] for k in sides]
                rt = [rate_s[row, side_cols(k)] for k in sides]
                s1 = [zero if group == 0 else reff_s[row, side_cols(k)] for k in sides]
                s2 = [zero if group == 0 else s2_s[row, side_cols(k)] for k in sides]
                g_new, d_new = [], []
                for n in names:
                    b, c = bb[row, cols(n)], cb[row, cols(n)]
                    out = ci_acc[row, cols(n)]
                    for k in sides:
                        lam = c * ds[k] + g[len(g_new)]
                        q = lam * fac[row, wide_cols(n, k)]
                        hp = hist[row, wide_cols(n, k)] * q
                        s1[k] = s1[k] + hp * decb[8 * n : 8 * n + 8, side_cols(k)]
                        s2[k] = s2[k] + lam * b
                        out = out + lam * u[k]
                        d_new.append(dacc[len(g_new)] + hp * rt[k])
                        g_new.append(q)
                    ci_acc[row, cols(n)] = out
                for k in sides:
                    s2_s[row, side_cols(k)] = s2[k]
                    reff_s[row, side_cols(k)] = s1[k]
                return tuple(g_new), tuple(d_new)

            none = (zero,) * (GROUP * SIDE)
            _, dacc = lax.fori_loop(0, steps, backward, (none, none), unroll=UNROLL)
            for n in range(GROUP):
                row = jnp.concatenate(
                    [jnp.sum(dacc[n * SIDE + k], axis=0, keepdims=True) for k in sides], 1
                )
                name = group * GROUP + n
                sums.append(row * decb[8 * name : 8 * name + 1, :])

        def behind(i, carried):
            row = pl.ds(pl.multiple_of(i * CHUNK, CHUNK), CHUNK)
            act, dscan, s2_all = act_ref[row, at], ds_s[row, :], s2_s[row, :]
            sact_ref[row, at] = rate_s[row, :] * s2_all + skip * dscan
            spre = (reff_s[row, :] + act * s2_all) * slope_s[row, :]
            spre_low[row, :] = spre.astype(BF16)
            totals = []
            for total, value in zip(carried, (spre, dscan * act)):
                for j in range(CHUNK // SUBLANES):
                    total = total + value[j * SUBLANES : (j + 1) * SUBLANES]
                totals.append(total)
            return tuple(totals)

        empty = jnp.zeros((SUBLANES, both), F32)
        head = [
            jnp.sum(v, axis=0, keepdims=True)
            for v in lax.fori_loop(0, rows // CHUNK, behind, (empty, empty))
        ]
        head.append(jnp.zeros((6, both), F32))
        small_ref[: states + 8, at] = jnp.concatenate(head + sums, 0).astype(BF16)
        small_ref[states + 8 :, at] = dot(
            sel_t[:rank_width, :].astype(BF16), spre_low[...]
        ).astype(BF16)
        rank_t[...] += dot(sw_ref[:, at], spre_low[...], NT)
        return 0

    yield LOAD, (0, 1, 2, 3, 6, 7)
    lax.fori_loop(0, channels // both, one_block, 0)
    yield STORE, (0, 1, 2, 3)
    high, low = slice(0, rows // 2), slice(rows // 2, rows)
    for acc, base in ((ci_acc, rank_width), (co_acc, rank_width + states)):
        sel_t[base : base + states, :] = dot(acc[...].astype(BF16), spread, NT).T
    sel_t[:rank_width, :] = rank_t[...]
    mine_ref[...] = jnp.where(first, sel_t[:, high], sel_t[:, low])
    other_ref[...] = jnp.where(first, sel_t[:, low], sel_t[:, high])


def mixer(layout, core, position, act, gate, gated_grad, total, rest, step_w, params):
    rows, channels = act.shape
    rank_width, states = layout[:2]
    count = total.shape[0]
    wide = states * LANES
    return whole(
        partial(scan_kernel, layout), "mixer", [core],
        (position, act, gate, gated_grad, total, rest, step_w, params),
        [
            shape((rows, channels), BF16), shape((rows, channels), BF16),
            shape((rows, channels), F32), shape((rank_width + states + 8, channels), BF16),
            shape((count, rows // 2), F32), shape((count, rows // 2), F32),
        ],
        [
            pltpu.VMEM((rows, wide), F32), pltpu.VMEM((rows, wide), F32),
            pltpu.VMEM((rows + 8, SIDE * wide), F32), pltpu.VMEM((rows, SIDE * wide), F32),
            pltpu.VMEM((rows, wide), F32), pltpu.VMEM((rows, wide), F32),
        ]
        + [pltpu.VMEM((rows, SIDE * LANES), F32)] * 7
        + [
            pltpu.VMEM((rows, SIDE * LANES), BF16),
            pltpu.VMEM((8 * states, SIDE * LANES), F32), pltpu.VMEM((count, rows), F32),
            pltpu.VMEM((rows, rank_width), BF16), pltpu.VMEM((rank_width, rows), F32),
        ],
    )


def step(*values):
    return lax.optimization_barrier(values)


def swap(value, axis, name="swap"):
    with jax.named_scope(f"{name}_{axis}"):
        return lax.ppermute(value, axis, SWAP)


def exchange_z(value, distance, name):
    size = lax.axis_size("z")
    with jax.named_scope(f"{name}_z"):
        return lax.ppermute(value, "z", [(i, i ^ distance) for i in range(size)])


def from_z(blocks, name):
    size = lax.axis_size("z")
    got = [blocks[0]]
    for shift in range(1, size):
        with jax.named_scope(f"{name}_z"):
            got.append(
                lax.ppermute(blocks[shift], "z", [(i, (i + shift) % size) for i in range(size)])
            )
    return got


def plus(value, *more):
    total = value.astype(F32)
    for v in more:
        total = total + v.astype(F32)
    return total.astype(BF16)


def to_owners(value):
    return lax.all_to_all(value, ZK, 0, 0, tiled=True)


def rank_in_class(keys):
    count = keys.shape[1]
    earlier = jnp.arange(count)[:, None] > jnp.arange(count)[None, :]
    same = (keys[:, :, None] == keys[:, None, :]) & earlier[None]
    return jnp.sum(same.astype(jnp.int32), axis=2)


def body(
    tokens, cotangent, owner_slot, sequence_lengths, norm_gain, inner_weight, filter_weight,
    convolution_bias, select_weight, step_weight, step_bias, decay_log, skip_weight, output_weight,
):
    rings = lax.axis_size("r")
    zs = lax.axis_size("z")
    members = zs * 4
    ri, zi, xi, ki, ti = (lax.axis_index(a) for a in ("r", "z", "x", "k", "t"))
    local_rows, width = tokens.shape
    rank_width = step_weight.shape[0]
    states = decay_log.shape[0]
    taps = filter_weight.shape[0]
    half_channels = inner_weight.shape[2]
    part = half_channels // (2 * zs)
    channels = 2 * part
    block_rows = inner_weight.shape[0]
    ring_rows = rings * block_rows
    depth = width // 2
    batch_rows = local_rows // MB
    group_rows = zs * local_rows
    segments = group_rows // batch_rows
    share = local_rows // 4

    def to_blocks(value):
        if rings == 1:
            return value
        value = value.reshape(-1, rings, members, block_rows)
        return value.transpose(0, 2, 1, 3).reshape(-1, width)

    def from_blocks(value):
        if rings == 1:
            return value
        value = value.reshape(-1, members, rings, block_rows)
        return value.transpose(0, 2, 1, 3).reshape(-1, width)

    inner = inner_weight
    outer = output_weight.T
    gain = norm_gain[None, :]
    if rings > 1:
        inner = lax.all_gather(inner, "r", axis=0, tiled=True)
        outer = lax.all_gather(outer, "r", axis=0, tiled=True)
        gain = lax.all_gather(gain, "r", axis=1, tiled=True)

    blocks_w = 3 * zs
    kept, sent = whole(
        first_pack_kernel, "pack", [zi, ki], (inner[:, 0], inner[:, 1], outer),
        [shape((blocks_w, ring_rows, part), BF16)] * 2,
    )

    slot_rows = owner_slot.reshape(rings, members, local_rows)
    tok, cot = tokens, cotangent
    ring_block = members * local_rows
    if rings > 1:
        per_ring = local_rows // rings
        flat = slot_rows.reshape(rings * members, local_rows)
        target = flat // ring_block
        place = target * per_ring + rank_in_class(target)
        chosen = jnp.arange(local_rows, dtype=jnp.int32)[None, :, None] == place[:, None, :]
        ordered = jnp.sum(jnp.where(chosen, flat[:, None, :], 0), axis=2)
        ordered = ordered.reshape(rings, members, rings, per_ring)
        ordered = lax.dynamic_index_in_dim(ordered, ri, 2, keepdims=False)
        slots = ordered.transpose(1, 0, 2).reshape(members, local_rows)
        own_place = lax.dynamic_index_in_dim(place, ri * members + zi * 4 + xi * 2 + ki, 0, False)
        ring_order = (
            jnp.arange(local_rows, dtype=jnp.int32)[:, None] == own_place[None, :]
        ).astype(BF16)

        def over_rings(value):
            value = value.reshape(rings, per_ring, width)
            return lax.all_to_all(value, "r", 0, 0, tiled=True).reshape(local_rows, width)

        tok, cot = (over_rings(dot(ring_order, v).astype(BF16)) for v in (tokens, cotangent))
    else:
        slots = slot_rows[0]
    local_slot = slots - ri * ring_block
    owner = local_slot // local_rows
    owner_z, owner_x, owner_k = owner // 4, (owner // 2) % 2, owner % 2
    rank = rank_in_class(owner_x * 2 + owner_k)
    in_owner = local_slot % local_rows
    scan_place = (in_owner % batch_rows) * segments + owner_z * MB + in_owner // batch_rows
    here = zi * 4 + xi * 2 + ki
    mine = [lax.dynamic_index_in_dim(v, here, 0, False) for v in (owner_x, owner_k, rank)]
    send_place = (mine[1] ^ ti) * (2 * share) + (mine[0] ^ xi) * share + mine[2]
    in_group = (owner_x == xi) & (owner_k == ti)
    ranked = (
        jnp.arange(share, dtype=jnp.int32)[None, :, None] == rank[:, None, :]
    ) & in_group[:, None, :]
    arrival = jnp.sum(jnp.where(ranked, scan_place[:, None, :], 0), axis=2)
    arrival = arrival.reshape(zs, 2, 2, share)
    arrival = jnp.where(xi == 0, arrival, arrival[:, ::-1]).transpose(0, 2, 1, 3)
    arrived = arrival.reshape(1, group_rows)
    returned = jnp.where(ki == 0, arrival, arrival[:, ::-1]).transpose(1, 0, 2, 3)
    returned = returned.reshape(group_rows, 1)

    blocks = [to_blocks(tok), to_blocks(cot)]
    lengths = sequence_lengths.reshape(1, -1).astype(BF16)
    lengths = jnp.concatenate([lengths, jnp.zeros((1, ring_rows - lengths.shape[1]), BF16)], 1)
    note = jnp.concatenate([gain, lengths, jnp.zeros((share - 2, ring_rows), BF16)], 0)
    noted, plain = shape((share, width + LANES), BF16), shape((share, width), BF16)
    first = (zi * 2 + ki) * part

    def own_channels(value):
        return lax.dynamic_slice_in_dim(value, first, part, 1)

    rows_f = taps + 3 + states
    floats = own_channels(
        jnp.concatenate(
            [
                filter_weight, convolution_bias[None], step_bias[None], decay_log,
                skip_weight[None], jnp.zeros((-rows_f % 8, half_channels), F32),
            ],
            axis=0,
        )
    )
    layout = (rank_width, states, taps + 1, taps + 2, taps + 2 + states)
    select_t = lax.dynamic_slice_in_dim(select_weight, first, part, 0).T
    lows = jnp.concatenate([own_channels(step_weight), select_t], 0)
    count = select_t.shape[0]
    half_out = [shape((count, group_rows // 2), F32)] * 2
    half_rows = [shape((group_rows // 2, width), BF16)] * 2
    full = shape((group_rows, channels), F32)
    wide_low = shape((group_rows, width), BF16)
    half = depth // 2

    def gathered(keep, send):
        return lax.all_gather(jnp.concatenate([keep, send], 0), ZK, axis=0, tiled=True)

    (other_core,) = step(swap(sent, "k", "weights"))
    packed = whole(
        second_pack_kernel, "pack_cores", [ki], (kept, other_core),
        [shape((2 * ring_rows, part), BF16)] * blocks_w,
    )
    *packed, tok, cot = step(*packed, *blocks)
    tok_keep, tok_send, cot_keep, cot_send = whole(
        prep_kernel, "prep", [xi], (send_place[None], tok, cot, note), [noted, noted, plain, plain]
    )
    stream_own, floats_t, lows_t, tok_keep, tok_send, cot_keep, cot_send, *packed = step(
        jnp.concatenate(from_z(packed[:zs], "stream_w"), 0),
        swap(floats, "t", "params"), swap(lows, "t", "params_low"),
        tok_keep, tok_send, cot_keep, cot_send, *packed[zs:],
    )
    tok_got, stream_own = step(swap(tok_send, "x", "tokens"), stream_own)
    group_tokens = gathered(tok_keep, tok_got)
    params = jnp.concatenate([floats, floats_t], axis=1)
    lows = jnp.concatenate([lows, lows_t], axis=1)
    stream_x, stream_t, gate_own, params, step_w, select_w, arrived, returned, cot_got, *packed = step(
        swap(stream_own, "x", "stream_w"), swap(stream_own, "t", "stream_w"),
        jnp.concatenate(from_z(packed[:zs], "gate_w"), 0), params, lows[:rank_width],
        lows[rank_width:], arrived, returned, swap(cot_send, "x", "cot"), *packed[zs:],
    )
    group_cot = gathered(cot_keep, cot_got)
    stream_low, stream_high, outer_own, gate_own, group_tokens = step(
        swap(stream_x[:half], "t", "stream_w_far"), swap(stream_t[half:], "x", "stream_w_far"),
        jnp.concatenate(from_z(packed, "outer_w"), 0), gate_own, group_tokens,
    )
    ws = (stream_own, stream_x, stream_t, stream_low, stream_high)
    normed, stream, act, sel_mine, sel_other, position, gain_row = whole(
        partial(front_kernel, (taps, sequence_lengths.shape[1])), "front", [ki, ti, zi],
        (group_tokens, arrived, *ws, params, select_w),
        [wide_low, full, full, *half_out, shape((group_rows, LANES), F32), shape((8, width), F32)],
        [pltpu.VMEM((group_rows, width), BF16), pltpu.VMEM((group_rows, channels), BF16)],
    )
    normed, stream, act, sel_mine, sel_other, gate_x, outer_t = step(
        normed, stream, act, sel_mine, sel_other,
        swap(gate_own, "x", "gate_w"), swap(outer_own, "t", "outer_w"),
    )
    sent = (sel_mine + swap(sel_other, "k", "select")).astype(BF16)
    got, gate_t, outer_x, sent = step(
        exchange_z(sent, 1, "select"), swap(gate_own, "t", "gate_w"),
        swap(outer_own, "x", "outer_w"), sent,
    )
    sent = plus(sent, got)
    got, gate_d, outer_d, sent = step(
        exchange_z(sent, 2, "select"), swap(gate_x, "t", "gate_w_far"),
        swap(outer_t, "x", "outer_w_far"), sent,
    )
    total = sent.astype(F32) + got.astype(F32)
    wg, wo = (gate_own, gate_x, gate_t, gate_d), (outer_own, outer_x, outer_t, outer_d)
    upstream, gate, gated_grad = whole(
        late_kernel, "late", [zi], (group_cot, arrived, normed, *wg, *wo), [wide_low, full, full],
    )
    rest = swap(total, "k", "select_rest")
    gated, gate_grad, act_grad, small_a, sel_mine, sel_other = mixer(
        layout, ki, position, act, gate, gated_grad, total, rest, step_w, params
    )

    out_mine, out_other = whole(
        out_kernel, "out_rows", [zi], (returned, gated, *wo), half_rows,
    )
    got, out_mine, out_other, gated, gate_grad = step(
        swap(sel_other, "k", "select"), out_mine, out_other, gated, gate_grad
    )
    sent = (sel_mine + got).astype(BF16)
    pieces = whole(
        late_grad_kernel, "late_grad", [zi], (normed, upstream, gate_grad, gated),
        [shape((2 * zs, part, ring_rows), BF16)] * 4
        + [shape((2, 2 * zs, part, ring_rows), BF16)] * 2,
    )
    got, out_got, sent, *pieces = step(
        exchange_z(sent, 1, "select"), swap(out_other, "k", "rows"), sent, *pieces
    )
    out_total = plus(out_mine, out_got)
    sent = plus(sent, got)
    got, sent, out_total, *pieces = step(
        exchange_z(sent, 2, "select"), sent, out_total, *pieces
    )
    out_back = lax.psum_scatter(out_total, "z", scatter_dimension=0, tiled=True)
    total = sent.astype(F32) + got.astype(F32)
    rest = swap(total, "k", "select_rest")
    low, small_b, *stream_g = whole(
        partial(back_kernel, taps), "back", [ki, zi],
        (total, rest, position, stream, act_grad, params, select_w, normed),
        [shape((group_rows, channels), BF16), shape((count + 8, channels), BF16)]
        + [shape((2 * zs, part // 2, ring_rows), BF16)] * 4
        + [shape((2, 2 * zs, part // 2, ring_rows), BF16)] * 2,
        [pltpu.VMEM((group_rows, channels), BF16), pltpu.VMEM((channels, group_rows), BF16)],
    )
    gate_own_g, gate_t_g, outer_own_g, outer_x_g, x_way_l, t_way_l = pieces
    in_mine, in_other = whole(
        in_kernel, "in_rows", [zi], (returned, low, gate_grad, *ws, *wg),
        half_rows, [pltpu.VMEM((group_rows, 2 * channels), BF16)],
    )
    x_way_l, t_way_l, in_mine, in_other, out_back, small_b, *stream_g = step(
        swap(x_way_l, "x", "late_g"), swap(t_way_l, "t", "late_g"), in_mine, in_other, out_back,
        small_b, *stream_g,
    )
    in_total = plus(in_mine, swap(in_other, "k", "rows"))
    in_back = lax.psum_scatter(in_total, "z", scatter_dimension=0, tiled=True)
    small = jnp.concatenate([small_a, small_b], axis=0)
    gate_second, outer_second, small_got, small, *stream_g = step(
        swap(plus(gate_t_g, x_way_l[0]), "t", "gate_g_sum"),
        swap(plus(outer_x_g, t_way_l[0]), "x", "outer_g_sum"),
        swap(small[:, part:], "t", "small"), small, *stream_g,
    )
    late_sum = jnp.concatenate(
        [plus(gate_own_g, x_way_l[1], gate_second), plus(outer_own_g, t_way_l[1], outer_second)],
        axis=1,
    )
    late_home = to_owners(late_sum)
    own_low, own_high, by_x_high, by_t_low, x_way, t_way = stream_g
    small = plus(small[:, :part], small_got)
    small_half = small.shape[0] // 2
    small_kept = lax.dynamic_slice_in_dim(small, xi * small_half, small_half, 0)
    small_sent = lax.dynamic_slice_in_dim(small, (1 - xi) * small_half, small_half, 0)

    def near_rows(rows):
        return jnp.concatenate([rows[:share], swap(rows[share:], "x", "rows")], 0)

    x_way, t_way, small_got, small, out_near, in_near = step(
        swap(x_way, "x", "stream_g"), swap(t_way, "t", "stream_g"), swap(small_sent, "x", "small"),
        small_kept, near_rows(out_back), near_rows(in_back),
    )
    small = plus(small, small_got)
    if rings > 1:
        small = lax.psum(small.astype(F32), "r").astype(BF16)
    low_second, high_second, out_far, in_far, *gathered_small = step(
        swap(plus(by_t_low, x_way[0]), "t", "stream_g_sum"),
        swap(plus(by_x_high, t_way[0]), "x", "stream_g_sum"),
        swap(out_near, "t", "rows"), swap(in_near, "t", "rows"),
        *from_z([small] * zs, "small"),
    )
    stream_sum = jnp.concatenate(
        [plus(own_low, x_way[1], low_second), plus(own_high, t_way[1], high_second)], axis=1
    )
    stream_home = to_owners(stream_sum)
    small_near = jnp.concatenate(gathered_small, 0)
    small_near = jnp.concatenate([small_near, swap(small_near, "x", "small_all")], 0)

    back_place = send_place[:, None]
    if rings > 1:
        def own_rows(near, far, name):
            rows = whole(
                output_kernel, name, [xi], (back_place, near, far, jnp.zeros_like(tokens)),
                [shape(tokens.shape, BF16)],
            )[0]
            return dot(ring_order, from_blocks(over_rings(rows)), TN)

        output = (tokens.astype(F32) + own_rows(out_near, out_far, "output")).astype(BF16)
        rows = own_rows(in_near, in_far, "rows_back")
        own_x = tokens.astype(F32)
        inverse = lax.rsqrt(jnp.mean(own_x * own_x, axis=1, keepdims=True) + EPSILON)
        hat = own_x * inverse
        gain_rel = gain_row[:1].reshape(2, zs, 2, ring_rows)
        gain_abs = jnp.where(xi == 0, gain_rel, gain_rel[::-1]).transpose(1, 0, 2, 3)
        grad = rows * from_blocks(gain_abs.reshape(1, width))
        input_grad = cotangent.astype(F32) + inverse * (
            grad - hat * jnp.mean(grad * hat, axis=1, keepdims=True)
        )
    else:
        output = whole(
            output_kernel, "output", [xi], (back_place, out_near, out_far, tokens),
            [shape(tokens.shape, BF16)],
        )[0]
        input_grad = whole(
            input_kernel, "input_grad", [xi],
            (back_place, in_near, in_far, tokens, cotangent, gain_row),
            [shape(tokens.shape, F32)],
        )[0]
    one_row = shape((1, half_channels), F32)
    select_grad, step_w_grad, decay_grad, filter_grad, filter_b_grad, step_b_grad, skip_grad = whole(
        partial(small_kernel, (count, states, taps, zs)), "small", [zi, xi, ki],
        (small_near, swap(small_near, "k", "small")),
        [
            shape((count, half_channels), F32), shape((rank_width, half_channels), F32),
            shape((states, half_channels), F32), shape((taps, half_channels), F32),
            one_row, one_row, one_row,
        ],
    )
    late_home, stream_home, output, input_grad, select_grad = step(
        late_home, stream_home, output, input_grad, select_grad
    )
    gate_home, outer_home = late_home[:, :part], late_home[:, part:]
    outer_home = outer_home.reshape(half_channels, ring_rows).astype(F32)
    inner_home = jnp.stack(
        [v.reshape(half_channels, ring_rows).T for v in (stream_home, gate_home)], axis=1
    ).astype(F32)
    if rings > 1:
        outer_home = lax.psum_scatter(outer_home, "r", scatter_dimension=1, tiled=True)
        inner_home = lax.psum_scatter(inner_home, "r", scatter_dimension=0, tiled=True)
    gain_grad = jnp.sum(inner_home * inner_weight.astype(F32), axis=(1, 2))
    gain_grad = (gain_grad + swap(gain_grad, "t", "gain")) / norm_gain.astype(F32)
    return (
        output,
        input_grad,
        gain_grad,
        inner_home,
        filter_grad,
        filter_b_grad[0],
        select_grad.T,
        step_w_grad,
        step_b_grad[0],
        decay_grad,
        skip_grad[0],
        outer_home,
    )


def solution(mesh):
    devices = mesh.devices
    split = Mesh(
        devices.reshape(devices.shape[0] // 16, 4, 2, 2, devices.shape[1]), DP + ("t",)
    )
    in_specs = (
        P(DP, None), P(DP, None), P(), P(DP, None), P(DP), P(DP, None, "t"), P(None, "t"), P("t"),
        P("t", None), P(None, "t"), P("t"), P(None, "t"), P("t"), P("t", DP),
    )
    out_specs = (
        P(DP, None), P(DP, None), P(DP), P(DP, None, "t"), P(None, "t"), P("t"), P("t", None),
        P(None, "t"), P("t"), P(None, "t"), P("t"), P("t", DP),
    )
    return jax.shard_map(body, mesh=split, in_specs=in_specs, out_specs=out_specs, check_vma=False)
```

```python
from functools import partial
from inspect import isgeneratorfunction

import jax
import jax.numpy as jnp
from jax import lax
from jax.experimental import pallas as pl
from jax.experimental.pallas import tpu as pltpu
from jax.sharding import Mesh, PartitionSpec as P

MB = 2
EPSILON = 1e-05
ZK = ("z", "k")
DP = ("r", "z", "x", "k")
SWAP = [(0, 1), (1, 0)]
LOG2E = 1.4426950408889634
RESET_RATE = 1e30
LANES = 128
MICROSECONDS = {
    "pack": 3, "pack_cores": 3, "prep": 2, "front": 8, "late": 8, "mixer": 24, "out_rows": 5,
    "late_grad": 6, "back": 7, "in_rows": 7, "output": 3, "input_grad": 4, "small": 3,
    "rows_back": 3,
}
SUBLANES = 8
SIDE = 2
GROUP = 8
CHUNK = 64
UNROLL = 4
LOAD, STORE = 0, 1
F32 = jnp.float32
BF16 = jnp.bfloat16
NT = ((1,), (1,))
TN = ((0,), (0,))


def dot(lhs, rhs, contract=((1,), (0,))):
    return lax.dot_general(lhs, rhs, (contract, ((), ())), preferred_element_type=F32)


def split_dot(lhs, rhs, contract=((1,), (0,))):
    high = lhs.astype(BF16)
    rest = (lhs - high.astype(F32)).astype(BF16)
    return dot(high, rhs, contract) + dot(rest, rhs, contract)


def shape(dims, dtype):
    return jax.ShapeDtypeStruct(dims, dtype)


def whole(kernel, name, scalars, arrays, outs, scratch=()):
    scalars = [jnp.reshape(v, (1,)).astype(jnp.int32) for v in scalars]
    few, many, made = len(scalars), len(arrays), len(outs)

    def copied(*refs):
        inputs, refs_rest = refs[few : few + many], refs[few + many :]
        outputs, refs_rest = refs_rest[:made], refs_rest[made:]
        held, results = refs_rest[:many], refs_rest[many : many + made]
        *rest, semaphores = refs_rest[many + made :]
        loads = [
            pltpu.make_async_copy(source, target, semaphores.at[i])
            for i, (source, target) in enumerate(zip(inputs, held))
        ]
        stores = [
            pltpu.make_async_copy(source, target, semaphores.at[many + i])
            for i, (source, target) in enumerate(zip(results, outputs))
        ]
        for copy in loads:
            copy.start()
        asked = {LOAD: set(), STORE: set()}

        def ask(kind, numbers):
            for i in numbers:
                if i not in asked[kind]:
                    asked[kind].add(i)
                    loads[i].wait() if kind == LOAD else stores[i].start()

        lazy = isgeneratorfunction(getattr(kernel, "func", kernel))
        if not lazy:
            ask(LOAD, range(many))
        parts = kernel(*refs[:few], *held, *results, *rest)
        for kind, numbers in parts if lazy else ():
            ask(kind, numbers)
        ask(LOAD, range(many))
        ask(STORE, range(made))
        for copy in stores:
            copy.wait()

    return pl.pallas_call(
        copied,
        in_specs=[pl.BlockSpec(memory_space=pltpu.SMEM)] * few
        + [pl.BlockSpec(memory_space=pltpu.HBM)] * many,
        out_specs=[pl.BlockSpec(memory_space=pltpu.HBM)] * made,
        out_shape=list(outs),
        scratch_shapes=[
            *(pltpu.VMEM(v.shape, v.dtype) for v in (*arrays, *outs)),
            *scratch,
            pltpu.SemaphoreType.DMA((many + made,)),
        ],
        compiler_params=pltpu.CompilerParams(vmem_limit_bytes=60 << 20),
        cost_estimate=pl.CostEstimate(
            flops=0, bytes_accessed=MICROSECONDS[name] * 3690000, transcendentals=0
        ),
        name=name,
    )(*scalars, *arrays)


def row_matches(places, count):
    rows = lax.broadcasted_iota(jnp.int32, (count, places.shape[1]), 0)
    return (rows == places).astype(F32).astype(BF16)


def column_matches(places, count):
    columns = lax.broadcasted_iota(jnp.int32, (places.shape[0], count), 1)
    return (columns == places).astype(F32).astype(BF16)


def tiles(count, size):
    return [slice(i, i + size) for i in range(0, count, size)]


def prep_kernel(x_ref, place_ref, tok_ref, cot_ref, note_ref, tok_keep, tok_send, cot_keep, cot_send):
    share = tok_keep.shape[0]
    width = tok_ref.shape[1]
    half = width // 2
    order = row_matches(place_ref[...], 2 * share)
    for source, outs in ((tok_ref, (tok_keep, tok_send)), (cot_ref, (cot_keep, cot_send))):
        rows = dot(order, source[...])
        for side in (0, 1):
            part = rows[side * share : (side + 1) * share]
            for x in (0, 1):
                same = x_ref[0] == (x ^ side)
                for zk in range(half // LANES):
                    place = (zk // 2) * 4 + zk % 2
                    zero = part[:, place * LANES : (place + 1) * LANES]
                    one = part[:, (place + 2) * LANES : (place + 3) * LANES]
                    to = slice(x * half + zk * LANES, x * half + (zk + 1) * LANES)
                    outs[side][:, to] = jnp.where(same, zero, one).astype(BF16)
    tok_keep[:, width:] = note_ref[...]
    tok_send[:, width:] = note_ref[...]


def place_rows(x_ref, place_ref, near_ref, far_ref):
    share = near_ref.shape[0] // 2
    width = near_ref.shape[1]
    half = width // 2
    order = column_matches(place_ref[...], 4 * share)
    total = None
    for group in range(4):
        source = (near_ref, far_ref)[group // 2]
        rows = slice((group % 2) * share, (group % 2 + 1) * share)
        blocks = []
        for block in range(width // LANES):
            z, x, k = block // 4, (block // 2) % 2, block % 2
            same = x_ref[0] == (x ^ (group % 2))
            at = (z * 2 + k) * LANES
            first = source[rows, at : at + LANES].astype(F32)
            second = source[rows, half + at : half + at + LANES].astype(F32)
            blocks.append(jnp.where(same, first, second).astype(BF16))
        piece = dot(order[:, group * share : (group + 1) * share], jnp.concatenate(blocks, 1))
        total = piece if total is None else total + piece
    return total


def output_kernel(x_ref, place_ref, near_ref, far_ref, tok_ref, out_ref):
    rows = place_rows(x_ref, place_ref, near_ref, far_ref)
    out_ref[...] = (tok_ref[...].astype(F32) + rows).astype(BF16)


def input_kernel(x_ref, place_ref, near_ref, far_ref, tok_ref, cot_ref, gain_ref, out_ref):
    rows = place_rows(x_ref, place_ref, near_ref, far_ref)
    x = tok_ref[...].astype(F32)
    inverse = lax.rsqrt(jnp.mean(x * x, axis=1, keepdims=True) + EPSILON)
    hat = x * inverse
    half = gain_ref.shape[1] // 2
    gains = []
    for block in range(x.shape[1] // LANES):
        z, side, k = block // 4, (block // 2) % 2, block % 2
        at = (z * 2 + k) * LANES
        gains.append(
            jnp.where(
                x_ref[0] == side,
                gain_ref[0:1, at : at + LANES],
                gain_ref[0:1, half + at : half + at + LANES],
            )
        )
    grad = rows * jnp.concatenate(gains, 1)
    out_ref[...] = cot_ref[...].astype(F32) + inverse * (
        grad - hat * jnp.mean(grad * hat, axis=1, keepdims=True)
    )


def column_sum(rows_ref, pieces):
    own, by_x, by_t, *diagonal = pieces
    depth = own.shape[0]
    near, far = rows_ref[:, :depth], rows_ref[:, depth:]
    a = dot(near, own[...]) + dot(far, by_x[...])
    b = dot(near, by_t[...])
    for i, at in enumerate(tiles(depth, diagonal[0].shape[0])):
        b = b + dot(far[:, at], diagonal[i][...])
    return a, b


def z_block(z_ref, step, size):
    return lax.rem(z_ref[0] + (size - step), size)


def row_sum(z_ref, sides, out_refs):
    depth = sides[0][1][0].shape[0]
    rows = sides[0][0].shape[0] // 2
    block = 2 * LANES
    for base in range(0, 2 * depth, block):
        at = slice(base % depth, base % depth + block)
        value = None
        for lhs, (own, by_x, by_t, *diagonal) in sides:
            part = lhs.shape[1] // 2
            if base < depth:
                near, far = own[at, :], by_t[at, :]
            else:
                size = diagonal[0].shape[0]
                inner = slice(at.start % size, at.start % size + block)
                near, far = by_x[at, :], diagonal[at.start // size][inner, :]
            term = dot(lhs[:, :part], near, NT) + dot(lhs[:, part:], far, NT)
            value = term if value is None else value + term
        place = z_block(z_ref, at.start // block, depth // block) * block
        to = pl.ds(pl.multiple_of(base // depth * depth + place, block), block)
        for i, out in enumerate(out_refs):
            out[:, to] = value[i * rows : (i + 1) * rows].astype(BF16)


def reorder_rows(z_ref, order, source, out):
    block = 2 * LANES
    half = out.shape[1] // 2
    for base in range(0, 2 * half, block):
        step = base % half // block
        place = base // half * half + z_block(z_ref, step, half // block) * block
        at = pl.ds(pl.multiple_of(place, block), block)
        out[:, base : base + block] = dot(order, source[:, at]).astype(BF16)


def grad_pieces(z_ref, channels_t, rows_ref, outs):
    part = channels_t.shape[0] // 2
    depth = rows_ref.shape[1] // 2
    for at in tiles(2 * depth, 2 * LANES):
        value = dot(channels_t, rows_ref[:, at])
        near_out, far_out = (outs[0], outs[2]) if at.start < depth else (outs[1], outs[3])
        block = 2 * z_block(z_ref, (at.start % depth) // (2 * LANES), depth // (2 * LANES))
        for i in (0, 1):
            lanes = value[:, i * LANES : (i + 1) * LANES].astype(BF16)
            for refs, rows in ((near_out, lanes[:part]), (far_out, lanes[part:])):
                size = part // len(refs)
                for j, ref in enumerate(refs):
                    ref[block + i, :, :] = rows[j * size : (j + 1) * size]


def first_pack_kernel(z_ref, k_ref, stream, gate, outer, keep, send):
    count = keep.shape[0] // 3
    part = keep.shape[2]
    for i, source in enumerate((stream, gate, outer)):
        for step in range(count):
            z = lax.rem(z_ref[0] + step, count)
            for out, core in ((keep, k_ref[0]), (send, 1 - k_ref[0])):
                at = pl.ds(pl.multiple_of((z * 2 + core) * part, part), part)
                out[i * count + step] = source[:, at]


def second_pack_kernel(k_ref, kept, got, *outs):
    first = k_ref[0] == 0
    height = kept.shape[1]
    for i, out in enumerate(outs):
        mine, other = kept[i].astype(F32), got[i].astype(F32)
        out[:height, :] = jnp.where(first, mine, other).astype(BF16)
        out[height:, :] = jnp.where(first, other, mine).astype(BF16)


def down(value, count):
    if count == 0:
        return value
    return jnp.concatenate([jnp.zeros((count, value.shape[1]), value.dtype), value[:-count]], 0)


def up(value, count):
    if count == 0:
        return value
    return jnp.concatenate([value[count:], jnp.zeros((count, value.shape[1]), value.dtype)], 0)


def lag_masks(place, taps):
    return [None] + [place >= lag for lag in range(1, taps)]


def masked(value, mask):
    return value if mask is None else jnp.where(mask, value, 0.0)


def filter_sum(stream, masks, weights):
    taps = len(masks)
    total = weights[taps : taps + 1, :] + weights[taps - 1 : taps, :] * stream
    for lag in range(1, taps):
        total = total + weights[taps - 1 - lag : taps - lag, :] * masked(
            down(stream, SUBLANES * lag), masks[lag]
        )
    return total


def places(notes, rows, per_device):
    segments = len(notes) * MB
    zero = lax.broadcasted_iota(jnp.int32, (segments, LANES), 0) % MB
    lane = lax.broadcasted_iota(jnp.int32, (segments, LANES), 1)
    table = jnp.concatenate([v for v in notes for _ in range(MB)], 0)
    begin = jnp.zeros((segments, 1), F32)
    step = lax.broadcasted_iota(jnp.int32, (rows, LANES), 0) // segments
    step = step.astype(F32)
    latest = jnp.zeros((rows, LANES), F32)
    for i in range(per_device - 1):
        picked = jnp.where(lane == zero * per_device + i, table, 0.0)
        begin = begin + jnp.sum(picked, axis=1, keepdims=True)
        every = jnp.concatenate(
            [jnp.broadcast_to(begin, (segments, LANES))] * (rows // segments), 0
        )
        latest = jnp.where(every <= step, every, latest)
    return step - latest


def front_kernel(
    sizes, core_ref, tensor_ref, z_ref, x_ref, place_ref, own, by_x, by_t, low, high, par_ref, sel_ref,
    n_ref, stream_ref, act_ref, mine_ref, other_ref, pos_ref, gain_ref, nrm, act_low,
):
    yield LOAD, (0, 1)
    taps, per_device = sizes
    rows = x_ref.shape[0]
    width = n_ref.shape[1]
    depth = width // 2
    part = own.shape[1]
    members = depth // LANES
    share = rows // (2 * members)
    note = slice(width, width + LANES)
    for side in (0, 1):
        for member in range(members):
            row = member * 2 * share + side * share
            at = side * depth + member * LANES
            gain_ref[0:1, at : at + LANES] = x_ref[row : row + 16, note].astype(F32)[0:1]
    notes = []
    for z in range(members // 2):
        two = [
            x_ref[m * 2 * share : m * 2 * share + 16, note].astype(F32)[1:2]
            for m in (2 * z, 2 * z + 1)
        ]
        notes.append(jnp.where(tensor_ref[0] == 0, two[0], two[1]))
    place = places(notes, rows, per_device)
    pos_ref[...] = place

    def norm(i, _):
        at = pl.ds(pl.multiple_of(i * 64, 64), 64)
        x = x_ref[at, :width].astype(F32)
        inverse = lax.rsqrt(jnp.mean(x * x, axis=1, keepdims=True) + EPSILON)
        nrm[at, :] = (x * inverse * gain_ref[0:1, :]).astype(BF16)
        return 0

    lax.fori_loop(0, rows // 64, norm, 0)
    reorder_rows(z_ref, row_matches(place_ref[...], rows), nrm, n_ref)
    yield STORE, (0, 5, 6)
    yield LOAD, (2, 3, 4, 5, 6)
    near, far = column_sum(n_ref, (own, by_x, by_t, low, high))
    stream_ref[:, :part] = near
    stream_ref[:, part:] = far
    yield STORE, (1,)
    yield LOAD, (7, 8)
    masks = lag_masks(place, taps)
    for at in tiles(2 * part, LANES):
        filtered = filter_sum(stream_ref[:, at], masks, par_ref[:, at])
        act = filtered * jax.nn.sigmoid(filtered)
        act_ref[:, at] = act
        act_low[:, at] = act.astype(BF16)
    yield STORE, (2,)
    selected = dot(sel_ref[...], act_low[...], NT)
    first = core_ref[0] == 0
    mine_ref[...] = jnp.where(first, selected[:, : rows // 2], selected[:, rows // 2 :])
    other_ref[...] = jnp.where(first, selected[:, rows // 2 :], selected[:, : rows // 2])


def late_kernel(z_ref, cot_ref, place_ref, n_ref, *refs):
    gate_pieces, out_pieces = refs[:4], refs[4:8]
    up_ref, gate_ref, gg_ref = refs[8:]
    part = gate_pieces[0].shape[1]
    yield LOAD, (0, 1)
    reorder_rows(z_ref, row_matches(place_ref[...], cot_ref.shape[0]), cot_ref, up_ref)
    yield STORE, (0,)
    for i, (source, out, pieces) in enumerate(
        ((n_ref, gate_ref, gate_pieces), (up_ref, gg_ref, out_pieces))
    ):
        yield LOAD, (2, *range(3 + 4 * i, 7 + 4 * i))
        near, far = column_sum(source, pieces)
        out[:, :part] = near
        out[:, part:] = far
        yield STORE, (1 + i,)


def out_kernel(z_ref, place_ref, gated_ref, *refs):
    yield LOAD, (0, 1)
    order = row_matches(place_ref[...], gated_ref.shape[0])
    rows = dot(order, gated_ref[...], TN).astype(BF16)
    yield LOAD, (2, 3, 4, 5)
    row_sum(z_ref, [(rows, refs[:4])], refs[4:])


def late_grad_kernel(z_ref, n_ref, up_ref, gate_grad_ref, gated_ref, *outs):
    gate_own, gate_t, outer_own, outer_x, x_way, t_way = outs
    for source, rows_ref, pieces, needs, ends in (
        (gate_grad_ref, n_ref, (gate_own, x_way.at[1], gate_t, x_way.at[0]), (2, 0), (4, 1, 0)),
        (gated_ref, up_ref, (outer_own, outer_x, t_way.at[1], t_way.at[0]), (3, 1), (5, 3, 2)),
    ):
        yield LOAD, needs[:1]
        channels_t = source[...].astype(F32).T.astype(BF16)
        yield LOAD, needs[1:]
        grad_pieces(z_ref, channels_t, rows_ref, [[v] for v in pieces])
        yield STORE, ends


def back_kernel(
    taps, core_ref, z_ref, total_ref, rest_ref, pos_ref, stream_ref, sact_ref, par_ref, sel_ref, n_ref,
    low_ref, small_ref, *refs,
):
    *outs, act_low, grad_t = refs
    yield LOAD, (0, 1, 2, 3, 4, 5, 6)
    rows, channels = stream_ref.shape
    first = core_ref[0] == 0
    total, rest = total_ref[...], rest_ref[...]
    selected_t = jnp.concatenate(
        [jnp.where(first, total, rest), jnp.where(first, rest, total)], 1
    )
    selected_low = selected_t.astype(BF16)
    count = selected_t.shape[0]
    padded = jnp.concatenate(
        [selected_t, jnp.zeros((-count % LANES, rows), F32)], 0
    )
    selected = padded.T.astype(BF16)
    masks = lag_masks(pos_ref[...], taps)
    spare = jnp.zeros((SUBLANES - taps - 1, LANES), F32)
    for at in tiles(channels, LANES):
        stream = stream_ref[:, at]
        weights = par_ref[:, at]
        filtered = filter_sum(stream, masks, weights)
        slope = jax.nn.sigmoid(filtered)
        act_low[:, at] = (filtered * slope).astype(BF16)
        select = jnp.concatenate(
            [sel_ref[:, at], jnp.zeros((-count % LANES, LANES), BF16)], 0
        )
        act_grad = sact_ref[:, at] + dot(selected, select)
        grad = act_grad * (slope * (1.0 + filtered * (1.0 - slope)))
        stream_grad = weights[taps - 1 : taps, :] * grad
        sums = [jnp.sum(grad * stream, axis=0, keepdims=True)]
        for lag in range(1, taps):
            part_grad = masked(grad, masks[lag])
            sums.append(
                jnp.sum(part_grad * down(stream, SUBLANES * lag), axis=0, keepdims=True)
            )
            stream_grad = stream_grad + weights[taps - 1 - lag : taps - lag, :] * up(
                part_grad, SUBLANES * lag
            )
        sums = sums[::-1] + [jnp.sum(grad, axis=0, keepdims=True), spare]
        small_ref[count:, at] = jnp.concatenate(sums, 0).astype(BF16)
        low_ref[:, at] = stream_grad.astype(BF16)
        grad_t[at, :] = stream_grad.T.astype(BF16)
    yield STORE, (0,)
    small_ref[:count, :] = dot(selected_low, act_low[...]).astype(BF16)
    yield STORE, (1,)
    yield LOAD, (7,)
    own_low, own_high, by_x_high, by_t_low, x_way, t_way = outs
    grad_pieces(
        z_ref, grad_t[...], n_ref,
        [
            (own_low, own_high), (x_way.at[1], by_x_high),
            (by_t_low, t_way.at[1]), (x_way.at[0], t_way.at[0]),
        ],
    )


def in_kernel(z_ref, place_ref, low_ref, gate_grad_ref, *refs):
    stream_pieces, gate_pieces, outs, stage = refs[:5], refs[5:9], refs[9:11], refs[11]
    channels = low_ref.shape[1]
    yield LOAD, (0, 1, 2)
    order = row_matches(place_ref[...], low_ref.shape[0])
    stage[:, :channels] = dot(order, low_ref[...], TN).astype(BF16)
    stage[:, channels:] = dot(order, gate_grad_ref[...], TN).astype(BF16)
    yield LOAD, range(3, 12)
    row_sum(
        z_ref, [(stage[:, :channels], stream_pieces), (stage[:, channels:], gate_pieces)], outs
    )


def small_kernel(sizes, z_ref, x_ref, k_ref, mine, other, *outs):
    count, states, taps, zs = sizes
    select, step_w, decay, filters, filter_b, step_b, skip = outs
    part = mine.shape[1]
    rank = step_w.shape[0]
    half = mine.shape[0] // (2 * zs)
    first_x = x_ref[0] == 0
    for source, core in ((mine, k_ref[0]), (other, 1 - k_ref[0])):
        for shift in range(zs):
            near = source[shift * half : (shift + 1) * half, :].astype(F32)
            far = source[(zs + shift) * half : (zs + shift + 1) * half, :].astype(F32)
            block = jnp.concatenate(
                [jnp.where(first_x, near, far), jnp.where(first_x, far, near)], 0
            )
            place = (z_block(z_ref, shift, zs) * 2 + core) * part
            at = pl.ds(pl.multiple_of(place, part), part)
            step_b[:, at] = block[0:1]
            skip[:, at] = block[1:2]
            decay[:, at] = block[8 : states + 8]
            step_w[:, at] = block[states + 8 : states + 8 + rank]
            rest = block[states + 8 + rank :]
            filters[:, at] = rest[count : count + taps]
            filter_b[:, at] = rest[count + taps : count + taps + 1]
            select[:, at] = rest[:count]


def scan_kernel(
    layout, core_ref, pos_ref, act_ref, gate_ref, gg_ref, total_ref, rest_ref, sw_ref, par_ref,
    gated_ref, gateg_ref, sact_ref, small_ref, mine_ref, other_ref,
    bb, cb, hist, fac, ci_acc, co_acc, rate_s, reff_s, u_s, ds_s, y_s, s2_s, slope_s, spre_low, decb, sel_t, rate_low, rank_t,
):
    rank_width, states, bias_row, decay_row, skip_row = layout
    rows, channels = act_ref.shape
    lanes = LANES
    steps = rows // SUBLANES
    wide = states * lanes
    first = core_ref[0] == 0
    spread = (
        lax.broadcasted_iota(jnp.int32, (states, wide), 1) // lanes
        == lax.broadcasted_iota(jnp.int32, (states, wide), 0)
    ).astype(F32).astype(BF16)
    yield LOAD, (4, 5)
    total, rest = total_ref[...], rest_ref[...]
    sel_t[:, : rows // 2] = jnp.where(first, total, rest)
    sel_t[:, rows // 2 :] = jnp.where(first, rest, total)
    rate_low[...] = sel_t[:rank_width, :].T.astype(BF16)
    twice = jnp.concatenate([spread, spread], 0)
    for out, base in ((bb, rank_width), (cb, rank_width + states)):
        value = sel_t[base : base + states, :]
        high = value.astype(BF16).astype(F32)
        parts = jnp.concatenate([high, value - high], 0).astype(BF16)
        out[...] = dot(parts, twice, TN)
    hist[0:SUBLANES, :] = jnp.zeros((SUBLANES, SIDE * wide), F32)
    ci_acc[...] = jnp.zeros_like(ci_acc)
    co_acc[...] = jnp.zeros_like(co_acc)
    rank_t[...] = jnp.zeros_like(rank_t)
    zero = jnp.zeros((8, lanes), F32)
    sides = range(SIDE)
    both = SIDE * lanes

    def cols(n):
        return slice(n * lanes, (n + 1) * lanes)

    def wide_cols(n, side):
        return slice((n * SIDE + side) * lanes, (n * SIDE + side + 1) * lanes)

    def side_cols(side):
        return slice(side * lanes, (side + 1) * lanes)

    def one_block(block, _):
        at = pl.ds(pl.multiple_of(block * both, both), both)
        decay = -jnp.exp(par_ref[decay_row : decay_row + states, at])
        for n in range(states):
            decb[8 * n : 8 * n + 8, :] = jnp.broadcast_to(decay[n : n + 1, :], (8, both))
        rate_s[...] = dot(rate_low[...], sw_ref[:, at]) + par_ref[bias_row : bias_row + 1, at]

        def before(i, _):
            row = pl.ds(pl.multiple_of(i * CHUNK, CHUNK), CHUNK)
            step_pre = rate_s[row, :]
            small = jnp.exp(-jnp.abs(step_pre))
            rate = jnp.maximum(step_pre, 0.0) + jnp.log1p(small)
            inverse = 1.0 / (1.0 + small)
            slope_s[row, :] = jnp.where(step_pre >= 0.0, inverse, small * inverse)
            rate_s[row, :] = rate
            keep = pos_ref[row, :] > 0.0
            for side in sides:
                reff_s[row, side_cols(side)] = jnp.where(
                    keep, rate[:, side_cols(side)] * LOG2E, RESET_RATE
                )
            u_s[row, :] = rate * act_ref[row, at]
            gate = gate_ref[row, at]
            ds_s[row, :] = gg_ref[row, at] * (gate * jax.nn.sigmoid(gate))
            return 0

        lax.fori_loop(0, rows // CHUNK, before, 0)

        for group in range(states // GROUP):
            names = range(group * GROUP, (group + 1) * GROUP)

            def forward(t, h, names=names, group=group):
                row = pl.ds(pl.multiple_of(t * 8, 8), 8)
                next_row = pl.ds(pl.multiple_of(t * 8 + 8, 8), 8)
                reff = [reff_s[row, side_cols(i)] for i in sides]
                u = [u_s[row, side_cols(i)] for i in sides]
                ds = [ds_s[row, side_cols(i)] for i in sides]
                y = [zero if group == 0 else y_s[row, side_cols(i)] for i in sides]
                fresh = []
                for n in names:
                    b, c = bb[row, cols(n)], cb[row, cols(n)]
                    out = co_acc[row, cols(n)]
                    for i in sides:
                        a = jnp.exp2(reff[i] * decb[8 * n : 8 * n + 8, side_cols(i)])
                        hn = a * h[len(fresh)] + b * u[i]
                        hist[next_row, wide_cols(n, i)] = hn
                        fac[row, wide_cols(n, i)] = a
                        y[i] = y[i] + c * hn
                        out = out + ds[i] * hn
                        fresh.append(hn)
                    co_acc[row, cols(n)] = out
                for i in sides:
                    y_s[row, side_cols(i)] = y[i]
                return tuple(fresh)

            lax.fori_loop(0, steps, forward, (zero,) * (GROUP * SIDE), unroll=UNROLL)

        skip = par_ref[skip_row : skip_row + 1, at]

        def between(i, _):
            row = pl.ds(pl.multiple_of(i * CHUNK, CHUNK), CHUNK)
            scanned = y_s[row, :] + skip * act_ref[row, at]
            gate = gate_ref[row, at]
            sig = jax.nn.sigmoid(gate)
            gated_ref[row, at] = (scanned * (gate * sig)).astype(BF16)
            gateg_ref[row, at] = (
                gg_ref[row, at] * scanned * (sig * (1.0 + gate * (1.0 - sig)))
            ).astype(BF16)
            return 0

        lax.fori_loop(0, rows // CHUNK, between, 0)

        sums = []
        for group in range(states // GROUP):
            names = range(group * GROUP, (group + 1) * GROUP)

            def backward(i, carried, names=names, group=group):
                g, dacc = carried
                t = steps - 1 - i
                row = pl.ds(pl.multiple_of(t * 8, 8), 8)
                ds = [ds_s[row, side_cols(k)] for k in sides]
                u = [u_s[row, side_cols(k)] for k in sides]
                rt = [rate_s[row, side_cols(k)] for k in sides]
                s1 = [zero if group == 0 else reff_s[row, side_cols(k)] for k in sides]
                s2 = [zero if group == 0 else s2_s[row, side_cols(k)] for k in sides]
                g_new, d_new = [], []
                for n in names:
                    b, c = bb[row, cols(n)], cb[row, cols(n)]
                    out = ci_acc[row, cols(n)]
                    for k in sides:
                        lam = c * ds[k] + g[len(g_new)]
                        q = lam * fac[row, wide_cols(n, k)]
                        hp = hist[row, wide_cols(n, k)] * q
                        s1[k] = s1[k] + hp * decb[8 * n : 8 * n + 8, side_cols(k)]
                        s2[k] = s2[k] + lam * b
                        out = out + lam * u[k]
                        d_new.append(dacc[len(g_new)] + hp * rt[k])
                        g_new.append(q)
                    ci_acc[row, cols(n)] = out
                for k in sides:
                    s2_s[row, side_cols(k)] = s2[k]
                    reff_s[row, side_cols(k)] = s1[k]
                return tuple(g_new), tuple(d_new)

            none = (zero,) * (GROUP * SIDE)
            _, dacc = lax.fori_loop(0, steps, backward, (none, none), unroll=UNROLL)
            for n in range(GROUP):
                row = jnp.concatenate(
                    [jnp.sum(dacc[n * SIDE + k], axis=0, keepdims=True) for k in sides], 1
                )
                name = group * GROUP + n
                sums.append(row * decb[8 * name : 8 * name + 1, :])

        def behind(i, carried):
            row = pl.ds(pl.multiple_of(i * CHUNK, CHUNK), CHUNK)
            act, dscan, s2_all = act_ref[row, at], ds_s[row, :], s2_s[row, :]
            sact_ref[row, at] = rate_s[row, :] * s2_all + skip * dscan
            spre = (reff_s[row, :] + act * s2_all) * slope_s[row, :]
            spre_low[row, :] = spre.astype(BF16)
            totals = []
            for total, value in zip(carried, (spre, dscan * act)):
                for j in range(CHUNK // SUBLANES):
                    total = total + value[j * SUBLANES : (j + 1) * SUBLANES]
                totals.append(total)
            return tuple(totals)

        empty = jnp.zeros((SUBLANES, both), F32)
        head = [
            jnp.sum(v, axis=0, keepdims=True)
            for v in lax.fori_loop(0, rows // CHUNK, behind, (empty, empty))
        ]
        head.append(jnp.zeros((6, both), F32))
        small_ref[: states + 8, at] = jnp.concatenate(head + sums, 0).astype(BF16)
        small_ref[states + 8 :, at] = dot(
            sel_t[:rank_width, :].astype(BF16), spre_low[...]
        ).astype(BF16)
        rank_t[...] += dot(sw_ref[:, at], spre_low[...], NT)
        return 0

    yield LOAD, (0, 1, 2, 3, 6, 7)
    lax.fori_loop(0, channels // both, one_block, 0)
    yield STORE, (0, 1, 2, 3)
    high, low = slice(0, rows // 2), slice(rows // 2, rows)
    for acc, base in ((ci_acc, rank_width), (co_acc, rank_width + states)):
        sel_t[base : base + states, :] = dot(acc[...].astype(BF16), spread, NT).T
    sel_t[:rank_width, :] = rank_t[...]
    mine_ref[...] = jnp.where(first, sel_t[:, high], sel_t[:, low])
    other_ref[...] = jnp.where(first, sel_t[:, low], sel_t[:, high])


def mixer(layout, core, position, act, gate, gated_grad, total, rest, step_w, params):
    rows, channels = act.shape
    rank_width, states = layout[:2]
    count = total.shape[0]
    wide = states * LANES
    return whole(
        partial(scan_kernel, layout), "mixer", [core],
        (position, act, gate, gated_grad, total, rest, step_w, params),
        [
            shape((rows, channels), BF16), shape((rows, channels), BF16),
            shape((rows, channels), F32), shape((rank_width + states + 8, channels), BF16),
            shape((count, rows // 2), F32), shape((count, rows // 2), F32),
        ],
        [
            pltpu.VMEM((rows, wide), F32), pltpu.VMEM((rows, wide), F32),
            pltpu.VMEM((rows + 8, SIDE * wide), F32), pltpu.VMEM((rows, SIDE * wide), F32),
            pltpu.VMEM((rows, wide), F32), pltpu.VMEM((rows, wide), F32),
        ]
        + [pltpu.VMEM((rows, SIDE * LANES), F32)] * 7
        + [
            pltpu.VMEM((rows, SIDE * LANES), BF16),
            pltpu.VMEM((8 * states, SIDE * LANES), F32), pltpu.VMEM((count, rows), F32),
            pltpu.VMEM((rows, rank_width), BF16), pltpu.VMEM((rank_width, rows), F32),
        ],
    )


def step(*values):
    return lax.optimization_barrier(values)


def swap(value, axis, name="swap"):
    with jax.named_scope(f"{name}_{axis}"):
        return lax.ppermute(value, axis, SWAP)


def exchange_z(value, distance, name):
    size = lax.axis_size("z")
    with jax.named_scope(f"{name}_z"):
        return lax.ppermute(value, "z", [(i, i ^ distance) for i in range(size)])


def from_z(blocks, name):
    size = lax.axis_size("z")
    got = [blocks[0]]
    for shift in range(1, size):
        with jax.named_scope(f"{name}_z"):
            got.append(
                lax.ppermute(blocks[shift], "z", [(i, (i + shift) % size) for i in range(size)])
            )
    return got


def plus(value, *more):
    total = value.astype(F32)
    for v in more:
        total = total + v.astype(F32)
    return total.astype(BF16)


def to_owners(value):
    return lax.all_to_all(value, ZK, 0, 0, tiled=True)


def rank_in_class(keys):
    count = keys.shape[1]
    earlier = jnp.arange(count)[:, None] > jnp.arange(count)[None, :]
    same = (keys[:, :, None] == keys[:, None, :]) & earlier[None]
    return jnp.sum(same.astype(jnp.int32), axis=2)


def body(
    tokens, cotangent, owner_slot, sequence_lengths, norm_gain, inner_weight, filter_weight,
    convolution_bias, select_weight, step_weight, step_bias, decay_log, skip_weight, output_weight,
):
    rings = lax.axis_size("r")
    zs = lax.axis_size("z")
    members = zs * 4
    ri, zi, xi, ki, ti = (lax.axis_index(a) for a in ("r", "z", "x", "k", "t"))
    local_rows, width = tokens.shape
    rank_width = step_weight.shape[0]
    states = decay_log.shape[0]
    taps = filter_weight.shape[0]
    half_channels = inner_weight.shape[2]
    part = half_channels // (2 * zs)
    channels = 2 * part
    block_rows = inner_weight.shape[0]
    ring_rows = rings * block_rows
    depth = width // 2
    batch_rows = local_rows // MB
    group_rows = zs * local_rows
    segments = group_rows // batch_rows
    share = local_rows // 4

    def to_blocks(value):
        if rings == 1:
            return value
        value = value.reshape(-1, rings, members, block_rows)
        return value.transpose(0, 2, 1, 3).reshape(-1, width)

    def from_blocks(value):
        if rings == 1:
            return value
        value = value.reshape(-1, members, rings, block_rows)
        return value.transpose(0, 2, 1, 3).reshape(-1, width)

    inner = inner_weight
    outer = output_weight.T
    gain = norm_gain[None, :]
    if rings > 1:
        inner = lax.all_gather(inner, "r", axis=0, tiled=True)
        outer = lax.all_gather(outer, "r", axis=0, tiled=True)
        gain = lax.all_gather(gain, "r", axis=1, tiled=True)

    blocks_w = 3 * zs
    kept, sent = whole(
        first_pack_kernel, "pack", [zi, ki], (inner[:, 0], inner[:, 1], outer),
        [shape((blocks_w, ring_rows, part), BF16)] * 2,
    )

    slot_rows = owner_slot.reshape(rings, members, local_rows)
    tok, cot = tokens, cotangent
    ring_block = members * local_rows
    if rings > 1:
        per_ring = local_rows // rings
        flat = slot_rows.reshape(rings * members, local_rows)
        target = flat // ring_block
        place = target * per_ring + rank_in_class(target)
        chosen = jnp.arange(local_rows, dtype=jnp.int32)[None, :, None] == place[:, None, :]
        ordered = jnp.sum(jnp.where(chosen, flat[:, None, :], 0), axis=2)
        ordered = ordered.reshape(rings, members, rings, per_ring)
        ordered = lax.dynamic_index_in_dim(ordered, ri, 2, keepdims=False)
        slots = ordered.transpose(1, 0, 2).reshape(members, local_rows)
        own_place = lax.dynamic_index_in_dim(place, ri * members + zi * 4 + xi * 2 + ki, 0, False)
        ring_order = (
            jnp.arange(local_rows, dtype=jnp.int32)[:, None] == own_place[None, :]
        ).astype(BF16)

        def over_rings(value):
            value = value.reshape(rings, per_ring, width)
            return lax.all_to_all(value, "r", 0, 0, tiled=True).reshape(local_rows, width)

        tok, cot = (over_rings(dot(ring_order, v).astype(BF16)) for v in (tokens, cotangent))
    else:
        slots = slot_rows[0]
    local_slot = slots - ri * ring_block
    owner = local_slot // local_rows
    owner_z, owner_x, owner_k = owner // 4, (owner // 2) % 2, owner % 2
    rank = rank_in_class(owner_x * 2 + owner_k)
    in_owner = local_slot % local_rows
    scan_place = (in_owner % batch_rows) * segments + owner_z * MB + in_owner // batch_rows
    here = zi * 4 + xi * 2 + ki
    mine = [lax.dynamic_index_in_dim(v, here, 0, False) for v in (owner_x, owner_k, rank)]
    send_place = (mine[1] ^ ti) * (2 * share) + (mine[0] ^ xi) * share + mine[2]
    in_group = (owner_x == xi) & (owner_k == ti)
    ranked = (
        jnp.arange(share, dtype=jnp.int32)[None, :, None] == rank[:, None, :]
    ) & in_group[:, None, :]
    arrival = jnp.sum(jnp.where(ranked, scan_place[:, None, :], 0), axis=2)
    arrival = arrival.reshape(zs, 2, 2, share)
    arrival = jnp.where(xi == 0, arrival, arrival[:, ::-1]).transpose(0, 2, 1, 3)
    arrived = arrival.reshape(1, group_rows)
    returned = jnp.where(ki == 0, arrival, arrival[:, ::-1]).transpose(1, 0, 2, 3)
    returned = returned.reshape(1, group_rows)

    blocks = [to_blocks(tok), to_blocks(cot)]
    lengths = sequence_lengths.reshape(1, -1).astype(BF16)
    lengths = jnp.concatenate([lengths, jnp.zeros((1, ring_rows - lengths.shape[1]), BF16)], 1)
    note = jnp.concatenate([gain, lengths, jnp.zeros((share - 2, ring_rows), BF16)], 0)
    noted, plain = shape((share, width + LANES), BF16), shape((share, width), BF16)
    first = (zi * 2 + ki) * part

    def own_channels(value):
        return lax.dynamic_slice_in_dim(value, first, part, 1)

    rows_f = taps + 3 + states
    floats = own_channels(
        jnp.concatenate(
            [
                filter_weight, convolution_bias[None], step_bias[None], decay_log,
                skip_weight[None], jnp.zeros((-rows_f % 8, half_channels), F32),
            ],
            axis=0,
        )
    )
    layout = (rank_width, states, taps + 1, taps + 2, taps + 2 + states)
    select_t = lax.dynamic_slice_in_dim(select_weight, first, part, 0).T
    lows = jnp.concatenate([own_channels(step_weight), select_t], 0)
    count = select_t.shape[0]
    half_out = [shape((count, group_rows // 2), F32)] * 2
    half_rows = [shape((group_rows // 2, width), BF16)] * 2
    full = shape((group_rows, channels), F32)
    wide_low = shape((group_rows, width), BF16)
    half = depth // 2

    def gathered(keep, send):
        return lax.all_gather(jnp.concatenate([keep, send], 0), ZK, axis=0, tiled=True)

    (other_core,) = step(swap(sent, "k", "weights"))
    packed = whole(
        second_pack_kernel, "pack_cores", [ki], (kept, other_core),
        [shape((2 * ring_rows, part), BF16)] * blocks_w,
    )
    *packed, tok, cot = step(*packed, *blocks)
    tok_keep, tok_send, cot_keep, cot_send = whole(
        prep_kernel, "prep", [xi], (send_place[None], tok, cot, note), [noted, noted, plain, plain]
    )
    stream_own, floats_t, lows_t, tok_keep, tok_send, cot_keep, cot_send, *packed = step(
        jnp.concatenate(from_z(packed[:zs], "stream_w"), 0),
        swap(floats, "t", "params"), swap(lows, "t", "params_low"),
        tok_keep, tok_send, cot_keep, cot_send, *packed[zs:],
    )
    tok_got, stream_own = step(swap(tok_send, "x", "tokens"), stream_own)
    group_tokens = gathered(tok_keep, tok_got)
    params = jnp.concatenate([floats, floats_t], axis=1)
    lows = jnp.concatenate([lows, lows_t], axis=1)
    stream_x, stream_t, gate_own, params, step_w, select_w, arrived, returned, cot_got, *packed = step(
        swap(stream_own, "x", "stream_w"), swap(stream_own, "t", "stream_w"),
        jnp.concatenate(from_z(packed[:zs], "gate_w"), 0), params, lows[:rank_width],
        lows[rank_width:], arrived, returned, swap(cot_send, "x", "cot"), *packed[zs:],
    )
    group_cot = gathered(cot_keep, cot_got)
    stream_low, stream_high, outer_own, gate_own, group_tokens = step(
        swap(stream_x[:half], "t", "stream_w_far"), swap(stream_t[half:], "x", "stream_w_far"),
        jnp.concatenate(from_z(packed, "outer_w"), 0), gate_own, group_tokens,
    )
    ws = (stream_own, stream_x, stream_t, stream_low, stream_high)
    normed, stream, act, sel_mine, sel_other, position, gain_row = whole(
        partial(front_kernel, (taps, sequence_lengths.shape[1])), "front", [ki, ti, zi],
        (group_tokens, arrived, *ws, params, select_w),
        [wide_low, full, full, *half_out, shape((group_rows, LANES), F32), shape((8, width), F32)],
        [pltpu.VMEM((group_rows, width), BF16), pltpu.VMEM((group_rows, channels), BF16)],
    )
    normed, stream, act, sel_mine, sel_other, gate_x, outer_t = step(
        normed, stream, act, sel_mine, sel_other,
        swap(gate_own, "x", "gate_w"), swap(outer_own, "t", "outer_w"),
    )
    sent = (sel_mine + swap(sel_other, "k", "select")).astype(BF16)
    got, gate_t, outer_x, sent = step(
        exchange_z(sent, 1, "select"), swap(gate_own, "t", "gate_w"),
        swap(outer_own, "x", "outer_w"), sent,
    )
    sent = plus(sent, got)
    got, gate_d, outer_d, sent = step(
        exchange_z(sent, 2, "select"), swap(gate_x, "t", "gate_w_far"),
        swap(outer_t, "x", "outer_w_far"), sent,
    )
    total = sent.astype(F32) + got.astype(F32)
    wg, wo = (gate_own, gate_x, gate_t, gate_d), (outer_own, outer_x, outer_t, outer_d)
    upstream, gate, gated_grad = whole(
        late_kernel, "late", [zi], (group_cot, arrived, normed, *wg, *wo), [wide_low, full, full],
    )
    rest = swap(total, "k", "select_rest")
    gated, gate_grad, act_grad, small_a, sel_mine, sel_other = mixer(
        layout, ki, position, act, gate, gated_grad, total, rest, step_w, params
    )

    out_mine, out_other = whole(
        out_kernel, "out_rows", [zi], (returned, gated, *wo), half_rows,
    )
    got, out_mine, out_other, gated, gate_grad = step(
        swap(sel_other, "k", "select"), out_mine, out_other, gated, gate_grad
    )
    sent = (sel_mine + got).astype(BF16)
    pieces = whole(
        late_grad_kernel, "late_grad", [zi], (normed, upstream, gate_grad, gated),
        [shape((2 * zs, part, ring_rows), BF16)] * 4
        + [shape((2, 2 * zs, part, ring_rows), BF16)] * 2,
    )
    got, out_got, sent, *pieces = step(
        exchange_z(sent, 1, "select"), swap(out_other, "k", "rows"), sent, *pieces
    )
    out_total = plus(out_mine, out_got)
    sent = plus(sent, got)
    got, sent, out_total, *pieces = step(
        exchange_z(sent, 2, "select"), sent, out_total, *pieces
    )
    out_back = lax.psum_scatter(out_total, "z", scatter_dimension=0, tiled=True)
    total = sent.astype(F32) + got.astype(F32)
    rest = swap(total, "k", "select_rest")
    low, small_b, *stream_g = whole(
        partial(back_kernel, taps), "back", [ki, zi],
        (total, rest, position, stream, act_grad, params, select_w, normed),
        [shape((group_rows, channels), BF16), shape((count + 8, channels), BF16)]
        + [shape((2 * zs, part // 2, ring_rows), BF16)] * 4
        + [shape((2, 2 * zs, part // 2, ring_rows), BF16)] * 2,
        [pltpu.VMEM((group_rows, channels), BF16), pltpu.VMEM((channels, group_rows), BF16)],
    )
    gate_own_g, gate_t_g, outer_own_g, outer_x_g, x_way_l, t_way_l = pieces
    in_mine, in_other = whole(
        in_kernel, "in_rows", [zi], (returned, low, gate_grad, *ws, *wg),
        half_rows, [pltpu.VMEM((group_rows, 2 * channels), BF16)],
    )
    x_way_l, t_way_l, in_mine, in_other, out_back, small_b, *stream_g = step(
        swap(x_way_l, "x", "late_g"), swap(t_way_l, "t", "late_g"), in_mine, in_other, out_back,
        small_b, *stream_g,
    )
    in_total = plus(in_mine, swap(in_other, "k", "rows"))
    in_back = lax.psum_scatter(in_total, "z", scatter_dimension=0, tiled=True)
    small = jnp.concatenate([small_a, small_b], axis=0)
    gate_second, outer_second, small_got, small, *stream_g = step(
        swap(plus(gate_t_g, x_way_l[0]), "t", "gate_g_sum"),
        swap(plus(outer_x_g, t_way_l[0]), "x", "outer_g_sum"),
        swap(small[:, part:], "t", "small"), small, *stream_g,
    )
    late_sum = jnp.concatenate(
        [plus(gate_own_g, x_way_l[1], gate_second), plus(outer_own_g, t_way_l[1], outer_second)],
        axis=1,
    )
    late_home = to_owners(late_sum)
    own_low, own_high, by_x_high, by_t_low, x_way, t_way = stream_g
    small = plus(small[:, :part], small_got)
    small_half = small.shape[0] // 2
    small_kept = lax.dynamic_slice_in_dim(small, xi * small_half, small_half, 0)
    small_sent = lax.dynamic_slice_in_dim(small, (1 - xi) * small_half, small_half, 0)

    def near_rows(rows):
        return jnp.concatenate([rows[:share], swap(rows[share:], "x", "rows")], 0)

    x_way, t_way, small_got, small, out_near, in_near = step(
        swap(x_way, "x", "stream_g"), swap(t_way, "t", "stream_g"), swap(small_sent, "x", "small"),
        small_kept, near_rows(out_back), near_rows(in_back),
    )
    small = plus(small, small_got)
    if rings > 1:
        small = lax.psum(small.astype(F32), "r").astype(BF16)
    low_second, high_second, out_near, in_near, *gathered_small = step(
        swap(plus(by_t_low, x_way[0]), "t", "stream_g_sum"),
        swap(plus(by_x_high, t_way[0]), "x", "stream_g_sum"),
        out_near, in_near, *from_z([small] * zs, "small"),
    )
    stream_sum = jnp.concatenate(
        [plus(own_low, x_way[1], low_second), plus(own_high, t_way[1], high_second)], axis=1
    )
    stream_sum, out_far, in_near = step(stream_sum, swap(out_near, "t", "rows"), in_near)
    stream_home = to_owners(stream_sum)
    in_far = swap(in_near, "t", "rows")
    small_near = jnp.concatenate(gathered_small, 0)
    small_near = jnp.concatenate([small_near, swap(small_near, "x", "small_all")], 0)

    one_row = shape((1, half_channels), F32)
    select_grad, step_w_grad, decay_grad, filter_grad, filter_b_grad, step_b_grad, skip_grad = whole(
        partial(small_kernel, (count, states, taps, zs)), "small", [zi, xi, ki],
        (small_near, swap(small_near, "k", "small")),
        [
            shape((count, half_channels), F32), shape((rank_width, half_channels), F32),
            shape((states, half_channels), F32), shape((taps, half_channels), F32),
            one_row, one_row, one_row,
        ],
    )
    in_far, select_grad = step(in_far, select_grad)

    back_place = send_place[:, None]
    if rings > 1:
        def own_rows(near, far, name):
            rows = whole(
                output_kernel, name, [xi], (back_place, near, far, jnp.zeros_like(tokens)),
                [shape(tokens.shape, BF16)],
            )[0]
            return dot(ring_order, from_blocks(over_rings(rows)), TN)

        output = (tokens.astype(F32) + own_rows(out_near, out_far, "output")).astype(BF16)
        rows = own_rows(in_near, in_far, "rows_back")
        own_x = tokens.astype(F32)
        inverse = lax.rsqrt(jnp.mean(own_x * own_x, axis=1, keepdims=True) + EPSILON)
        hat = own_x * inverse
        gain_rel = gain_row[:1].reshape(2, zs, 2, ring_rows)
        gain_abs = jnp.where(xi == 0, gain_rel, gain_rel[::-1]).transpose(1, 0, 2, 3)
        grad = rows * from_blocks(gain_abs.reshape(1, width))
        input_grad = cotangent.astype(F32) + inverse * (
            grad - hat * jnp.mean(grad * hat, axis=1, keepdims=True)
        )
    else:
        output = whole(
            output_kernel, "output", [xi], (back_place, out_near, out_far, tokens),
            [shape(tokens.shape, BF16)],
        )[0]
        input_grad = whole(
            input_kernel, "input_grad", [xi],
            (back_place, in_near, in_far, tokens, cotangent, gain_row),
            [shape(tokens.shape, F32)],
        )[0]
    late_home, stream_home, output, input_grad, select_grad = step(
        late_home, stream_home, output, input_grad, select_grad
    )
    gate_home, outer_home = late_home[:, :part], late_home[:, part:]
    outer_home = outer_home.reshape(half_channels, ring_rows).astype(F32)
    inner_home = jnp.stack(
        [v.reshape(half_channels, ring_rows).T for v in (stream_home, gate_home)], axis=1
    ).astype(F32)
    if rings > 1:
        outer_home = lax.psum_scatter(outer_home, "r", scatter_dimension=1, tiled=True)
        inner_home = lax.psum_scatter(inner_home, "r", scatter_dimension=0, tiled=True)
    gain_grad = jnp.sum(inner_home * inner_weight.astype(F32), axis=(1, 2))
    gain_grad = (gain_grad + swap(gain_grad, "t", "gain")) / norm_gain.astype(F32)
    return (
        output,
        input_grad,
        gain_grad,
        inner_home,
        filter_grad,
        filter_b_grad[0],
        select_grad.T,
        step_w_grad,
        step_b_grad[0],
        decay_grad,
        skip_grad[0],
        outer_home,
    )


def solution(mesh):
    devices = mesh.devices
    split = Mesh(
        devices.reshape(devices.shape[0] // 16, 4, 2, 2, devices.shape[1]), DP + ("t",)
    )
    in_specs = (
        P(DP, None), P(DP, None), P(), P(DP, None), P(DP), P(DP, None, "t"), P(None, "t"), P("t"),
        P("t", None), P(None, "t"), P("t"), P(None, "t"), P("t"), P("t", DP),
    )
    out_specs = (
        P(DP, None), P(DP, None), P(DP), P(DP, None, "t"), P(None, "t"), P("t"), P("t", None),
        P(None, "t"), P("t"), P(None, "t"), P("t"), P("t", DP),
    )
    return jax.shard_map(body, mesh=split, in_specs=in_specs, out_specs=out_specs, check_vma=False)
```

```python
from functools import partial
from inspect import isgeneratorfunction

import jax
import jax.numpy as jnp
from jax import lax
from jax.experimental import pallas as pl
from jax.experimental.pallas import tpu as pltpu
from jax.sharding import Mesh, PartitionSpec as P

MB = 2
EPSILON = 1e-05
ZK = ("z", "k")
DP = ("r", "z", "x", "k")
SWAP = [(0, 1), (1, 0)]
LOG2E = 1.4426950408889634
RESET_RATE = 1e30
LANES = 128
MICROSECONDS = {
    "pack": 3, "pack_cores": 3, "prep": 2, "front": 8, "late": 8, "mixer": 24, "out_rows": 5,
    "late_grad": 6, "back": 7, "in_rows": 7, "output": 3, "input_grad": 4, "small": 3,
    "rows_back": 3,
}
SUBLANES = 8
SIDE = 2
GROUP = 8
CHUNK = 64
UNROLL = 8
LOAD, STORE = 0, 1
F32 = jnp.float32
BF16 = jnp.bfloat16
NT = ((1,), (1,))
TN = ((0,), (0,))


def dot(lhs, rhs, contract=((1,), (0,))):
    return lax.dot_general(lhs, rhs, (contract, ((), ())), preferred_element_type=F32)


def split_dot(lhs, rhs, contract=((1,), (0,))):
    high = lhs.astype(BF16)
    rest = (lhs - high.astype(F32)).astype(BF16)
    return dot(high, rhs, contract) + dot(rest, rhs, contract)


def shape(dims, dtype):
    return jax.ShapeDtypeStruct(dims, dtype)


def whole(kernel, name, scalars, arrays, outs, scratch=()):
    scalars = [jnp.reshape(v, (1,)).astype(jnp.int32) for v in scalars]
    few, many, made = len(scalars), len(arrays), len(outs)

    def copied(*refs):
        inputs, refs_rest = refs[few : few + many], refs[few + many :]
        outputs, refs_rest = refs_rest[:made], refs_rest[made:]
        held, results = refs_rest[:many], refs_rest[many : many + made]
        *rest, semaphores = refs_rest[many + made :]
        loads = [
            pltpu.make_async_copy(source, target, semaphores.at[i])
            for i, (source, target) in enumerate(zip(inputs, held))
        ]
        stores = [
            pltpu.make_async_copy(source, target, semaphores.at[many + i])
            for i, (source, target) in enumerate(zip(results, outputs))
        ]
        for copy in loads:
            copy.start()
        asked = {LOAD: set(), STORE: set()}

        def ask(kind, numbers):
            for i in numbers:
                if i not in asked[kind]:
                    asked[kind].add(i)
                    loads[i].wait() if kind == LOAD else stores[i].start()

        lazy = isgeneratorfunction(getattr(kernel, "func", kernel))
        if not lazy:
            ask(LOAD, range(many))
        parts = kernel(*refs[:few], *held, *results, *rest)
        for kind, numbers in parts if lazy else ():
            ask(kind, numbers)
        ask(LOAD, range(many))
        ask(STORE, range(made))
        for copy in stores:
            copy.wait()

    return pl.pallas_call(
        copied,
        in_specs=[pl.BlockSpec(memory_space=pltpu.SMEM)] * few
        + [pl.BlockSpec(memory_space=pltpu.HBM)] * many,
        out_specs=[pl.BlockSpec(memory_space=pltpu.HBM)] * made,
        out_shape=list(outs),
        scratch_shapes=[
            *(pltpu.VMEM(v.shape, v.dtype) for v in (*arrays, *outs)),
            *scratch,
            pltpu.SemaphoreType.DMA((many + made,)),
        ],
        compiler_params=pltpu.CompilerParams(vmem_limit_bytes=60 << 20),
        cost_estimate=pl.CostEstimate(
            flops=0, bytes_accessed=MICROSECONDS[name] * 3690000, transcendentals=0
        ),
        name=name,
    )(*scalars, *arrays)


def row_matches(places, count):
    rows = lax.broadcasted_iota(jnp.int32, (count, places.shape[1]), 0)
    return (rows == places).astype(F32).astype(BF16)


def column_matches(places, count):
    columns = lax.broadcasted_iota(jnp.int32, (places.shape[0], count), 1)
    return (columns == places).astype(F32).astype(BF16)


def tiles(count, size):
    return [slice(i, i + size) for i in range(0, count, size)]


def prep_kernel(x_ref, place_ref, tok_ref, cot_ref, note_ref, tok_keep, tok_send, cot_keep, cot_send):
    share = tok_keep.shape[0]
    width = tok_ref.shape[1]
    half = width // 2
    order = row_matches(place_ref[...], 2 * share)
    for source, outs in ((tok_ref, (tok_keep, tok_send)), (cot_ref, (cot_keep, cot_send))):
        rows = dot(order, source[...])
        for side in (0, 1):
            part = rows[side * share : (side + 1) * share]
            for x in (0, 1):
                same = x_ref[0] == (x ^ side)
                for zk in range(half // LANES):
                    place = (zk // 2) * 4 + zk % 2
                    zero = part[:, place * LANES : (place + 1) * LANES]
                    one = part[:, (place + 2) * LANES : (place + 3) * LANES]
                    to = slice(x * half + zk * LANES, x * half + (zk + 1) * LANES)
                    outs[side][:, to] = jnp.where(same, zero, one).astype(BF16)
    tok_keep[:, width:] = note_ref[...]
    tok_send[:, width:] = note_ref[...]


def place_rows(x_ref, place_ref, near_ref, far_ref):
    share = near_ref.shape[0] // 2
    width = near_ref.shape[1]
    half = width // 2
    order = column_matches(place_ref[...], 4 * share)
    total = None
    for group in range(4):
        source = (near_ref, far_ref)[group // 2]
        rows = slice((group % 2) * share, (group % 2 + 1) * share)
        blocks = []
        for block in range(width // LANES):
            z, x, k = block // 4, (block // 2) % 2, block % 2
            same = x_ref[0] == (x ^ (group % 2))
            at = (z * 2 + k) * LANES
            first = source[rows, at : at + LANES].astype(F32)
            second = source[rows, half + at : half + at + LANES].astype(F32)
            blocks.append(jnp.where(same, first, second).astype(BF16))
        piece = dot(order[:, group * share : (group + 1) * share], jnp.concatenate(blocks, 1))
        total = piece if total is None else total + piece
    return total


def output_kernel(x_ref, place_ref, near_ref, far_ref, tok_ref, out_ref):
    rows = place_rows(x_ref, place_ref, near_ref, far_ref)
    out_ref[...] = (tok_ref[...].astype(F32) + rows).astype(BF16)


def input_kernel(x_ref, place_ref, near_ref, far_ref, tok_ref, cot_ref, gain_ref, out_ref):
    rows = place_rows(x_ref, place_ref, near_ref, far_ref)
    x = tok_ref[...].astype(F32)
    inverse = lax.rsqrt(jnp.mean(x * x, axis=1, keepdims=True) + EPSILON)
    hat = x * inverse
    half = gain_ref.shape[1] // 2
    gains = []
    for block in range(x.shape[1] // LANES):
        z, side, k = block // 4, (block // 2) % 2, block % 2
        at = (z * 2 + k) * LANES
        gains.append(
            jnp.where(
                x_ref[0] == side,
                gain_ref[0:1, at : at + LANES],
                gain_ref[0:1, half + at : half + at + LANES],
            )
        )
    grad = rows * jnp.concatenate(gains, 1)
    out_ref[...] = cot_ref[...].astype(F32) + inverse * (
        grad - hat * jnp.mean(grad * hat, axis=1, keepdims=True)
    )


def column_sum(rows_ref, pieces):
    own, by_x, by_t, *diagonal = pieces
    depth = own.shape[0]
    near, far = rows_ref[:, :depth], rows_ref[:, depth:]
    a = dot(near, own[...]) + dot(far, by_x[...])
    b = dot(near, by_t[...])
    for i, at in enumerate(tiles(depth, diagonal[0].shape[0])):
        b = b + dot(far[:, at], diagonal[i][...])
    return a, b


def z_block(z_ref, step, size):
    return lax.rem(z_ref[0] + (size - step), size)


def row_sum(z_ref, sides, out_refs):
    depth = sides[0][1][0].shape[0]
    rows = sides[0][0].shape[0] // 2
    block = 2 * LANES
    for base in range(0, 2 * depth, block):
        at = slice(base % depth, base % depth + block)
        value = None
        for lhs, (own, by_x, by_t, *diagonal) in sides:
            part = lhs.shape[1] // 2
            if base < depth:
                near, far = own[at, :], by_t[at, :]
            else:
                size = diagonal[0].shape[0]
                inner = slice(at.start % size, at.start % size + block)
                near, far = by_x[at, :], diagonal[at.start // size][inner, :]
            term = dot(lhs[:, :part], near, NT) + dot(lhs[:, part:], far, NT)
            value = term if value is None else value + term
        place = z_block(z_ref, at.start // block, depth // block) * block
        to = pl.ds(pl.multiple_of(base // depth * depth + place, block), block)
        for i, out in enumerate(out_refs):
            out[:, to] = value[i * rows : (i + 1) * rows].astype(BF16)


def reorder_rows(z_ref, order, source, out):
    block = 2 * LANES
    half = out.shape[1] // 2
    for base in range(0, 2 * half, block):
        step = base % half // block
        place = base // half * half + z_block(z_ref, step, half // block) * block
        at = pl.ds(pl.multiple_of(place, block), block)
        out[:, base : base + block] = dot(order, source[:, at]).astype(BF16)


def grad_pieces(z_ref, channels_t, rows_ref, outs):
    part = channels_t.shape[0] // 2
    depth = rows_ref.shape[1] // 2
    for at in tiles(2 * depth, 2 * LANES):
        value = dot(channels_t, rows_ref[:, at])
        near_out, far_out = (outs[0], outs[2]) if at.start < depth else (outs[1], outs[3])
        block = 2 * z_block(z_ref, (at.start % depth) // (2 * LANES), depth // (2 * LANES))
        for i in (0, 1):
            lanes = value[:, i * LANES : (i + 1) * LANES].astype(BF16)
            for refs, rows in ((near_out, lanes[:part]), (far_out, lanes[part:])):
                size = part // len(refs)
                for j, ref in enumerate(refs):
                    ref[block + i, :, :] = rows[j * size : (j + 1) * size]


def first_pack_kernel(z_ref, k_ref, stream, gate, outer, keep, send):
    count = keep.shape[0] // 3
    part = keep.shape[2]
    for i, source in enumerate((stream, gate, outer)):
        for step in range(count):
            z = lax.rem(z_ref[0] + step, count)
            for out, core in ((keep, k_ref[0]), (send, 1 - k_ref[0])):
                at = pl.ds(pl.multiple_of((z * 2 + core) * part, part), part)
                out[i * count + step] = source[:, at]


def second_pack_kernel(k_ref, kept, got, *outs):
    first = k_ref[0] == 0
    height = kept.shape[1]
    for i, out in enumerate(outs):
        mine, other = kept[i].astype(F32), got[i].astype(F32)
        out[:height, :] = jnp.where(first, mine, other).astype(BF16)
        out[height:, :] = jnp.where(first, other, mine).astype(BF16)


def down(value, count):
    if count == 0:
        return value
    return jnp.concatenate([jnp.zeros((count, value.shape[1]), value.dtype), value[:-count]], 0)


def up(value, count):
    if count == 0:
        return value
    return jnp.concatenate([value[count:], jnp.zeros((count, value.shape[1]), value.dtype)], 0)


def lag_masks(place, taps):
    return [None] + [place >= lag for lag in range(1, taps)]


def masked(value, mask):
    return value if mask is None else jnp.where(mask, value, 0.0)


def filter_sum(stream, masks, weights):
    taps = len(masks)
    total = weights[taps : taps + 1, :] + weights[taps - 1 : taps, :] * stream
    for lag in range(1, taps):
        total = total + weights[taps - 1 - lag : taps - lag, :] * masked(
            down(stream, SUBLANES * lag), masks[lag]
        )
    return total


def places(notes, rows, per_device):
    segments = len(notes) * MB
    zero = lax.broadcasted_iota(jnp.int32, (segments, LANES), 0) % MB
    lane = lax.broadcasted_iota(jnp.int32, (segments, LANES), 1)
    table = jnp.concatenate([v for v in notes for _ in range(MB)], 0)
    begin = jnp.zeros((segments, 1), F32)
    step = lax.broadcasted_iota(jnp.int32, (rows, LANES), 0) // segments
    step = step.astype(F32)
    latest = jnp.zeros((rows, LANES), F32)
    for i in range(per_device - 1):
        picked = jnp.where(lane == zero * per_device + i, table, 0.0)
        begin = begin + jnp.sum(picked, axis=1, keepdims=True)
        every = jnp.concatenate(
            [jnp.broadcast_to(begin, (segments, LANES))] * (rows // segments), 0
        )
        latest = jnp.where(every <= step, every, latest)
    return step - latest


def front_kernel(
    sizes, core_ref, tensor_ref, z_ref, x_ref, place_ref, own, by_x, by_t, low, high, par_ref, sel_ref,
    n_ref, stream_ref, act_ref, mine_ref, other_ref, pos_ref, gain_ref, nrm, act_low,
):
    yield LOAD, (0, 1)
    taps, per_device = sizes
    rows = x_ref.shape[0]
    width = n_ref.shape[1]
    depth = width // 2
    part = own.shape[1]
    members = depth // LANES
    share = rows // (2 * members)
    note = slice(width, width + LANES)
    for side in (0, 1):
        for member in range(members):
            row = member * 2 * share + side * share
            at = side * depth + member * LANES
            gain_ref[0:1, at : at + LANES] = x_ref[row : row + 16, note].astype(F32)[0:1]
    notes = []
    for z in range(members // 2):
        two = [
            x_ref[m * 2 * share : m * 2 * share + 16, note].astype(F32)[1:2]
            for m in (2 * z, 2 * z + 1)
        ]
        notes.append(jnp.where(tensor_ref[0] == 0, two[0], two[1]))
    place = places(notes, rows, per_device)
    pos_ref[...] = place

    def norm(i, _):
        at = pl.ds(pl.multiple_of(i * 64, 64), 64)
        x = x_ref[at, :width].astype(F32)
        inverse = lax.rsqrt(jnp.mean(x * x, axis=1, keepdims=True) + EPSILON)
        nrm[at, :] = (x * inverse * gain_ref[0:1, :]).astype(BF16)
        return 0

    lax.fori_loop(0, rows // 64, norm, 0)
    reorder_rows(z_ref, row_matches(place_ref[...], rows), nrm, n_ref)
    yield STORE, (0, 5, 6)
    yield LOAD, (2, 3, 4, 5, 6)
    near, far = column_sum(n_ref, (own, by_x, by_t, low, high))
    stream_ref[:, :part] = near
    stream_ref[:, part:] = far
    yield STORE, (1,)
    yield LOAD, (7, 8)
    masks = lag_masks(place, taps)
    for at in tiles(2 * part, LANES):
        filtered = filter_sum(stream_ref[:, at], masks, par_ref[:, at])
        act = filtered * jax.nn.sigmoid(filtered)
        act_ref[:, at] = act
        act_low[:, at] = act.astype(BF16)
    yield STORE, (2,)
    selected = dot(sel_ref[...], act_low[...], NT)
    first = core_ref[0] == 0
    mine_ref[...] = jnp.where(first, selected[:, : rows // 2], selected[:, rows // 2 :])
    other_ref[...] = jnp.where(first, selected[:, rows // 2 :], selected[:, : rows // 2])


def late_kernel(z_ref, cot_ref, place_ref, n_ref, *refs):
    gate_pieces, out_pieces = refs[:4], refs[4:8]
    up_ref, gate_ref, gg_ref = refs[8:]
    part = gate_pieces[0].shape[1]
    yield LOAD, (0, 1)
    reorder_rows(z_ref, row_matches(place_ref[...], cot_ref.shape[0]), cot_ref, up_ref)
    yield STORE, (0,)
    for i, (source, out, pieces) in enumerate(
        ((n_ref, gate_ref, gate_pieces), (up_ref, gg_ref, out_pieces))
    ):
        yield LOAD, (2, *range(3 + 4 * i, 7 + 4 * i))
        near, far = column_sum(source, pieces)
        out[:, :part] = near
        out[:, part:] = far
        yield STORE, (1 + i,)


def out_kernel(z_ref, place_ref, gated_ref, *refs):
    yield LOAD, (0, 1)
    order = row_matches(place_ref[...], gated_ref.shape[0])
    rows = dot(order, gated_ref[...], TN).astype(BF16)
    yield LOAD, (2, 3, 4, 5)
    row_sum(z_ref, [(rows, refs[:4])], refs[4:])


def late_grad_kernel(z_ref, n_ref, up_ref, gate_grad_ref, gated_ref, *outs):
    gate_own, gate_t, outer_own, outer_x, x_way, t_way = outs
    for source, rows_ref, pieces, needs, ends in (
        (gate_grad_ref, n_ref, (gate_own, x_way.at[1], gate_t, x_way.at[0]), (2, 0), (4, 1, 0)),
        (gated_ref, up_ref, (outer_own, outer_x, t_way.at[1], t_way.at[0]), (3, 1), (5, 3, 2)),
    ):
        yield LOAD, needs[:1]
        channels_t = source[...].astype(F32).T.astype(BF16)
        yield LOAD, needs[1:]
        grad_pieces(z_ref, channels_t, rows_ref, [[v] for v in pieces])
        yield STORE, ends


def back_kernel(
    taps, core_ref, z_ref, total_ref, rest_ref, pos_ref, stream_ref, sact_ref, par_ref, sel_ref, n_ref,
    low_ref, small_ref, *refs,
):
    *outs, act_low, grad_t = refs
    yield LOAD, (0, 1, 2, 3, 4, 5, 6)
    rows, channels = stream_ref.shape
    first = core_ref[0] == 0
    total, rest = total_ref[...], rest_ref[...]
    selected_t = jnp.concatenate(
        [jnp.where(first, total, rest), jnp.where(first, rest, total)], 1
    )
    selected_low = selected_t.astype(BF16)
    count = selected_t.shape[0]
    padded = jnp.concatenate(
        [selected_t, jnp.zeros((-count % LANES, rows), F32)], 0
    )
    selected = padded.T.astype(BF16)
    masks = lag_masks(pos_ref[...], taps)
    spare = jnp.zeros((SUBLANES - taps - 1, LANES), F32)
    for at in tiles(channels, LANES):
        stream = stream_ref[:, at]
        weights = par_ref[:, at]
        filtered = filter_sum(stream, masks, weights)
        slope = jax.nn.sigmoid(filtered)
        act_low[:, at] = (filtered * slope).astype(BF16)
        select = jnp.concatenate(
            [sel_ref[:, at], jnp.zeros((-count % LANES, LANES), BF16)], 0
        )
        act_grad = sact_ref[:, at] + dot(selected, select)
        grad = act_grad * (slope * (1.0 + filtered * (1.0 - slope)))
        stream_grad = weights[taps - 1 : taps, :] * grad
        sums = [jnp.sum(grad * stream, axis=0, keepdims=True)]
        for lag in range(1, taps):
            part_grad = masked(grad, masks[lag])
            sums.append(
                jnp.sum(part_grad * down(stream, SUBLANES * lag), axis=0, keepdims=True)
            )
            stream_grad = stream_grad + weights[taps - 1 - lag : taps - lag, :] * up(
                part_grad, SUBLANES * lag
            )
        sums = sums[::-1] + [jnp.sum(grad, axis=0, keepdims=True), spare]
        small_ref[count:, at] = jnp.concatenate(sums, 0).astype(BF16)
        low_ref[:, at] = stream_grad.astype(BF16)
        grad_t[at, :] = stream_grad.T.astype(BF16)
    yield STORE, (0,)
    small_ref[:count, :] = dot(selected_low, act_low[...]).astype(BF16)
    yield STORE, (1,)
    yield LOAD, (7,)
    own_low, own_high, by_x_high, by_t_low, x_way, t_way = outs
    grad_pieces(
        z_ref, grad_t[...], n_ref,
        [
            (own_low, own_high), (x_way.at[1], by_x_high),
            (by_t_low, t_way.at[1]), (x_way.at[0], t_way.at[0]),
        ],
    )


def in_kernel(z_ref, place_ref, low_ref, gate_grad_ref, *refs):
    stream_pieces, gate_pieces, outs, stage = refs[:5], refs[5:9], refs[9:11], refs[11]
    channels = low_ref.shape[1]
    yield LOAD, (0, 1, 2)
    order = row_matches(place_ref[...], low_ref.shape[0])
    stage[:, :channels] = dot(order, low_ref[...], TN).astype(BF16)
    stage[:, channels:] = dot(order, gate_grad_ref[...], TN).astype(BF16)
    yield LOAD, range(3, 12)
    row_sum(
        z_ref, [(stage[:, :channels], stream_pieces), (stage[:, channels:], gate_pieces)], outs
    )


def small_kernel(sizes, z_ref, x_ref, k_ref, mine, other, *outs):
    count, states, taps, zs = sizes
    select, step_w, decay, filters, filter_b, step_b, skip = outs
    part = mine.shape[1]
    rank = step_w.shape[0]
    half = mine.shape[0] // (2 * zs)
    first_x = x_ref[0] == 0
    for source, core in ((mine, k_ref[0]), (other, 1 - k_ref[0])):
        for shift in range(zs):
            near = source[shift * half : (shift + 1) * half, :].astype(F32)
            far = source[(zs + shift) * half : (zs + shift + 1) * half, :].astype(F32)
            block = jnp.concatenate(
                [jnp.where(first_x, near, far), jnp.where(first_x, far, near)], 0
            )
            place = (z_block(z_ref, shift, zs) * 2 + core) * part
            at = pl.ds(pl.multiple_of(place, part), part)
            step_b[:, at] = block[0:1]
            skip[:, at] = block[1:2]
            decay[:, at] = block[8 : states + 8]
            step_w[:, at] = block[states + 8 : states + 8 + rank]
            rest = block[states + 8 + rank :]
            filters[:, at] = rest[count : count + taps]
            filter_b[:, at] = rest[count + taps : count + taps + 1]
            select[:, at] = rest[:count]


def scan_kernel(
    layout, core_ref, pos_ref, act_ref, gate_ref, gg_ref, total_ref, rest_ref, sw_ref, par_ref,
    gated_ref, gateg_ref, sact_ref, small_ref, mine_ref, other_ref,
    bb, cb, hist, fac, ci_acc, co_acc, rate_s, reff_s, u_s, ds_s, y_s, s2_s, slope_s, spre_low, decb, sel_t, rate_low, rank_t,
):
    rank_width, states, bias_row, decay_row, skip_row = layout
    rows, channels = act_ref.shape
    lanes = LANES
    steps = rows // SUBLANES
    wide = states * lanes
    first = core_ref[0] == 0
    spread = (
        lax.broadcasted_iota(jnp.int32, (states, wide), 1) // lanes
        == lax.broadcasted_iota(jnp.int32, (states, wide), 0)
    ).astype(F32).astype(BF16)
    yield LOAD, (4, 5)
    total, rest = total_ref[...], rest_ref[...]
    sel_t[:, : rows // 2] = jnp.where(first, total, rest)
    sel_t[:, rows // 2 :] = jnp.where(first, rest, total)
    rate_low[...] = sel_t[:rank_width, :].T.astype(BF16)
    twice = jnp.concatenate([spread, spread], 0)
    for out, base in ((bb, rank_width), (cb, rank_width + states)):
        value = sel_t[base : base + states, :]
        high = value.astype(BF16).astype(F32)
        parts = jnp.concatenate([high, value - high], 0).astype(BF16)
        out[...] = dot(parts, twice, TN)
    hist[0:SUBLANES, :] = jnp.zeros((SUBLANES, SIDE * wide), F32)
    ci_acc[...] = jnp.zeros_like(ci_acc)
    co_acc[...] = jnp.zeros_like(co_acc)
    rank_t[...] = jnp.zeros_like(rank_t)
    zero = jnp.zeros((8, lanes), F32)
    sides = range(SIDE)
    both = SIDE * lanes

    def cols(n):
        return slice(n * lanes, (n + 1) * lanes)

    def wide_cols(n, side):
        return slice((n * SIDE + side) * lanes, (n * SIDE + side + 1) * lanes)

    def side_cols(side):
        return slice(side * lanes, (side + 1) * lanes)

    def one_block(block, _):
        at = pl.ds(pl.multiple_of(block * both, both), both)
        decay = -jnp.exp(par_ref[decay_row : decay_row + states, at])
        for n in range(states):
            decb[8 * n : 8 * n + 8, :] = jnp.broadcast_to(decay[n : n + 1, :], (8, both))
        rate_s[...] = dot(rate_low[...], sw_ref[:, at]) + par_ref[bias_row : bias_row + 1, at]

        def before(i, _):
            row = pl.ds(pl.multiple_of(i * CHUNK, CHUNK), CHUNK)
            step_pre = rate_s[row, :]
            small = jnp.exp(-jnp.abs(step_pre))
            rate = jnp.maximum(step_pre, 0.0) + jnp.log1p(small)
            inverse = 1.0 / (1.0 + small)
            slope_s[row, :] = jnp.where(step_pre >= 0.0, inverse, small * inverse)
            rate_s[row, :] = rate
            keep = pos_ref[row, :] > 0.0
            for side in sides:
                reff_s[row, side_cols(side)] = jnp.where(
                    keep, rate[:, side_cols(side)] * LOG2E, RESET_RATE
                )
            u_s[row, :] = rate * act_ref[row, at]
            gate = gate_ref[row, at]
            ds_s[row, :] = gg_ref[row, at] * (gate * jax.nn.sigmoid(gate))
            return 0

        lax.fori_loop(0, rows // CHUNK, before, 0)

        for group in range(states // GROUP):
            names = range(group * GROUP, (group + 1) * GROUP)

            def forward(t, h, names=names, group=group):
                row = pl.ds(pl.multiple_of(t * 8, 8), 8)
                next_row = pl.ds(pl.multiple_of(t * 8 + 8, 8), 8)
                reff = [reff_s[row, side_cols(i)] for i in sides]
                u = [u_s[row, side_cols(i)] for i in sides]
                ds = [ds_s[row, side_cols(i)] for i in sides]
                y = [zero if group == 0 else y_s[row, side_cols(i)] for i in sides]
                fresh = []
                for n in names:
                    b, c = bb[row, cols(n)], cb[row, cols(n)]
                    out = co_acc[row, cols(n)]
                    for i in sides:
                        a = jnp.exp2(reff[i] * decb[8 * n : 8 * n + 8, side_cols(i)])
                        hn = a * h[len(fresh)] + b * u[i]
                        hist[next_row, wide_cols(n, i)] = hn
                        fac[row, wide_cols(n, i)] = a
                        y[i] = y[i] + c * hn
                        out = out + ds[i] * hn
                        fresh.append(hn)
                    co_acc[row, cols(n)] = out
                for i in sides:
                    y_s[row, side_cols(i)] = y[i]
                return tuple(fresh)

            lax.fori_loop(0, steps, forward, (zero,) * (GROUP * SIDE), unroll=UNROLL)

        skip = par_ref[skip_row : skip_row + 1, at]

        def between(i, _):
            row = pl.ds(pl.multiple_of(i * CHUNK, CHUNK), CHUNK)
            scanned = y_s[row, :] + skip * act_ref[row, at]
            gate = gate_ref[row, at]
            sig = jax.nn.sigmoid(gate)
            gated_ref[row, at] = (scanned * (gate * sig)).astype(BF16)
            gateg_ref[row, at] = (
                gg_ref[row, at] * scanned * (sig * (1.0 + gate * (1.0 - sig)))
            ).astype(BF16)
            return 0

        lax.fori_loop(0, rows // CHUNK, between, 0)

        sums = []
        for group in range(states // GROUP):
            names = range(group * GROUP, (group + 1) * GROUP)

            def backward(i, carried, names=names, group=group):
                g, dacc = carried
                t = steps - 1 - i
                row = pl.ds(pl.multiple_of(t * 8, 8), 8)
                ds = [ds_s[row, side_cols(k)] for k in sides]
                u = [u_s[row, side_cols(k)] for k in sides]
                rt = [rate_s[row, side_cols(k)] for k in sides]
                s1 = [zero if group == 0 else reff_s[row, side_cols(k)] for k in sides]
                s2 = [zero if group == 0 else s2_s[row, side_cols(k)] for k in sides]
                g_new, d_new = [], []
                for n in names:
                    b, c = bb[row, cols(n)], cb[row, cols(n)]
                    out = ci_acc[row, cols(n)]
                    for k in sides:
                        lam = c * ds[k] + g[len(g_new)]
                        q = lam * fac[row, wide_cols(n, k)]
                        hp = hist[row, wide_cols(n, k)] * q
                        s1[k] = s1[k] + hp * decb[8 * n : 8 * n + 8, side_cols(k)]
                        s2[k] = s2[k] + lam * b
                        out = out + lam * u[k]
                        d_new.append(dacc[len(g_new)] + hp * rt[k])
                        g_new.append(q)
                    ci_acc[row, cols(n)] = out
                for k in sides:
                    s2_s[row, side_cols(k)] = s2[k]
                    reff_s[row, side_cols(k)] = s1[k]
                return tuple(g_new), tuple(d_new)

            none = (zero,) * (GROUP * SIDE)
            _, dacc = lax.fori_loop(0, steps, backward, (none, none), unroll=UNROLL)
            for n in range(GROUP):
                row = jnp.concatenate(
                    [jnp.sum(dacc[n * SIDE + k], axis=0, keepdims=True) for k in sides], 1
                )
                name = group * GROUP + n
                sums.append(row * decb[8 * name : 8 * name + 1, :])

        def behind(i, carried):
            row = pl.ds(pl.multiple_of(i * CHUNK, CHUNK), CHUNK)
            act, dscan, s2_all = act_ref[row, at], ds_s[row, :], s2_s[row, :]
            sact_ref[row, at] = rate_s[row, :] * s2_all + skip * dscan
            spre = (reff_s[row, :] + act * s2_all) * slope_s[row, :]
            spre_low[row, :] = spre.astype(BF16)
            totals = []
            for total, value in zip(carried, (spre, dscan * act)):
                for j in range(CHUNK // SUBLANES):
                    total = total + value[j * SUBLANES : (j + 1) * SUBLANES]
                totals.append(total)
            return tuple(totals)

        empty = jnp.zeros((SUBLANES, both), F32)
        head = [
            jnp.sum(v, axis=0, keepdims=True)
            for v in lax.fori_loop(0, rows // CHUNK, behind, (empty, empty))
        ]
        head.append(jnp.zeros((6, both), F32))
        small_ref[: states + 8, at] = jnp.concatenate(head + sums, 0).astype(BF16)
        small_ref[states + 8 :, at] = dot(
            sel_t[:rank_width, :].astype(BF16), spre_low[...]
        ).astype(BF16)
        rank_t[...] += dot(sw_ref[:, at], spre_low[...], NT)
        return 0

    yield LOAD, (0, 1, 2, 3, 6, 7)
    lax.fori_loop(0, channels // both, one_block, 0)
    yield STORE, (0, 1, 2, 3)
    high, low = slice(0, rows // 2), slice(rows // 2, rows)
    for acc, base in ((ci_acc, rank_width), (co_acc, rank_width + states)):
        sel_t[base : base + states, :] = dot(acc[...].astype(BF16), spread, NT).T
    sel_t[:rank_width, :] = rank_t[...]
    mine_ref[...] = jnp.where(first, sel_t[:, high], sel_t[:, low])
    other_ref[...] = jnp.where(first, sel_t[:, low], sel_t[:, high])


def mixer(layout, core, position, act, gate, gated_grad, total, rest, step_w, params):
    rows, channels = act.shape
    rank_width, states = layout[:2]
    count = total.shape[0]
    wide = states * LANES
    return whole(
        partial(scan_kernel, layout), "mixer", [core],
        (position, act, gate, gated_grad, total, rest, step_w, params),
        [
            shape((rows, channels), BF16), shape((rows, channels), BF16),
            shape((rows, channels), F32), shape((rank_width + states + 8, channels), BF16),
            shape((count, rows // 2), F32), shape((count, rows // 2), F32),
        ],
        [
            pltpu.VMEM((rows, wide), F32), pltpu.VMEM((rows, wide), F32),
            pltpu.VMEM((rows + 8, SIDE * wide), F32), pltpu.VMEM((rows, SIDE * wide), F32),
            pltpu.VMEM((rows, wide), F32), pltpu.VMEM((rows, wide), F32),
        ]
        + [pltpu.VMEM((rows, SIDE * LANES), F32)] * 7
        + [
            pltpu.VMEM((rows, SIDE * LANES), BF16),
            pltpu.VMEM((8 * states, SIDE * LANES), F32), pltpu.VMEM((count, rows), F32),
            pltpu.VMEM((rows, rank_width), BF16), pltpu.VMEM((rank_width, rows), F32),
        ],
    )


def step(*values):
    return lax.optimization_barrier(values)


def swap(value, axis, name="swap"):
    with jax.named_scope(f"{name}_{axis}"):
        return lax.ppermute(value, axis, SWAP)


def exchange_z(value, distance, name):
    size = lax.axis_size("z")
    with jax.named_scope(f"{name}_z"):
        return lax.ppermute(value, "z", [(i, i ^ distance) for i in range(size)])


def from_z(blocks, name):
    size = lax.axis_size("z")
    got = [blocks[0]]
    for shift in range(1, size):
        with jax.named_scope(f"{name}_z"):
            got.append(
                lax.ppermute(blocks[shift], "z", [(i, (i + shift) % size) for i in range(size)])
            )
    return got


def plus(value, *more):
    total = value.astype(F32)
    for v in more:
        total = total + v.astype(F32)
    return total.astype(BF16)


def to_owners(value):
    return lax.all_to_all(value, ZK, 0, 0, tiled=True)


def rank_in_class(keys):
    count = keys.shape[1]
    earlier = jnp.arange(count)[:, None] > jnp.arange(count)[None, :]
    same = (keys[:, :, None] == keys[:, None, :]) & earlier[None]
    return jnp.sum(same.astype(jnp.int32), axis=2)


def body(
    tokens, cotangent, owner_slot, sequence_lengths, norm_gain, inner_weight, filter_weight,
    convolution_bias, select_weight, step_weight, step_bias, decay_log, skip_weight, output_weight,
):
    rings = lax.axis_size("r")
    zs = lax.axis_size("z")
    members = zs * 4
    ri, zi, xi, ki, ti = (lax.axis_index(a) for a in ("r", "z", "x", "k", "t"))
    local_rows, width = tokens.shape
    rank_width = step_weight.shape[0]
    states = decay_log.shape[0]
    taps = filter_weight.shape[0]
    half_channels = inner_weight.shape[2]
    part = half_channels // (2 * zs)
    channels = 2 * part
    block_rows = inner_weight.shape[0]
    ring_rows = rings * block_rows
    depth = width // 2
    batch_rows = local_rows // MB
    group_rows = zs * local_rows
    segments = group_rows // batch_rows
    share = local_rows // 4

    def to_blocks(value):
        if rings == 1:
            return value
        value = value.reshape(-1, rings, members, block_rows)
        return value.transpose(0, 2, 1, 3).reshape(-1, width)

    def from_blocks(value):
        if rings == 1:
            return value
        value = value.reshape(-1, members, rings, block_rows)
        return value.transpose(0, 2, 1, 3).reshape(-1, width)

    inner = inner_weight
    outer = output_weight.T
    gain = norm_gain[None, :]
    if rings > 1:
        inner = lax.all_gather(inner, "r", axis=0, tiled=True)
        outer = lax.all_gather(outer, "r", axis=0, tiled=True)
        gain = lax.all_gather(gain, "r", axis=1, tiled=True)

    blocks_w = 3 * zs
    kept, sent = whole(
        first_pack_kernel, "pack", [zi, ki], (inner[:, 0], inner[:, 1], outer),
        [shape((blocks_w, ring_rows, part), BF16)] * 2,
    )

    slot_rows = owner_slot.reshape(rings, members, local_rows)
    tok, cot = tokens, cotangent
    ring_block = members * local_rows
    if rings > 1:
        per_ring = local_rows // rings
        flat = slot_rows.reshape(rings * members, local_rows)
        target = flat // ring_block
        place = target * per_ring + rank_in_class(target)
        chosen = jnp.arange(local_rows, dtype=jnp.int32)[None, :, None] == place[:, None, :]
        ordered = jnp.sum(jnp.where(chosen, flat[:, None, :], 0), axis=2)
        ordered = ordered.reshape(rings, members, rings, per_ring)
        ordered = lax.dynamic_index_in_dim(ordered, ri, 2, keepdims=False)
        slots = ordered.transpose(1, 0, 2).reshape(members, local_rows)
        own_place = lax.dynamic_index_in_dim(place, ri * members + zi * 4 + xi * 2 + ki, 0, False)
        ring_order = (
            jnp.arange(local_rows, dtype=jnp.int32)[:, None] == own_place[None, :]
        ).astype(BF16)

        def over_rings(value):
            value = value.reshape(rings, per_ring, width)
            return lax.all_to_all(value, "r", 0, 0, tiled=True).reshape(local_rows, width)

        tok, cot = (over_rings(dot(ring_order, v).astype(BF16)) for v in (tokens, cotangent))
    else:
        slots = slot_rows[0]
    local_slot = slots - ri * ring_block
    owner = local_slot // local_rows
    owner_z, owner_x, owner_k = owner // 4, (owner // 2) % 2, owner % 2
    rank = rank_in_class(owner_x * 2 + owner_k)
    in_owner = local_slot % local_rows
    scan_place = (in_owner % batch_rows) * segments + owner_z * MB + in_owner // batch_rows
    here = zi * 4 + xi * 2 + ki
    mine = [lax.dynamic_index_in_dim(v, here, 0, False) for v in (owner_x, owner_k, rank)]
    send_place = (mine[1] ^ ti) * (2 * share) + (mine[0] ^ xi) * share + mine[2]
    in_group = (owner_x == xi) & (owner_k == ti)
    ranked = (
        jnp.arange(share, dtype=jnp.int32)[None, :, None] == rank[:, None, :]
    ) & in_group[:, None, :]
    arrival = jnp.sum(jnp.where(ranked, scan_place[:, None, :], 0), axis=2)
    arrival = arrival.reshape(zs, 2, 2, share)
    arrival = jnp.where(xi == 0, arrival, arrival[:, ::-1]).transpose(0, 2, 1, 3)
    arrived = arrival.reshape(1, group_rows)
    returned = jnp.where(ki == 0, arrival, arrival[:, ::-1]).transpose(1, 0, 2, 3)
    returned = returned.reshape(1, group_rows)

    blocks = [to_blocks(tok), to_blocks(cot)]
    lengths = sequence_lengths.reshape(1, -1).astype(BF16)
    lengths = jnp.concatenate([lengths, jnp.zeros((1, ring_rows - lengths.shape[1]), BF16)], 1)
    note = jnp.concatenate([gain, lengths, jnp.zeros((share - 2, ring_rows), BF16)], 0)
    noted, plain = shape((share, width + LANES), BF16), shape((share, width), BF16)
    first = (zi * 2 + ki) * part

    def own_channels(value):
        return lax.dynamic_slice_in_dim(value, first, part, 1)

    rows_f = taps + 3 + states
    floats = own_channels(
        jnp.concatenate(
            [
                filter_weight, convolution_bias[None], step_bias[None], decay_log,
                skip_weight[None], jnp.zeros((-rows_f % 8, half_channels), F32),
            ],
            axis=0,
        )
    )
    layout = (rank_width, states, taps + 1, taps + 2, taps + 2 + states)
    select_t = lax.dynamic_slice_in_dim(select_weight, first, part, 0).T
    lows = jnp.concatenate([own_channels(step_weight), select_t], 0)
    count = select_t.shape[0]
    half_out = [shape((count, group_rows // 2), F32)] * 2
    half_rows = [shape((group_rows // 2, width), BF16)] * 2
    full = shape((group_rows, channels), F32)
    wide_low = shape((group_rows, width), BF16)
    half = depth // 2

    def gathered(keep, send):
        return lax.all_gather(jnp.concatenate([keep, send], 0), ZK, axis=0, tiled=True)

    (other_core,) = step(swap(sent, "k", "weights"))
    packed = whole(
        second_pack_kernel, "pack_cores", [ki], (kept, other_core),
        [shape((2 * ring_rows, part), BF16)] * blocks_w,
    )
    *packed, tok, cot = step(*packed, *blocks)
    tok_keep, tok_send, cot_keep, cot_send = whole(
        prep_kernel, "prep", [xi], (send_place[None], tok, cot, note), [noted, noted, plain, plain]
    )
    stream_own, floats_t, lows_t, tok_keep, tok_send, cot_keep, cot_send, *packed = step(
        jnp.concatenate(from_z(packed[:zs], "stream_w"), 0),
        swap(floats, "t", "params"), swap(lows, "t", "params_low"),
        tok_keep, tok_send, cot_keep, cot_send, *packed[zs:],
    )
    tok_got, stream_own = step(swap(tok_send, "x", "tokens"), stream_own)
    group_tokens = gathered(tok_keep, tok_got)
    params = jnp.concatenate([floats, floats_t], axis=1)
    lows = jnp.concatenate([lows, lows_t], axis=1)
    stream_x, stream_t, gate_own, params, step_w, select_w, arrived, returned, cot_got, *packed = step(
        swap(stream_own, "x", "stream_w"), swap(stream_own, "t", "stream_w"),
        jnp.concatenate(from_z(packed[:zs], "gate_w"), 0), params, lows[:rank_width],
        lows[rank_width:], arrived, returned, swap(cot_send, "x", "cot"), *packed[zs:],
    )
    group_cot = gathered(cot_keep, cot_got)
    stream_low, stream_high, outer_own, gate_x, gate_t, gate_own, group_tokens = step(
        swap(stream_x[:half], "t", "stream_w_far"), swap(stream_t[half:], "x", "stream_w_far"),
        jnp.concatenate(from_z(packed, "outer_w"), 0), swap(gate_own, "x", "gate_w"),
        swap(gate_own, "t", "gate_w"), gate_own, group_tokens,
    )
    ws = (stream_own, stream_x, stream_t, stream_low, stream_high)
    normed, stream, act, sel_mine, sel_other, position, gain_row = whole(
        partial(front_kernel, (taps, sequence_lengths.shape[1])), "front", [ki, ti, zi],
        (group_tokens, arrived, *ws, params, select_w),
        [wide_low, full, full, *half_out, shape((group_rows, LANES), F32), shape((8, width), F32)],
        [pltpu.VMEM((group_rows, width), BF16), pltpu.VMEM((group_rows, channels), BF16)],
    )
    normed, stream, act, sel_mine, sel_other, outer_x, outer_t = step(
        normed, stream, act, sel_mine, sel_other,
        swap(outer_own, "x", "outer_w"), swap(outer_own, "t", "outer_w"),
    )
    sent = (sel_mine + swap(sel_other, "k", "select")).astype(BF16)
    got, sent = step(exchange_z(sent, 1, "select"), sent)
    sent = plus(sent, got)
    got, gate_d, outer_d, sent = step(
        exchange_z(sent, 2, "select"), swap(gate_x, "t", "gate_w_far"),
        swap(outer_t, "x", "outer_w_far"), sent,
    )
    total = sent.astype(F32) + got.astype(F32)
    wg, wo = (gate_own, gate_x, gate_t, gate_d), (outer_own, outer_x, outer_t, outer_d)
    upstream, gate, gated_grad = whole(
        late_kernel, "late", [zi], (group_cot, arrived, normed, *wg, *wo), [wide_low, full, full],
    )
    rest = swap(total, "k", "select_rest")
    gated, gate_grad, act_grad, small_a, sel_mine, sel_other = mixer(
        layout, ki, position, act, gate, gated_grad, total, rest, step_w, params
    )

    out_mine, out_other = whole(
        out_kernel, "out_rows", [zi], (returned, gated, *wo), half_rows,
    )
    got, out_mine, out_other, gated, gate_grad = step(
        swap(sel_other, "k", "select"), out_mine, out_other, gated, gate_grad
    )
    sent = (sel_mine + got).astype(BF16)
    pieces = whole(
        late_grad_kernel, "late_grad", [zi], (normed, upstream, gate_grad, gated),
        [shape((2 * zs, part, ring_rows), BF16)] * 4
        + [shape((2, 2 * zs, part, ring_rows), BF16)] * 2,
    )
    got, out_got, sent, *pieces = step(
        exchange_z(sent, 1, "select"), swap(out_other, "k", "rows"), sent, *pieces
    )
    out_total = plus(out_mine, out_got)
    sent = plus(sent, got)
    got, sent, out_total, *pieces = step(
        exchange_z(sent, 2, "select"), sent, out_total, *pieces
    )
    out_back = lax.psum_scatter(out_total, "z", scatter_dimension=0, tiled=True)
    total = sent.astype(F32) + got.astype(F32)
    rest = swap(total, "k", "select_rest")
    low, small_b, *stream_g = whole(
        partial(back_kernel, taps), "back", [ki, zi],
        (total, rest, position, stream, act_grad, params, select_w, normed),
        [shape((group_rows, channels), BF16), shape((count + 8, channels), BF16)]
        + [shape((2 * zs, part // 2, ring_rows), BF16)] * 4
        + [shape((2, 2 * zs, part // 2, ring_rows), BF16)] * 2,
        [pltpu.VMEM((group_rows, channels), BF16), pltpu.VMEM((channels, group_rows), BF16)],
    )
    gate_own_g, gate_t_g, outer_own_g, outer_x_g, x_way_l, t_way_l = pieces
    in_mine, in_other = whole(
        in_kernel, "in_rows", [zi], (returned, low, gate_grad, *ws, *wg),
        half_rows, [pltpu.VMEM((group_rows, 2 * channels), BF16)],
    )
    x_way_l, t_way_l, in_mine, in_other, out_back, small_b, *stream_g = step(
        swap(x_way_l, "x", "late_g"), swap(t_way_l, "t", "late_g"), in_mine, in_other, out_back,
        small_b, *stream_g,
    )
    in_total = plus(in_mine, swap(in_other, "k", "rows"))
    in_back = lax.psum_scatter(in_total, "z", scatter_dimension=0, tiled=True)
    small = jnp.concatenate([small_a, small_b], axis=0)
    gate_second, outer_second, small_got, small, *stream_g = step(
        swap(plus(gate_t_g, x_way_l[0]), "t", "gate_g_sum"),
        swap(plus(outer_x_g, t_way_l[0]), "x", "outer_g_sum"),
        swap(small[:, part:], "t", "small"), small, *stream_g,
    )
    late_sum = jnp.concatenate(
        [plus(gate_own_g, x_way_l[1], gate_second), plus(outer_own_g, t_way_l[1], outer_second)],
        axis=1,
    )
    late_home = to_owners(late_sum)
    own_low, own_high, by_x_high, by_t_low, x_way, t_way = stream_g
    small = plus(small[:, :part], small_got)
    small_half = small.shape[0] // 2
    small_kept = lax.dynamic_slice_in_dim(small, xi * small_half, small_half, 0)
    small_sent = lax.dynamic_slice_in_dim(small, (1 - xi) * small_half, small_half, 0)

    def near_rows(rows):
        return jnp.concatenate([rows[:share], swap(rows[share:], "x", "rows")], 0)

    x_way, t_way, small_got, small, out_near, in_near = step(
        swap(x_way, "x", "stream_g"), swap(t_way, "t", "stream_g"), swap(small_sent, "x", "small"),
        small_kept, near_rows(out_back), near_rows(in_back),
    )
    small = plus(small, small_got)
    if rings > 1:
        small = lax.psum(small.astype(F32), "r").astype(BF16)
    low_second, high_second, out_near, in_near, *gathered_small = step(
        swap(plus(by_t_low, x_way[0]), "t", "stream_g_sum"),
        swap(plus(by_x_high, t_way[0]), "x", "stream_g_sum"),
        out_near, in_near, *from_z([small] * zs, "small"),
    )
    stream_sum = jnp.concatenate(
        [plus(own_low, x_way[1], low_second), plus(own_high, t_way[1], high_second)], axis=1
    )
    stream_sum, out_far, in_near = step(stream_sum, swap(out_near, "t", "rows"), in_near)
    stream_home = to_owners(stream_sum)
    in_far = swap(in_near, "t", "rows")
    small_near = jnp.concatenate(gathered_small, 0)
    small_near = jnp.concatenate([small_near, swap(small_near, "x", "small_all")], 0)

    one_row = shape((1, half_channels), F32)
    select_grad, step_w_grad, decay_grad, filter_grad, filter_b_grad, step_b_grad, skip_grad = whole(
        partial(small_kernel, (count, states, taps, zs)), "small", [zi, xi, ki],
        (small_near, swap(small_near, "k", "small")),
        [
            shape((count, half_channels), F32), shape((rank_width, half_channels), F32),
            shape((states, half_channels), F32), shape((taps, half_channels), F32),
            one_row, one_row, one_row,
        ],
    )
    in_far, select_grad = step(in_far, select_grad)

    back_place = send_place[:, None]
    if rings > 1:
        def own_rows(near, far, name):
            rows = whole(
                output_kernel, name, [xi], (back_place, near, far, jnp.zeros_like(tokens)),
                [shape(tokens.shape, BF16)],
            )[0]
            return dot(ring_order, from_blocks(over_rings(rows)), TN)

        output = (tokens.astype(F32) + own_rows(out_near, out_far, "output")).astype(BF16)
        rows = own_rows(in_near, in_far, "rows_back")
        own_x = tokens.astype(F32)
        inverse = lax.rsqrt(jnp.mean(own_x * own_x, axis=1, keepdims=True) + EPSILON)
        hat = own_x * inverse
        gain_rel = gain_row[:1].reshape(2, zs, 2, ring_rows)
        gain_abs = jnp.where(xi == 0, gain_rel, gain_rel[::-1]).transpose(1, 0, 2, 3)
        grad = rows * from_blocks(gain_abs.reshape(1, width))
        input_grad = cotangent.astype(F32) + inverse * (
            grad - hat * jnp.mean(grad * hat, axis=1, keepdims=True)
        )
    else:
        output = whole(
            output_kernel, "output", [xi], (back_place, out_near, out_far, tokens),
            [shape(tokens.shape, BF16)],
        )[0]
        input_grad = whole(
            input_kernel, "input_grad", [xi],
            (back_place, in_near, in_far, tokens, cotangent, gain_row),
            [shape(tokens.shape, F32)],
        )[0]
    late_home, stream_home, output, input_grad, select_grad = step(
        late_home, stream_home, output, input_grad, select_grad
    )
    gate_home, outer_home = late_home[:, :part], late_home[:, part:]
    outer_home = outer_home.reshape(half_channels, ring_rows).astype(F32)
    inner_home = jnp.stack(
        [v.reshape(half_channels, ring_rows).T for v in (stream_home, gate_home)], axis=1
    ).astype(F32)
    if rings > 1:
        outer_home = lax.psum_scatter(outer_home, "r", scatter_dimension=1, tiled=True)
        inner_home = lax.psum_scatter(inner_home, "r", scatter_dimension=0, tiled=True)
    gain_grad = jnp.sum(inner_home * inner_weight.astype(F32), axis=(1, 2))
    gain_grad = (gain_grad + swap(gain_grad, "t", "gain")) / norm_gain.astype(F32)
    return (
        output,
        input_grad,
        gain_grad,
        inner_home,
        filter_grad,
        filter_b_grad[0],
        select_grad.T,
        step_w_grad,
        step_b_grad[0],
        decay_grad,
        skip_grad[0],
        outer_home,
    )


def solution(mesh):
    devices = mesh.devices
    split = Mesh(
        devices.reshape(devices.shape[0] // 16, 4, 2, 2, devices.shape[1]), DP + ("t",)
    )
    in_specs = (
        P(DP, None), P(DP, None), P(), P(DP, None), P(DP), P(DP, None, "t"), P(None, "t"), P("t"),
        P("t", None), P(None, "t"), P("t"), P(None, "t"), P("t"), P("t", DP),
    )
    out_specs = (
        P(DP, None), P(DP, None), P(DP), P(DP, None, "t"), P(None, "t"), P("t"), P("t", None),
        P(None, "t"), P("t"), P(None, "t"), P("t"), P("t", DP),
    )
    return jax.shard_map(body, mesh=split, in_specs=in_specs, out_specs=out_specs, check_vma=False)
```
